256 devices in a mesh: gz: 8 (over x, core), gx: 32 (over z, y).
Axes of the slice: x: 4, y: 4, z: 8, core: 2. Of those that a mesh axis runs over, the one named last changes fastest.
Arguments:
- volume: float32 [256, 512, 256], P('gz', 'gx')
- measured: float32 [2, 256, 2048], P(None, 'gz')
- weight_blocks: bfloat16 [64, 128, 128], replicated, may hold values from 0 to 2
- view_order: int32 [2], replicated, may hold values from 0 to 1, each once
- tile_voxel: int32 [2, 8, 16384], P(None, 'gz', 'gx'), may hold values from 0 to 1023
- tile_column: int32 [2, 8, 16384], P(None, 'gz', 'gx'), may hold values from 0 to 15
- tile_block: int32 [2, 8, 16384], P(None, 'gz', 'gx'), may hold values from 0 to 63
- entry_count: int32 [2, 8, 32], P(None, 'gz', 'gx'), may hold values from 1 to 512, as said below
Outputs:
- volume_out: float32 [256, 512, 256], P('gz', 'gx')
The draws below stay inside these ranges and needn't reach their ends.
Inputs may be any that keep to these rules, and one draw needn't show every extreme that they name: Entries of block (a, c) of view v at or past entry_count[v, a, c] are not used; in every view some block has 512 live entries.
All inputs are finite; a program needn't handle non-finite values.
Results may differ from the reference program's by a relative error of at most 0.0027.
Values may be sent and summed in bfloat16 or wider, within the bound.
A program may use at most 64 MiB of HBM per device.

```python
import math
import jax
import jax.numpy as jnp
from jax import lax

CZ = 32
CX = 16
NY = 256
U = 2048
NB = 64
E_DEV = 512
SUB = 2
TV_STEPS = 4
NZ = 256
NX = 512
N_GZ = 8
N_GX = 32


def draw_volume(key, part):
    key_line, key_cell = jax.random.split(key)
    rise_z = jnp.arange(NZ, dtype=jnp.float32)[:, None, None] / NZ
    rise_x = jnp.arange(NX, dtype=jnp.float32)[None, :, None] / NX
    spread = jax.random.uniform(key_line, (NZ, NX, 1), jnp.float32)
    line_scale = 0.004 * jnp.exp(math.log(100.0) * rise_z + math.log(3.0) * rise_x + math.log(10.0) * (spread - 0.5))
    cell_noise = jax.random.normal(key_cell, (NZ, NX, NY), jnp.float32)
    return line_scale * (0.6 + 0.6 * cell_noise)


def draw_measured(key, part):
    key_row, key_cell = jax.random.split(key)
    rise_row = jnp.arange(NZ, dtype=jnp.float32)[None, :, None] / NZ
    spread = jax.random.uniform(key_row, (SUB, NZ, 1), jnp.float32)
    row_scale = 0.06 * jnp.exp(math.log(100.0) * rise_row + math.log(10.0) * (spread - 0.5))
    factor = 0.5 + jax.random.uniform(key_cell, (SUB, NZ, U), jnp.float32)
    return row_scale * factor


def draw_weight_blocks(key, part):
    key_diag, key_off = jax.random.split(key)
    diagonal = jax.random.uniform(key_diag, (NB, 128, 1), jnp.float32, 0.5, 1.5)
    eye_mask = (jnp.arange(128)[:, None] == jnp.arange(128)[None, :]).astype(jnp.float32)
    off_reach = 1.0 / 127.0
    off_part = jax.random.uniform(key_off, (NB, 128, 128), jnp.float32, 0.0, off_reach)
    return (eye_mask[None, :, :] * diagonal + off_part).astype(jnp.bfloat16)


def draw_entry_count(key, part):
    position = jnp.arange(N_GX, dtype=jnp.int32)[None, None, :] + 1
    base_count = E_DEV // 8 + (E_DEV - E_DEV // 8) * position * position // (N_GX * N_GX)
    base_count = jnp.broadcast_to(base_count, (SUB, N_GZ, N_GX))
    jitter = jax.random.randint(key, (SUB, N_GZ, N_GX), 0, base_count // 8 + 1)
    return (base_count - jitter * (position < N_GX).astype(jnp.int32)).astype(jnp.int32)


def set_ends(values, own_key, smallest, high):
    extent = values.shape
    index_at = [jax.random.randint(jax.random.fold_in(own_key, axis), (), 0, extent[axis]) for axis in range(len(extent))]
    values = values.at[tuple(index_at)].set(smallest)
    longest = extent.index(max(extent))
    index_at[longest] = (index_at[longest] + 1) % extent[longest]
    return values.at[tuple(index_at)].set(high)


def setup_inputs(seed: int = 0) -> dict:
    splits = jax.random.split(jax.random.key(seed), 9)
    return {
        "volume": draw_volume(jax.random.fold_in(splits[8], 71), 0),
        "measured": draw_measured(jax.random.fold_in(splits[8], 71), 0),
        "weight_blocks": draw_weight_blocks(jax.random.fold_in(splits[8], 71), 0),
        "view_order": jax.random.permutation(splits[3], SUB).astype(jnp.int32),
        "tile_voxel": set_ends(jax.random.randint(splits[4], (SUB, N_GZ, N_GX * E_DEV), 0, CZ * CX * NY // 128), jax.random.fold_in(splits[4], 1), 0, (CZ * CX * NY // 128) - 1).astype(jnp.int32),
        "tile_column": set_ends(jax.random.randint(splits[5], (SUB, N_GZ, N_GX * E_DEV), 0, U // 128), jax.random.fold_in(splits[5], 1), 0, (U // 128) - 1).astype(jnp.int32),
        "tile_block": set_ends(jax.random.randint(splits[6], (SUB, N_GZ, N_GX * E_DEV), 0, NB), jax.random.fold_in(splits[6], 1), 0, NB - 1).astype(jnp.int32),
        "entry_count": draw_entry_count(jax.random.fold_in(splits[8], 71), 0),
    }


smooth_floor = 0.01
step_gain = 0.25
norm_floor = 1e-06

def tv_grad(padded):
    base_cells = padded[:-1, :-1, :-1]
    diff_z = padded[1:, :-1, :-1] - base_cells
    diff_x = padded[:-1, 1:, :-1] - base_cells
    diff_y = padded[:-1, :-1, 1:] - base_cells
    inverse = lax.rsqrt(diff_z * diff_z + diff_x * diff_x + diff_y * diff_y + smooth_floor)
    flow_z = diff_z * inverse
    flow_x = diff_x * inverse
    flow_y = diff_y * inverse
    flow_all = flow_z + flow_x + flow_y
    return flow_z[:-1, 1:, 1:] + flow_x[1:, :-1, 1:] + flow_y[1:, 1:, :-1] - flow_all[1:, 1:, 1:]

def reference(volume, measured, weight_blocks, view_order, tile_voxel, tile_column, tile_block, entry_count):
    tiles_y = NY // 128
    tiles_u = U // 128
    row_weight = lax.optimization_barrier(jnp.sum(weight_blocks.astype(jnp.float32), axis=2))
    col_weight = lax.optimization_barrier(jnp.sum(weight_blocks.astype(jnp.float32), axis=1))
    devices = N_GZ * N_GX
    device_index = jnp.arange(devices, dtype=jnp.int32)[:, None]
    group_z = device_index // N_GX
    group_x = device_index % N_GX
    current = volume
    for turn_index in range(SUB):
        view_index = view_order[turn_index]
        voxel_list = lax.dynamic_index_in_dim(tile_voxel, view_index, 0, keepdims=False).reshape(devices, E_DEV)
        column_list = lax.dynamic_index_in_dim(tile_column, view_index, 0, keepdims=False).reshape(devices, E_DEV)
        block_list = lax.dynamic_index_in_dim(tile_block, view_index, 0, keepdims=False).reshape(devices, E_DEV)
        live_count = lax.dynamic_index_in_dim(entry_count, view_index, 0, keepdims=False).reshape(devices, 1)
        live_mask = (jnp.arange(E_DEV, dtype=jnp.int32)[None, :] < live_count).astype(jnp.float32)
        local_z = voxel_list // (CX * tiles_y)
        remainder = voxel_list % (CX * tiles_y)
        local_x = remainder // tiles_y
        part_y = remainder % tiles_y
        voxel_index = ((group_z * CZ + local_z) * NX + group_x * CX + local_x) * tiles_y + part_y
        detector_index = (group_z * CZ + local_z) * tiles_u + column_list
        voxel_tiles = current.astype(jnp.bfloat16).reshape(-1, 128)

        def forward(running, members):
            voxels, detector, chosen, weight = members
            blocks = weight_blocks[chosen].astype(jnp.float32)
            cell_values = voxel_tiles[voxels].astype(jnp.float32)
            contrib = jnp.einsum('ejk,ek->ej', blocks, cell_values, precision=lax.Precision.HIGHEST)
            return (running.at[detector].add(contrib * weight[:, None]), None)
        members = (voxel_index, detector_index, block_list, live_mask)
        projection, _ = lax.scan(forward, jnp.zeros((NZ * tiles_u, 128), jnp.float32), members)
        ray_sum = jnp.zeros((NZ * tiles_u, 128), jnp.float32).at[detector_index.reshape(-1)].add(row_weight[block_list.reshape(-1)] * live_mask.reshape(-1)[:, None])
        target = lax.dynamic_index_in_dim(measured, view_index, 0, keepdims=False).reshape(-1, 128)
        residual = ((target - projection) / (ray_sum + 1.0)).astype(jnp.bfloat16)

        def backward(running, members):
            voxels, detector, chosen, weight = members
            blocks = weight_blocks[chosen].astype(jnp.float32)
            pixel_values = residual[detector].astype(jnp.float32)
            contrib = jnp.einsum('ejk,ej->ek', blocks, pixel_values, precision=lax.Precision.HIGHEST)
            return (running.at[voxels].add(contrib * weight[:, None]), None)
        back, _ = lax.scan(backward, jnp.zeros((NZ * NX * tiles_y, 128), jnp.float32), members)
        voxel_sum = jnp.zeros((NZ * NX * tiles_y, 128), jnp.float32).at[voxel_index.reshape(-1)].add(col_weight[block_list.reshape(-1)] * live_mask.reshape(-1)[:, None])
        current = current + (back / (voxel_sum + 1.0)).reshape(current.shape)
    art_volume = jnp.maximum(current, 0.0)
    difference = art_volume - volume
    change = jnp.sqrt(jnp.sum(difference * difference))
    smooth = art_volume
    for sweep_index in range(TV_STEPS):
        slope = tv_grad(jnp.pad(smooth, 1))
        step_scale = step_gain * change / jnp.sqrt(jnp.sum(slope * slope) + norm_floor)
        smooth = smooth - step_scale * slope
    return smooth
```

```python
import functools

import jax
import jax.numpy as jnp
from jax import lax
from jax.experimental import pallas as pl
from jax.experimental.pallas import tpu as pltpu
from jax.sharding import PartitionSpec as P

TV_STEPS = 4


smooth_floor = 0.01
step_gain = 0.25
norm_floor = 1e-06
group_rows = 128


MESH = pl.DeviceIdType.MESH


def _peer(axis, position):
    if axis == "gz":
        return (position, lax.axis_index("gx"))
    return (lax.axis_index("gz"), position)


def vector_sum_kernel(n, x_ref, o_ref, recv, red, gath, ssem1, rsem1, ssem2, rsem2):
    me = lax.axis_index("gx")
    barrier = pltpu.get_barrier_semaphore()
    for d in range(1, n):
        pl.semaphore_signal(barrier, inc=1, device_id=_peer("gx", lax.rem(me + d, n)), device_id_type=MESH)
    pl.semaphore_wait(barrier, n - 1)
    sends = []
    for d in range(1, n):
        dst = lax.rem(me + d, n)
        copy = pltpu.make_async_remote_copy(
            src_ref=x_ref.at[dst], dst_ref=recv.at[d], send_sem=ssem1.at[d], recv_sem=rsem1.at[d],
            device_id=_peer("gx", dst), device_id_type=MESH)
        copy.start()
        sends.append(copy)
    for copy in sends:
        copy.wait()
    total = x_ref[me].astype(jnp.float32)
    for d in range(1, n):
        total = total + recv[d].astype(jnp.float32)
    red[...] = total.astype(red.dtype)
    sends = []
    for d in range(1, n):
        dst = lax.rem(me + d, n)
        copy = pltpu.make_async_remote_copy(
            src_ref=red, dst_ref=gath.at[me], send_sem=ssem2.at[d], recv_sem=rsem2.at[d],
            device_id=_peer("gx", dst), device_id_type=MESH)
        copy.start()
        sends.append(copy)
    for copy in sends:
        copy.wait()
    gath[me] = red[...]
    o_ref[...] = gath[...]


def vector_sum(x):
    n, rows, cols = x.shape
    return pl.pallas_call(
        functools.partial(vector_sum_kernel, n),
        out_shape=jax.ShapeDtypeStruct(x.shape, x.dtype),
        in_specs=[pl.BlockSpec(memory_space=pltpu.VMEM)],
        out_specs=pl.BlockSpec(memory_space=pltpu.VMEM),
        scratch_shapes=[
            pltpu.VMEM(x.shape, x.dtype),
            pltpu.VMEM((rows, cols), x.dtype),
            pltpu.VMEM(x.shape, x.dtype),
            pltpu.SemaphoreType.DMA((n,)),
            pltpu.SemaphoreType.DMA((n,)),
            pltpu.SemaphoreType.DMA((n,)),
            pltpu.SemaphoreType.DMA((n,)),
        ],
        compiler_params=pltpu.CompilerParams(collective_id=1, has_side_effects=True),
    )(x)


def _stage_peers(stage):
    axis, stride, size = stage
    index = lax.axis_index(axis)
    position = lax.rem(index // stride, size)
    base = index - position * stride
    return [base + lax.rem(position + d, size) * stride for d in range(1, size)]


def scalar_sum_kernel(stages, x_ref, o_ref, buf, recv, ssem, rsem):
    barrier = pltpu.get_barrier_semaphore()
    count = 0
    for stage in stages:
        for peer in _stage_peers(stage):
            pl.semaphore_signal(barrier, inc=1, device_id=_peer(stage[0], peer), device_id_type=MESH)
            count += 1
    pl.semaphore_wait(barrier, count)
    total = x_ref[...]
    slot = 0
    for s, stage in enumerate(stages):
        source = x_ref if s == 0 else buf.at[s - 1]
        sends = []
        for d, peer in enumerate(_stage_peers(stage)):
            copy = pltpu.make_async_remote_copy(
                src_ref=source, dst_ref=recv.at[slot + d], send_sem=ssem.at[slot + d],
                recv_sem=rsem.at[slot + d], device_id=_peer(stage[0], peer), device_id_type=MESH)
            copy.start()
            sends.append(copy)
        for copy in sends:
            copy.wait()
        for d in range(len(sends)):
            total = total + recv[slot + d]
        slot += len(sends)
        if s + 1 < len(stages):
            buf[s] = total
    o_ref[...] = total


def scalar_sum(x, stages):
    slots = sum(size - 1 for _, _, size in stages)
    return pl.pallas_call(
        functools.partial(scalar_sum_kernel, stages),
        out_shape=jax.ShapeDtypeStruct(x.shape, x.dtype),
        in_specs=[pl.BlockSpec(memory_space=pltpu.VMEM)],
        out_specs=pl.BlockSpec(memory_space=pltpu.VMEM),
        scratch_shapes=[
            pltpu.VMEM((max(len(stages) - 1, 1),) + x.shape, x.dtype),
            pltpu.VMEM((slots,) + x.shape, x.dtype),
            pltpu.SemaphoreType.DMA((slots,)),
            pltpu.SemaphoreType.DMA((slots,)),
        ],
        compiler_params=pltpu.CompilerParams(collective_id=2, has_side_effects=True),
    )(x)


def scalar_stages(n_gz, n_gx):
    stages = [("gz", 1, n_gz)]
    if n_gx % 4 == 0 and n_gx > 4:
        stages += [("gx", 1, 4), ("gx", 4, n_gx // 4)]
    else:
        stages += [("gx", 1, n_gx)]
    return [stage for stage in stages if stage[2] > 1]


def pack_pair(a, b):
    lane = lax.broadcasted_iota(jnp.int32, (8, 128), 1)
    return jnp.where(lane == 0, a, jnp.where(lane == 1, b, 0.0)).astype(jnp.float32)


def padded_2(cells, sides, width):
    for axis, dim in sides:
        count = lax.axis_size(axis)
        ends = count - 1
        head = lax.slice_in_dim(cells, 0, width, axis=dim)
        tail = lax.slice_in_dim(cells, cells.shape[dim] - width, cells.shape[dim], axis=dim)
        cells = jnp.concatenate(
            [
                lax.ppermute(tail, axis, [(i, (i + 1) % count) for i in range(ends)]),
                cells,
                lax.ppermute(head, axis, [((i + 1) % count, i) for i in range(ends)]),
            ],
            axis=dim,
        )
    return cells


def tv_grad(padded):
    base_cells = padded[:-1, :-1, :-1]
    diff_z = padded[1:, :-1, :-1] - base_cells
    diff_x = padded[:-1, 1:, :-1] - base_cells
    diff_y = padded[:-1, :-1, 1:] - base_cells
    inverse = lax.rsqrt(diff_z * diff_z + diff_x * diff_x + diff_y * diff_y + smooth_floor)
    flow_z = diff_z * inverse
    flow_x = diff_x * inverse
    flow_y = diff_y * inverse
    flow_all = flow_z + flow_x + flow_y
    return flow_z[:-1, 1:, 1:] + flow_x[1:, :-1, 1:] + flow_y[1:, 1:, :-1] - flow_all[1:, 1:, 1:]


def pad_depth(field):
    return jnp.pad(field, ((0, 0), (0, 0), (1, 1)))


def body(
    volume, measured, weight_blocks, view_order, tile_voxel, tile_column, tile_block, entry_count
):
    depth_z, depth_x, depth_y = volume.shape
    tiles_y = depth_y // group_rows
    tiles_u = measured.shape[2] // group_rows
    slab_tiles = depth_z * tiles_u
    plane_tiles = depth_x * tiles_y
    row_weight = jnp.sum(weight_blocks, axis=2, dtype=jnp.float32)
    col_weight = jnp.sum(weight_blocks, axis=1, dtype=jnp.float32)
    offsets = jnp.arange(group_rows, dtype=jnp.int32)
    current = volume
    for turn_index in range(view_order.shape[0]):
        view_index = view_order[turn_index]
        voxel_list = lax.dynamic_index_in_dim(tile_voxel, view_index, 0, keepdims=False)[0]
        column_list = lax.dynamic_index_in_dim(tile_column, view_index, 0, keepdims=False)[0]
        block_list = lax.dynamic_index_in_dim(tile_block, view_index, 0, keepdims=False)[0]
        live_count = lax.dynamic_index_in_dim(entry_count, view_index, 0, keepdims=False)[0, 0]
        rounds = (live_count + group_rows - 1) // group_rows
        voxel_tiles = current.astype(jnp.bfloat16).reshape(-1, group_rows)

        def gather_group(index):
            begin = index * group_rows
            voxels = lax.dynamic_slice_in_dim(voxel_list, begin, group_rows)
            columns = lax.dynamic_slice_in_dim(column_list, begin, group_rows)
            chosen = lax.dynamic_slice_in_dim(block_list, begin, group_rows)
            weight = (begin + offsets < live_count).astype(jnp.float32)[:, None]
            detector = voxels // plane_tiles * tiles_u + columns
            return (voxels, detector, chosen, weight)

        def forward(index, carry):
            projection, ray_sum = carry
            voxels, detector, chosen, weight = gather_group(index)
            product = jnp.einsum(
                "ejk,ek->ej",
                weight_blocks[chosen],
                voxel_tiles[voxels],
                preferred_element_type=jnp.float32,
            )
            return (
                projection.at[detector].add(product * weight),
                ray_sum.at[detector].add(row_weight[chosen] * weight),
            )

        empty = jnp.zeros((slab_tiles, group_rows), jnp.float32)
        projection, ray_sum = lax.fori_loop(0, rounds, forward, (empty, empty))
        target = lax.dynamic_index_in_dim(measured, view_index, 0, keepdims=False).reshape(
            slab_tiles, group_rows
        )
        n_gx = lax.axis_size("gx")
        joined = jnp.concatenate([projection, ray_sum], axis=1).astype(jnp.bfloat16)
        joined = vector_sum(joined.reshape(n_gx, slab_tiles // n_gx, 2 * group_rows))
        joined = joined.reshape(slab_tiles, 2 * group_rows).astype(jnp.float32)
        projection, ray_sum = joined[:, :group_rows], joined[:, group_rows:]
        residual = ((target - projection) / (ray_sum + 1.0)).astype(jnp.bfloat16)

        def backward(index, carry):
            change, voxel_sum = carry
            voxels, detector, chosen, weight = gather_group(index)
            product = jnp.einsum(
                "ejk,ej->ek",
                weight_blocks[chosen],
                residual[detector],
                preferred_element_type=jnp.float32,
            )
            return (
                change.at[voxels].add(product * weight),
                voxel_sum.at[voxels].add(col_weight[chosen] * weight),
            )

        blank = jnp.zeros((voxel_tiles.shape[0], group_rows), jnp.float32)
        change, voxel_sum = lax.fori_loop(0, rounds, backward, (blank, blank))
        current = current + (change / (voxel_sum + 1.0)).reshape(current.shape)
    art_volume = jnp.maximum(current, 0.0)
    difference = art_volume - volume
    change_part = jnp.sum(difference * difference)
    stages = scalar_stages(lax.axis_size("gz"), lax.axis_size("gx"))
    smooth = art_volume
    change_total = None
    for sweep_index in range(TV_STEPS):
        padded = padded_2(smooth, (("gz", 0), ("gx", 1)), 1)
        slope = tv_grad(pad_depth(padded))
        slope_part = jnp.sum(slope * slope)
        if sweep_index == 0:
            totals = scalar_sum(pack_pair(slope_part, change_part), stages)
            change_total = totals[0, 1]
        else:
            totals = scalar_sum(pack_pair(slope_part, 0.0), stages)
        slope_total = totals[0, 0]
        scale_now = step_gain * jnp.sqrt(change_total) / jnp.sqrt(slope_total + norm_floor)
        smooth = smooth - scale_now * slope
    return smooth


def solution(mesh):
    return jax.shard_map(
        body,
        mesh=mesh,
        in_specs=(
            P("gz", "gx", None),
            P(None, "gz", None),
            P(),
            P(),
            P(None, "gz", "gx"),
            P(None, "gz", "gx"),
            P(None, "gz", "gx"),
            P(None, "gz", "gx"),
        ),
        out_specs=P("gz", "gx", None),
        check_vma=False,
    )
```

```python
import functools

import jax
import jax.numpy as jnp
from jax import lax
from jax.experimental import pallas as pl
from jax.experimental.pallas import tpu as pltpu
from jax.sharding import PartitionSpec as P

TV_STEPS = 4


smooth_floor = 0.01
step_gain = 0.25
norm_floor = 1e-06
group_rows = 128


MESH = pl.DeviceIdType.MESH


def _peer(axis, position):
    if axis == "gz":
        return (position, lax.axis_index("gx"))
    return (lax.axis_index("gz"), position)


def vector_sum_kernel(n, x_ref, o_ref, recv, red, gath, ssem1, rsem1, ssem2, rsem2):
    me = lax.axis_index("gx")
    barrier = pltpu.get_barrier_semaphore()
    for d in range(1, n):
        pl.semaphore_signal(barrier, inc=1, device_id=_peer("gx", lax.rem(me + d, n)), device_id_type=MESH)
    pl.semaphore_wait(barrier, n - 1)
    sends = []
    for d in range(1, n):
        dst = lax.rem(me + d, n)
        copy = pltpu.make_async_remote_copy(
            src_ref=x_ref.at[dst], dst_ref=recv.at[d], send_sem=ssem1.at[d], recv_sem=rsem1.at[d],
            device_id=_peer("gx", dst), device_id_type=MESH)
        copy.start()
        sends.append(copy)
    for copy in sends:
        copy.wait()
    total = x_ref[me].astype(jnp.float32)
    for d in range(1, n):
        total = total + recv[d].astype(jnp.float32)
    red[...] = total.astype(red.dtype)
    sends = []
    for d in range(1, n):
        dst = lax.rem(me + d, n)
        copy = pltpu.make_async_remote_copy(
            src_ref=red, dst_ref=gath.at[me], send_sem=ssem2.at[d], recv_sem=rsem2.at[d],
            device_id=_peer("gx", dst), device_id_type=MESH)
        copy.start()
        sends.append(copy)
    for copy in sends:
        copy.wait()
    gath[me] = red[...]
    o_ref[...] = gath[...]


def vector_sum(x):
    n, rows, cols = x.shape
    return pl.pallas_call(
        functools.partial(vector_sum_kernel, n),
        out_shape=jax.ShapeDtypeStruct(x.shape, x.dtype),
        in_specs=[pl.BlockSpec(memory_space=pltpu.VMEM)],
        out_specs=pl.BlockSpec(memory_space=pltpu.VMEM),
        scratch_shapes=[
            pltpu.VMEM(x.shape, x.dtype),
            pltpu.VMEM((rows, cols), x.dtype),
            pltpu.VMEM(x.shape, x.dtype),
            pltpu.SemaphoreType.DMA((n,)),
            pltpu.SemaphoreType.DMA((n,)),
            pltpu.SemaphoreType.DMA((n,)),
            pltpu.SemaphoreType.DMA((n,)),
        ],
        compiler_params=pltpu.CompilerParams(collective_id=1, has_side_effects=True),
    )(x)


def _stage_peers(stage):
    axis, stride, size = stage
    index = lax.axis_index(axis)
    position = lax.rem(index // stride, size)
    base = index - position * stride
    return [base + lax.rem(position + d, size) * stride for d in range(1, size)]


def scalar_sum_kernel(stages, x_ref, o_ref, buf, recv, ssem, rsem):
    barrier = pltpu.get_barrier_semaphore()
    count = 0
    for stage in stages:
        for peer in _stage_peers(stage):
            pl.semaphore_signal(barrier, inc=1, device_id=_peer(stage[0], peer), device_id_type=MESH)
            count += 1
    pl.semaphore_wait(barrier, count)
    total = x_ref[...]
    slot = 0
    for s, stage in enumerate(stages):
        source = x_ref if s == 0 else buf.at[s - 1]
        sends = []
        for d, peer in enumerate(_stage_peers(stage)):
            copy = pltpu.make_async_remote_copy(
                src_ref=source, dst_ref=recv.at[slot + d], send_sem=ssem.at[slot + d],
                recv_sem=rsem.at[slot + d], device_id=_peer(stage[0], peer), device_id_type=MESH)
            copy.start()
            sends.append(copy)
        for copy in sends:
            copy.wait()
        for d in range(len(sends)):
            total = total + recv[slot + d]
        slot += len(sends)
        if s + 1 < len(stages):
            buf[s] = total
    o_ref[...] = total


def scalar_sum(x, stages):
    slots = sum(size - 1 for _, _, size in stages)
    return pl.pallas_call(
        functools.partial(scalar_sum_kernel, stages),
        out_shape=jax.ShapeDtypeStruct(x.shape, x.dtype),
        in_specs=[pl.BlockSpec(memory_space=pltpu.VMEM)],
        out_specs=pl.BlockSpec(memory_space=pltpu.VMEM),
        scratch_shapes=[
            pltpu.VMEM((max(len(stages) - 1, 1),) + x.shape, x.dtype),
            pltpu.VMEM((slots,) + x.shape, x.dtype),
            pltpu.SemaphoreType.DMA((slots,)),
            pltpu.SemaphoreType.DMA((slots,)),
        ],
        compiler_params=pltpu.CompilerParams(collective_id=2, has_side_effects=True),
    )(x)


def scalar_stages(n_gz, n_gx):
    stages = [("gz", 1, n_gz)]
    if n_gx % 4 == 0 and n_gx > 4:
        stages += [("gx", 1, 4), ("gx", 4, n_gx // 4)]
    else:
        stages += [("gx", 1, n_gx)]
    return [stage for stage in stages if stage[2] > 1]


def pack_pair(a, b):
    lane = lax.broadcasted_iota(jnp.int32, (8, 128), 1)
    return jnp.where(lane == 0, a, jnp.where(lane == 1, b, 0.0)).astype(jnp.float32)


def one_hot(index, size):
    return (index[:, None] == jnp.arange(size, dtype=jnp.int32)[None, :]).astype(jnp.bfloat16)


def block_apply_kernel(transposed, x_ref, blk_ref, w_ref, o_ref):
    o_ref[...] = jnp.zeros_like(o_ref)
    x = x_ref[...]
    chosen = blk_ref[...]

    def step(b, carry):
        masked = jnp.where(chosen == b, x, jnp.zeros_like(x))
        if transposed:
            dims = (((1,), (1,)), ((), ()))
        else:
            dims = (((1,), (0,)), ((), ()))
        o_ref[...] += lax.dot_general(masked, w_ref[b], dims, preferred_element_type=jnp.float32)
        return carry

    lax.fori_loop(0, w_ref.shape[0], step, 0)


def block_apply(x, chosen, weights, transposed):
    entries, width = x.shape
    n_blocks = weights.shape[0]
    return pl.pallas_call(
        functools.partial(block_apply_kernel, transposed),
        out_shape=jax.ShapeDtypeStruct((entries, width), jnp.float32),
        in_specs=[pl.BlockSpec(memory_space=pltpu.VMEM)] * 3,
        out_specs=pl.BlockSpec(memory_space=pltpu.VMEM),
        cost_estimate=pl.CostEstimate(
            flops=2 * entries * width * width * n_blocks, transcendentals=0,
            bytes_accessed=weights.size * 2 + entries * width * 10),
    )(x, chosen, weights)


def padded_2(cells, sides, width):
    for axis, dim in sides:
        count = lax.axis_size(axis)
        ends = count - 1
        head = lax.slice_in_dim(cells, 0, width, axis=dim)
        tail = lax.slice_in_dim(cells, cells.shape[dim] - width, cells.shape[dim], axis=dim)
        cells = jnp.concatenate(
            [
                lax.ppermute(tail, axis, [(i, (i + 1) % count) for i in range(ends)]),
                cells,
                lax.ppermute(head, axis, [((i + 1) % count, i) for i in range(ends)]),
            ],
            axis=dim,
        )
    return cells


def tv_grad(padded):
    base_cells = padded[:-1, :-1, :-1]
    diff_z = padded[1:, :-1, :-1] - base_cells
    diff_x = padded[:-1, 1:, :-1] - base_cells
    diff_y = padded[:-1, :-1, 1:] - base_cells
    inverse = lax.rsqrt(diff_z * diff_z + diff_x * diff_x + diff_y * diff_y + smooth_floor)
    flow_z = diff_z * inverse
    flow_x = diff_x * inverse
    flow_y = diff_y * inverse
    flow_all = flow_z + flow_x + flow_y
    return flow_z[:-1, 1:, 1:] + flow_x[1:, :-1, 1:] + flow_y[1:, 1:, :-1] - flow_all[1:, 1:, 1:]


def pad_depth(field):
    return jnp.pad(field, ((0, 0), (0, 0), (1, 1)))


def body(
    volume, measured, weight_blocks, view_order, tile_voxel, tile_column, tile_block, entry_count
):
    depth_z, depth_x, depth_y = volume.shape
    tiles_y = depth_y // group_rows
    tiles_u = measured.shape[2] // group_rows
    slab_tiles = depth_z * tiles_u
    plane_tiles = depth_x * tiles_y
    row_weight = jnp.sum(weight_blocks, axis=2, dtype=jnp.float32)
    col_weight = jnp.sum(weight_blocks, axis=1, dtype=jnp.float32)
    n_blocks = weight_blocks.shape[0]
    current = volume
    for turn_index in range(view_order.shape[0]):
        view_index = view_order[turn_index]
        voxel_list = lax.dynamic_index_in_dim(tile_voxel, view_index, 0, keepdims=False)[0]
        column_list = lax.dynamic_index_in_dim(tile_column, view_index, 0, keepdims=False)[0]
        block_list = lax.dynamic_index_in_dim(tile_block, view_index, 0, keepdims=False)[0]
        live_count = lax.dynamic_index_in_dim(entry_count, view_index, 0, keepdims=False)[0, 0]
        entries = voxel_list.shape[0]
        live = (jnp.arange(entries, dtype=jnp.int32) < live_count)[:, None]
        detector = voxel_list // plane_tiles * tiles_u + column_list
        voxel_tiles = current.astype(jnp.bfloat16).reshape(-1, group_rows)
        pick_voxel = one_hot(voxel_list, voxel_tiles.shape[0])
        pick_detector = one_hot(detector, slab_tiles)
        pick_block = jnp.where(live, one_hot(block_list, n_blocks), 0)
        blocks_column = block_list[:, None]

        cells = jnp.dot(pick_voxel, voxel_tiles, preferred_element_type=jnp.float32)
        product = block_apply(cells.astype(jnp.bfloat16), blocks_column, weight_blocks, True)
        product = jnp.where(live, product, 0.0)
        projection = lax.dot_general(
            pick_detector.astype(jnp.float32), product, (((0,), (0,)), ((), ())),
            precision=lax.Precision.HIGHEST)
        detector_blocks = lax.dot_general(
            pick_detector, pick_block, (((0,), (0,)), ((), ())), preferred_element_type=jnp.float32)
        ray_sum = jnp.dot(detector_blocks, row_weight, precision=lax.Precision.HIGHEST)
        target = lax.dynamic_index_in_dim(measured, view_index, 0, keepdims=False).reshape(
            slab_tiles, group_rows
        )
        n_gx = lax.axis_size("gx")
        joined = jnp.concatenate([projection, ray_sum], axis=1).astype(jnp.bfloat16)
        joined = vector_sum(joined.reshape(n_gx, slab_tiles // n_gx, 2 * group_rows))
        joined = joined.reshape(slab_tiles, 2 * group_rows).astype(jnp.float32)
        projection, ray_sum = joined[:, :group_rows], joined[:, group_rows:]
        residual = ((target - projection) / (ray_sum + 1.0)).astype(jnp.bfloat16)

        pixels = jnp.dot(pick_detector, residual, preferred_element_type=jnp.float32)
        product = block_apply(pixels.astype(jnp.bfloat16), blocks_column, weight_blocks, False)
        product = jnp.where(live, product, 0.0)
        change = lax.dot_general(
            pick_voxel.astype(jnp.float32), product, (((0,), (0,)), ((), ())),
            precision=lax.Precision.HIGHEST)
        voxel_blocks = lax.dot_general(
            pick_voxel, pick_block, (((0,), (0,)), ((), ())), preferred_element_type=jnp.float32)
        voxel_sum = jnp.dot(voxel_blocks, col_weight, precision=lax.Precision.HIGHEST)
        current = current + (change / (voxel_sum + 1.0)).reshape(current.shape)
    art_volume = jnp.maximum(current, 0.0)
    difference = art_volume - volume
    change_part = jnp.sum(difference * difference)
    stages = scalar_stages(lax.axis_size("gz"), lax.axis_size("gx"))
    smooth = art_volume
    change_total = None
    for sweep_index in range(TV_STEPS):
        padded = padded_2(smooth, (("gz", 0), ("gx", 1)), 1)
        slope = tv_grad(pad_depth(padded))
        slope_part = jnp.sum(slope * slope)
        if sweep_index == 0:
            totals = scalar_sum(pack_pair(slope_part, change_part), stages)
            change_total = totals[0, 1]
        else:
            totals = scalar_sum(pack_pair(slope_part, 0.0), stages)
        slope_total = totals[0, 0]
        scale_now = step_gain * jnp.sqrt(change_total) / jnp.sqrt(slope_total + norm_floor)
        smooth = smooth - scale_now * slope
    return smooth


def solution(mesh):
    return jax.shard_map(
        body,
        mesh=mesh,
        in_specs=(
            P("gz", "gx", None),
            P(None, "gz", None),
            P(),
            P(),
            P(None, "gz", "gx"),
            P(None, "gz", "gx"),
            P(None, "gz", "gx"),
            P(None, "gz", "gx"),
        ),
        out_specs=P("gz", "gx", None),
        check_vma=False,
    )
```

```python
import functools

import jax
import jax.numpy as jnp
from jax import lax
from jax.experimental import pallas as pl
from jax.experimental.pallas import tpu as pltpu
from jax.sharding import PartitionSpec as P

TV_STEPS = 4


smooth_floor = 0.01
step_gain = 0.25
norm_floor = 1e-06
group_rows = 128


MESH = pl.DeviceIdType.MESH


def _peer(axis, position):
    if axis == "gz":
        return (position, lax.axis_index("gx"))
    return (lax.axis_index("gz"), position)


def vector_sum_kernel(n, x_ref, o_ref, recv, red, gath, ssem1, rsem1, ssem2, rsem2):
    me = lax.axis_index("gx")
    barrier = pltpu.get_barrier_semaphore()
    for d in range(1, n):
        pl.semaphore_signal(barrier, inc=1, device_id=_peer("gx", lax.rem(me + d, n)), device_id_type=MESH)
    pl.semaphore_wait(barrier, n - 1)
    sends = []
    for d in range(1, n):
        dst = lax.rem(me + d, n)
        copy = pltpu.make_async_remote_copy(
            src_ref=x_ref.at[dst], dst_ref=recv.at[d], send_sem=ssem1.at[d], recv_sem=rsem1.at[d],
            device_id=_peer("gx", dst), device_id_type=MESH)
        copy.start()
        sends.append(copy)
    for copy in sends:
        copy.wait()
    total = x_ref[me].astype(jnp.float32)
    for d in range(1, n):
        total = total + recv[d].astype(jnp.float32)
    red[...] = total.astype(red.dtype)
    sends = []
    for d in range(1, n):
        dst = lax.rem(me + d, n)
        copy = pltpu.make_async_remote_copy(
            src_ref=red, dst_ref=gath.at[me], send_sem=ssem2.at[d], recv_sem=rsem2.at[d],
            device_id=_peer("gx", dst), device_id_type=MESH)
        copy.start()
        sends.append(copy)
    for copy in sends:
        copy.wait()
    gath[me] = red[...]
    o_ref[...] = gath[...]


def vector_sum(x):
    n, rows, cols = x.shape
    return pl.pallas_call(
        functools.partial(vector_sum_kernel, n),
        out_shape=jax.ShapeDtypeStruct(x.shape, x.dtype),
        in_specs=[pl.BlockSpec(memory_space=pltpu.VMEM)],
        out_specs=pl.BlockSpec(memory_space=pltpu.VMEM),
        scratch_shapes=[
            pltpu.VMEM(x.shape, x.dtype),
            pltpu.VMEM((rows, cols), x.dtype),
            pltpu.VMEM(x.shape, x.dtype),
            pltpu.SemaphoreType.DMA((n,)),
            pltpu.SemaphoreType.DMA((n,)),
            pltpu.SemaphoreType.DMA((n,)),
            pltpu.SemaphoreType.DMA((n,)),
        ],
        compiler_params=pltpu.CompilerParams(collective_id=1, has_side_effects=True),
    )(x)


def _stage_peers(stage):
    axis, stride, size = stage
    index = lax.axis_index(axis)
    position = lax.rem(index // stride, size)
    base = index - position * stride
    return [base + lax.rem(position + d, size) * stride for d in range(1, size)]


def scalar_sum_kernel(stages, x_ref, o_ref, buf, recv, ssem, rsem):
    barrier = pltpu.get_barrier_semaphore()
    count = 0
    for stage in stages:
        for peer in _stage_peers(stage):
            pl.semaphore_signal(barrier, inc=1, device_id=_peer(stage[0], peer), device_id_type=MESH)
            count += 1
    pl.semaphore_wait(barrier, count)
    total = x_ref[...]
    slot = 0
    for s, stage in enumerate(stages):
        axis, stride, size = stage
        position = lax.rem(lax.axis_index(axis) // stride, size)
        source = x_ref if s == 0 else buf.at[s - 1]
        recv[slot] = total
        sends = []
        for d, peer in enumerate(_stage_peers(stage), start=1):
            copy = pltpu.make_async_remote_copy(
                src_ref=source, dst_ref=recv.at[slot + d], send_sem=ssem.at[slot + d],
                recv_sem=rsem.at[slot + d], device_id=_peer(axis, peer), device_id_type=MESH)
            copy.start()
            sends.append(copy)
        for copy in sends:
            copy.wait()
        total = recv[slot + position]
        for p in range(1, size):
            total = total + recv[slot + lax.rem(position - p + size, size)]
        slot += size
        if s + 1 < len(stages):
            buf[s] = total
    o_ref[...] = total


def scalar_sum(x, stages):
    slots = sum(size for _, _, size in stages)
    return pl.pallas_call(
        functools.partial(scalar_sum_kernel, stages),
        out_shape=jax.ShapeDtypeStruct(x.shape, x.dtype),
        in_specs=[pl.BlockSpec(memory_space=pltpu.VMEM)],
        out_specs=pl.BlockSpec(memory_space=pltpu.VMEM),
        scratch_shapes=[
            pltpu.VMEM((max(len(stages) - 1, 1),) + x.shape, x.dtype),
            pltpu.VMEM((slots,) + x.shape, x.dtype),
            pltpu.SemaphoreType.DMA((slots,)),
            pltpu.SemaphoreType.DMA((slots,)),
        ],
        cost_estimate=pl.CostEstimate(flops=0, transcendentals=0, bytes_accessed=40_000_000),
        compiler_params=pltpu.CompilerParams(collective_id=2, has_side_effects=True),
    )(x)


def scalar_stages(n_gz, n_gx):
    stages = [("gz", 1, n_gz)]
    if n_gx % 4 == 0 and n_gx > 4:
        stages += [("gx", 1, 4), ("gx", 4, n_gx // 4)]
    else:
        stages += [("gx", 1, n_gx)]
    return [stage for stage in stages if stage[2] > 1]


def pack_pair(a, b):
    lane = lax.broadcasted_iota(jnp.int32, (8, 128), 1)
    return jnp.where(lane == 0, a, jnp.where(lane == 1, b, 0.0)).astype(jnp.float32)


def one_hot(index, size):
    return (index[:, None] == jnp.arange(size, dtype=jnp.int32)[None, :]).astype(jnp.bfloat16)


def block_apply_kernel(transposed, x_ref, blk_ref, w_ref, o_ref):
    o_ref[...] = jnp.zeros_like(o_ref)
    x = x_ref[...]
    chosen = blk_ref[...]

    def step(b, carry):
        masked = jnp.where(chosen == b, x, jnp.zeros_like(x))
        if transposed:
            dims = (((1,), (1,)), ((), ()))
        else:
            dims = (((1,), (0,)), ((), ()))
        o_ref[...] += lax.dot_general(masked, w_ref[b], dims, preferred_element_type=jnp.float32)
        return carry

    lax.fori_loop(0, w_ref.shape[0], step, 0)


def block_apply(x, chosen, weights, transposed):
    entries, width = x.shape
    n_blocks = weights.shape[0]
    return pl.pallas_call(
        functools.partial(block_apply_kernel, transposed),
        out_shape=jax.ShapeDtypeStruct((entries, width), jnp.float32),
        in_specs=[pl.BlockSpec(memory_space=pltpu.VMEM)] * 3,
        out_specs=pl.BlockSpec(memory_space=pltpu.VMEM),
        cost_estimate=pl.CostEstimate(
            flops=2 * entries * width * width * n_blocks, transcendentals=0,
            bytes_accessed=weights.size * 2 + entries * width * 10),
    )(x, chosen, weights)


def shift_from(block, pairs_of):
    count_z, count_x = lax.axis_size("gz"), lax.axis_size("gx")
    pairs = []
    for z in range(count_z):
        for x in range(count_x):
            target = pairs_of(z, x)
            if 0 <= target[0] < count_z and 0 <= target[1] < count_x:
                pairs.append((z * count_x + x, target[0] * count_x + target[1]))
    return lax.ppermute(block, ("gz", "gx"), pairs)


def padded_2(cells):
    zero_line = jnp.zeros_like(cells[:1, :1])
    low_z = shift_from(cells[-1:], lambda z, x: (z + 1, x))
    high_z = shift_from(cells[:1], lambda z, x: (z - 1, x))
    low_x = shift_from(cells[:, -1:], lambda z, x: (z, x + 1))
    high_x = shift_from(cells[:, :1], lambda z, x: (z, x - 1))
    low_z_high_x = shift_from(cells[-1:, :1], lambda z, x: (z + 1, x - 1))
    high_z_low_x = shift_from(cells[:1, -1:], lambda z, x: (z - 1, x + 1))
    top = jnp.concatenate([zero_line, low_z, low_z_high_x], axis=1)
    middle = jnp.concatenate([low_x, cells, high_x], axis=1)
    bottom = jnp.concatenate([high_z_low_x, high_z, zero_line], axis=1)
    return jnp.concatenate([top, middle, bottom], axis=0)


def tv_grad(padded):
    base_cells = padded[:-1, :-1, :-1]
    diff_z = padded[1:, :-1, :-1] - base_cells
    diff_x = padded[:-1, 1:, :-1] - base_cells
    diff_y = padded[:-1, :-1, 1:] - base_cells
    inverse = lax.rsqrt(diff_z * diff_z + diff_x * diff_x + diff_y * diff_y + smooth_floor)
    flow_z = diff_z * inverse
    flow_x = diff_x * inverse
    flow_y = diff_y * inverse
    flow_all = flow_z + flow_x + flow_y
    return flow_z[:-1, 1:, 1:] + flow_x[1:, :-1, 1:] + flow_y[1:, 1:, :-1] - flow_all[1:, 1:, 1:]


def pad_depth(field):
    return jnp.pad(field, ((0, 0), (0, 0), (1, 1)))


def body(
    volume, measured, weight_blocks, view_order, tile_voxel, tile_column, tile_block, entry_count
):
    depth_z, depth_x, depth_y = volume.shape
    tiles_y = depth_y // group_rows
    tiles_u = measured.shape[2] // group_rows
    slab_tiles = depth_z * tiles_u
    plane_tiles = depth_x * tiles_y
    row_weight = jnp.sum(weight_blocks, axis=2, dtype=jnp.float32)
    col_weight = jnp.sum(weight_blocks, axis=1, dtype=jnp.float32)
    n_blocks = weight_blocks.shape[0]
    current = volume
    for turn_index in range(view_order.shape[0]):
        view_index = view_order[turn_index]
        voxel_list = lax.dynamic_index_in_dim(tile_voxel, view_index, 0, keepdims=False)[0]
        column_list = lax.dynamic_index_in_dim(tile_column, view_index, 0, keepdims=False)[0]
        block_list = lax.dynamic_index_in_dim(tile_block, view_index, 0, keepdims=False)[0]
        live_count = lax.dynamic_index_in_dim(entry_count, view_index, 0, keepdims=False)[0, 0]
        entries = voxel_list.shape[0]
        live = (jnp.arange(entries, dtype=jnp.int32) < live_count)[:, None]
        detector = voxel_list // plane_tiles * tiles_u + column_list
        voxel_tiles = current.astype(jnp.bfloat16).reshape(-1, group_rows)
        pick_voxel = one_hot(voxel_list, voxel_tiles.shape[0])
        pick_detector = one_hot(detector, slab_tiles)
        pick_block = jnp.where(live, one_hot(block_list, n_blocks), 0)
        blocks_column = block_list[:, None]

        cells = jnp.dot(pick_voxel, voxel_tiles, preferred_element_type=jnp.float32)
        product = block_apply(cells.astype(jnp.bfloat16), blocks_column, weight_blocks, True)
        product = jnp.where(live, product, 0.0)
        projection = lax.dot_general(
            pick_detector.astype(jnp.float32), product, (((0,), (0,)), ((), ())),
            precision=lax.Precision.HIGHEST)
        detector_blocks = lax.dot_general(
            pick_detector, pick_block, (((0,), (0,)), ((), ())), preferred_element_type=jnp.float32)
        ray_sum = jnp.dot(detector_blocks, row_weight, precision=lax.Precision.HIGHEST)
        target = lax.dynamic_index_in_dim(measured, view_index, 0, keepdims=False).reshape(
            slab_tiles, group_rows
        )
        n_gx = lax.axis_size("gx")
        joined = jnp.concatenate([projection, ray_sum], axis=1).astype(jnp.bfloat16)
        joined = vector_sum(joined.reshape(n_gx, slab_tiles // n_gx, 2 * group_rows))
        joined = joined.reshape(slab_tiles, 2 * group_rows).astype(jnp.float32)
        projection, ray_sum = joined[:, :group_rows], joined[:, group_rows:]
        residual = ((target - projection) / (ray_sum + 1.0)).astype(jnp.bfloat16)

        pixels = jnp.dot(pick_detector, residual, preferred_element_type=jnp.float32)
        product = block_apply(pixels.astype(jnp.bfloat16), blocks_column, weight_blocks, False)
        product = jnp.where(live, product, 0.0)
        change = lax.dot_general(
            pick_voxel.astype(jnp.float32), product, (((0,), (0,)), ((), ())),
            precision=lax.Precision.HIGHEST)
        voxel_blocks = lax.dot_general(
            pick_voxel, pick_block, (((0,), (0,)), ((), ())), preferred_element_type=jnp.float32)
        voxel_sum = jnp.dot(voxel_blocks, col_weight, precision=lax.Precision.HIGHEST)
        current = current + (change / (voxel_sum + 1.0)).reshape(current.shape)
    art_volume = jnp.maximum(current, 0.0)
    difference = art_volume - volume
    change_part = jnp.sum(difference * difference)
    stages = scalar_stages(lax.axis_size("gz"), lax.axis_size("gx"))
    padded = padded_2(art_volume)
    smooth = art_volume
    change_total = None
    for sweep_index in range(TV_STEPS):
        slope = tv_grad(pad_depth(padded))
        slope_part = jnp.sum(slope * slope)
        more = sweep_index + 1 < TV_STEPS
        if more:
            slope_padded = padded_2(slope)
        if sweep_index == 0:
            totals = scalar_sum(pack_pair(slope_part, change_part), stages)
            change_total = totals[0, 1]
        else:
            totals = scalar_sum(pack_pair(slope_part, 0.0), stages)
        slope_total = totals[0, 0]
        scale_now = step_gain * jnp.sqrt(change_total) / jnp.sqrt(slope_total + norm_floor)
        smooth = smooth - scale_now * slope
        if more:
            padded = padded - scale_now * slope_padded
    return smooth


def solution(mesh):
    return jax.shard_map(
        body,
        mesh=mesh,
        in_specs=(
            P("gz", "gx", None),
            P(None, "gz", None),
            P(),
            P(),
            P(None, "gz", "gx"),
            P(None, "gz", "gx"),
            P(None, "gz", "gx"),
            P(None, "gz", "gx"),
        ),
        out_specs=P("gz", "gx", None),
        check_vma=False,
    )
```

```python
import functools

import jax
import jax.numpy as jnp
from jax import lax
from jax.experimental import pallas as pl
from jax.experimental.pallas import tpu as pltpu
from jax.sharding import PartitionSpec as P

TV_STEPS = 4


smooth_floor = 0.01
step_gain = 0.25
norm_floor = 1e-06
group_rows = 128


MESH = pl.DeviceIdType.MESH


def _peer(axis, position):
    if axis == "gz":
        return (position, lax.axis_index("gx"))
    return (lax.axis_index("gz"), position)


def vector_sum_kernel(n, x_ref, o_ref, recv, red, gath, ssem1, rsem1, ssem2, rsem2):
    me = lax.axis_index("gx")
    barrier = pltpu.get_barrier_semaphore()
    for d in range(1, n):
        pl.semaphore_signal(barrier, inc=1, device_id=_peer("gx", lax.rem(me + d, n)), device_id_type=MESH)
    pl.semaphore_wait(barrier, n - 1)
    sends = []
    for d in range(1, n):
        dst = lax.rem(me + d, n)
        copy = pltpu.make_async_remote_copy(
            src_ref=x_ref.at[dst], dst_ref=recv.at[d], send_sem=ssem1.at[d], recv_sem=rsem1.at[d],
            device_id=_peer("gx", dst), device_id_type=MESH)
        copy.start()
        sends.append(copy)
    for copy in sends:
        copy.wait()
    total = x_ref[me].astype(jnp.float32)
    for d in range(1, n):
        total = total + recv[d].astype(jnp.float32)
    red[...] = total.astype(red.dtype)
    sends = []
    for d in range(1, n):
        dst = lax.rem(me + d, n)
        copy = pltpu.make_async_remote_copy(
            src_ref=red, dst_ref=gath.at[me], send_sem=ssem2.at[d], recv_sem=rsem2.at[d],
            device_id=_peer("gx", dst), device_id_type=MESH)
        copy.start()
        sends.append(copy)
    for copy in sends:
        copy.wait()
    gath[me] = red[...]
    o_ref[...] = gath[...]


def vector_sum(x):
    n, rows, cols = x.shape
    return pl.pallas_call(
        functools.partial(vector_sum_kernel, n),
        out_shape=jax.ShapeDtypeStruct(x.shape, x.dtype),
        in_specs=[pl.BlockSpec(memory_space=pltpu.VMEM)],
        out_specs=pl.BlockSpec(memory_space=pltpu.VMEM),
        scratch_shapes=[
            pltpu.VMEM(x.shape, x.dtype),
            pltpu.VMEM((rows, cols), x.dtype),
            pltpu.VMEM(x.shape, x.dtype),
            pltpu.SemaphoreType.DMA((n,)),
            pltpu.SemaphoreType.DMA((n,)),
            pltpu.SemaphoreType.DMA((n,)),
            pltpu.SemaphoreType.DMA((n,)),
        ],
        compiler_params=pltpu.CompilerParams(collective_id=1, has_side_effects=True),
    )(x)


def _stage_peers(stage):
    axis, stride, size = stage
    index = lax.axis_index(axis)
    position = lax.rem(index // stride, size)
    base = index - position * stride
    return [base + lax.rem(position + d, size) * stride for d in range(1, size)]


def scalar_sum_kernel(stages, x_ref, o_ref, buf, recv, ssem, rsem):
    barrier = pltpu.get_barrier_semaphore()
    count = 0
    for stage in stages:
        for peer in _stage_peers(stage):
            pl.semaphore_signal(barrier, inc=1, device_id=_peer(stage[0], peer), device_id_type=MESH)
            count += 1
    pl.semaphore_wait(barrier, count)
    total = x_ref[...]
    slot = 0
    for s, stage in enumerate(stages):
        axis, stride, size = stage
        position = lax.rem(lax.axis_index(axis) // stride, size)
        source = x_ref if s == 0 else buf.at[s - 1]
        recv[slot] = total
        sends = []
        for d, peer in enumerate(_stage_peers(stage), start=1):
            copy = pltpu.make_async_remote_copy(
                src_ref=source, dst_ref=recv.at[slot + d], send_sem=ssem.at[slot + d],
                recv_sem=rsem.at[slot + d], device_id=_peer(axis, peer), device_id_type=MESH)
            copy.start()
            sends.append(copy)
        for copy in sends:
            copy.wait()
        total = recv[slot + position]
        for p in range(1, size):
            total = total + recv[slot + lax.rem(position - p + size, size)]
        slot += size
        if s + 1 < len(stages):
            buf[s] = total
    o_ref[...] = total


def scalar_sum(x, stages):
    slots = sum(size for _, _, size in stages)
    return pl.pallas_call(
        functools.partial(scalar_sum_kernel, stages),
        out_shape=jax.ShapeDtypeStruct(x.shape, x.dtype),
        in_specs=[pl.BlockSpec(memory_space=pltpu.VMEM)],
        out_specs=pl.BlockSpec(memory_space=pltpu.VMEM),
        scratch_shapes=[
            pltpu.VMEM((max(len(stages) - 1, 1),) + x.shape, x.dtype),
            pltpu.VMEM((slots,) + x.shape, x.dtype),
            pltpu.SemaphoreType.DMA((slots,)),
            pltpu.SemaphoreType.DMA((slots,)),
        ],
        cost_estimate=pl.CostEstimate(flops=0, transcendentals=0, bytes_accessed=40_000_000),
        compiler_params=pltpu.CompilerParams(collective_id=2, has_side_effects=True),
    )(x)


def halo_routes(depth, width):
    count_z, count_x = lax.axis_size("gz"), lax.axis_size("gx")
    z, x = lax.axis_index("gz"), lax.axis_index("gx")
    up_z, down_z = lax.rem(z + 1, count_z), lax.rem(z + count_z - 1, count_z)
    up_x, down_x = lax.rem(x + 1, count_x), lax.rem(x + count_x - 1, count_x)
    return [
        (0, depth, (up_z, x)),
        (depth, depth, (down_z, x)),
        (2 * depth, width, (z, up_x)),
        (2 * depth + width, width, (z, down_x)),
        (2 * depth + 2 * width, 1, (up_z, down_x)),
        (2 * depth + 2 * width + 1, 1, (down_z, up_x)),
    ]


def tv_exchange_kernel(stages, shape, x_ref, f_ref, o_ref, h_ref, buf, recv, ssem, rsem, hrecv, hsend, hget):
    routes = halo_routes(*shape)
    barrier = pltpu.get_barrier_semaphore()
    count = 0
    for stage in stages:
        for peer in _stage_peers(stage):
            pl.semaphore_signal(barrier, inc=1, device_id=_peer(stage[0], peer), device_id_type=MESH)
            count += 1
    for _, _, target in routes:
        pl.semaphore_signal(barrier, inc=1, device_id=target, device_id_type=MESH)
        count += 1
    pl.semaphore_wait(barrier, count)
    halo = []
    for k, (row, rows, target) in enumerate(routes):
        copy = pltpu.make_async_remote_copy(
            src_ref=f_ref.at[pl.ds(row, rows)], dst_ref=hrecv.at[pl.ds(row, rows)],
            send_sem=hsend.at[k], recv_sem=hget.at[k], device_id=target, device_id_type=MESH)
        copy.start()
        halo.append(copy)
    total = x_ref[...]
    slot = 0
    for s, stage in enumerate(stages):
        axis, stride, size = stage
        position = lax.rem(lax.axis_index(axis) // stride, size)
        source = x_ref if s == 0 else buf.at[s - 1]
        recv[slot] = total
        sends = []
        for d, peer in enumerate(_stage_peers(stage), start=1):
            copy = pltpu.make_async_remote_copy(
                src_ref=source, dst_ref=recv.at[slot + d], send_sem=ssem.at[slot + d],
                recv_sem=rsem.at[slot + d], device_id=_peer(axis, peer), device_id_type=MESH)
            copy.start()
            sends.append(copy)
        for copy in sends:
            copy.wait()
        total = recv[slot + position]
        for p in range(1, size):
            total = total + recv[slot + lax.rem(position - p + size, size)]
        slot += size
        if s + 1 < len(stages):
            buf[s] = total
    o_ref[...] = total
    for copy in halo:
        copy.wait()
    h_ref[...] = hrecv[...]


def tv_exchange(x, cells, stages):
    faces = faces_of(cells)
    slots = sum(size for _, _, size in stages)
    return pl.pallas_call(
        functools.partial(tv_exchange_kernel, stages, (cells.shape[1], cells.shape[0])),
        out_shape=(jax.ShapeDtypeStruct(x.shape, x.dtype), jax.ShapeDtypeStruct(faces.shape, faces.dtype)),
        in_specs=[pl.BlockSpec(memory_space=pltpu.VMEM)] * 2,
        out_specs=(pl.BlockSpec(memory_space=pltpu.VMEM), pl.BlockSpec(memory_space=pltpu.VMEM)),
        scratch_shapes=[
            pltpu.VMEM((max(len(stages) - 1, 1),) + x.shape, x.dtype),
            pltpu.VMEM((slots,) + x.shape, x.dtype),
            pltpu.SemaphoreType.DMA((slots,)),
            pltpu.SemaphoreType.DMA((slots,)),
            pltpu.VMEM(faces.shape, faces.dtype),
            pltpu.SemaphoreType.DMA((6,)),
            pltpu.SemaphoreType.DMA((6,)),
        ],
        compiler_params=pltpu.CompilerParams(collective_id=3, has_side_effects=True),
    )(x, faces)


def faces_of(cells):
    return jnp.concatenate(
        [cells[-1], cells[0], cells[:, -1], cells[:, 0], cells[-1, :1], cells[0, -1:]], axis=0)


def padded_from(cells, halo):
    count_z, count_x = lax.axis_size("gz"), lax.axis_size("gx")
    z, x = lax.axis_index("gz"), lax.axis_index("gx")
    depth, width = cells.shape[1], cells.shape[0]
    low_z = jnp.where(z > 0, halo[:depth], 0.0)[None]
    high_z = jnp.where(z < count_z - 1, halo[depth:2 * depth], 0.0)[None]
    low_x = jnp.where(x > 0, halo[2 * depth:2 * depth + width], 0.0)[:, None]
    high_x = jnp.where(x < count_x - 1, halo[2 * depth + width:2 * depth + 2 * width], 0.0)[:, None]
    corner = 2 * depth + 2 * width
    low_z_high_x = jnp.where((z > 0) & (x < count_x - 1), halo[corner:corner + 1], 0.0)[None]
    high_z_low_x = jnp.where((z < count_z - 1) & (x > 0), halo[corner + 1:corner + 2], 0.0)[None]
    zero_line = jnp.zeros_like(cells[:1, :1])
    top = jnp.concatenate([zero_line, low_z, low_z_high_x], axis=1)
    middle = jnp.concatenate([low_x, cells, high_x], axis=1)
    bottom = jnp.concatenate([high_z_low_x, high_z, zero_line], axis=1)
    return jnp.concatenate([top, middle, bottom], axis=0)


def scalar_stages(n_gz, n_gx):
    stages = [("gz", 1, n_gz)]
    if n_gx % 4 == 0 and n_gx > 4:
        stages += [("gx", 1, 4), ("gx", 4, n_gx // 4)]
    else:
        stages += [("gx", 1, n_gx)]
    return [stage for stage in stages if stage[2] > 1]


def pack_pair(a, b):
    lane = lax.broadcasted_iota(jnp.int32, (8, 128), 1)
    return jnp.where(lane == 0, a, jnp.where(lane == 1, b, 0.0)).astype(jnp.float32)


def one_hot(index, size):
    return (index[:, None] == jnp.arange(size, dtype=jnp.int32)[None, :]).astype(jnp.bfloat16)


def block_apply_kernel(transposed, x_ref, blk_ref, w_ref, o_ref):
    o_ref[...] = jnp.zeros_like(o_ref)
    x = x_ref[...]
    chosen = blk_ref[...]

    def step(b, carry):
        masked = jnp.where(chosen == b, x, jnp.zeros_like(x))
        if transposed:
            dims = (((1,), (1,)), ((), ()))
        else:
            dims = (((1,), (0,)), ((), ()))
        o_ref[...] += lax.dot_general(masked, w_ref[b], dims, preferred_element_type=jnp.float32)
        return carry

    lax.fori_loop(0, w_ref.shape[0], step, 0)


def block_apply(x, chosen, weights, transposed):
    entries, width = x.shape
    n_blocks = weights.shape[0]
    return pl.pallas_call(
        functools.partial(block_apply_kernel, transposed),
        out_shape=jax.ShapeDtypeStruct((entries, width), jnp.float32),
        in_specs=[pl.BlockSpec(memory_space=pltpu.VMEM)] * 3,
        out_specs=pl.BlockSpec(memory_space=pltpu.VMEM),
        cost_estimate=pl.CostEstimate(
            flops=2 * entries * width * width * n_blocks, transcendentals=0,
            bytes_accessed=weights.size * 2 + entries * width * 10),
    )(x, chosen, weights)


def shift_from(block, pairs_of):
    count_z, count_x = lax.axis_size("gz"), lax.axis_size("gx")
    pairs = []
    for z in range(count_z):
        for x in range(count_x):
            target = pairs_of(z, x)
            if 0 <= target[0] < count_z and 0 <= target[1] < count_x:
                pairs.append((z * count_x + x, target[0] * count_x + target[1]))
    return lax.ppermute(block, ("gz", "gx"), pairs)


def padded_2(cells):
    zero_line = jnp.zeros_like(cells[:1, :1])
    low_z = shift_from(cells[-1:], lambda z, x: (z + 1, x))
    high_z = shift_from(cells[:1], lambda z, x: (z - 1, x))
    low_x = shift_from(cells[:, -1:], lambda z, x: (z, x + 1))
    high_x = shift_from(cells[:, :1], lambda z, x: (z, x - 1))
    low_z_high_x = shift_from(cells[-1:, :1], lambda z, x: (z + 1, x - 1))
    high_z_low_x = shift_from(cells[:1, -1:], lambda z, x: (z - 1, x + 1))
    top = jnp.concatenate([zero_line, low_z, low_z_high_x], axis=1)
    middle = jnp.concatenate([low_x, cells, high_x], axis=1)
    bottom = jnp.concatenate([high_z_low_x, high_z, zero_line], axis=1)
    return jnp.concatenate([top, middle, bottom], axis=0)


def tv_grad(padded):
    base_cells = padded[:-1, :-1, :-1]
    diff_z = padded[1:, :-1, :-1] - base_cells
    diff_x = padded[:-1, 1:, :-1] - base_cells
    diff_y = padded[:-1, :-1, 1:] - base_cells
    inverse = lax.rsqrt(diff_z * diff_z + diff_x * diff_x + diff_y * diff_y + smooth_floor)
    flow_z = diff_z * inverse
    flow_x = diff_x * inverse
    flow_y = diff_y * inverse
    flow_all = flow_z + flow_x + flow_y
    return flow_z[:-1, 1:, 1:] + flow_x[1:, :-1, 1:] + flow_y[1:, 1:, :-1] - flow_all[1:, 1:, 1:]


def pad_depth(field):
    return jnp.pad(field, ((0, 0), (0, 0), (1, 1)))


def body(
    volume, measured, weight_blocks, view_order, tile_voxel, tile_column, tile_block, entry_count
):
    depth_z, depth_x, depth_y = volume.shape
    tiles_y = depth_y // group_rows
    tiles_u = measured.shape[2] // group_rows
    slab_tiles = depth_z * tiles_u
    plane_tiles = depth_x * tiles_y
    row_weight = jnp.sum(weight_blocks, axis=2, dtype=jnp.float32)
    col_weight = jnp.sum(weight_blocks, axis=1, dtype=jnp.float32)
    n_blocks = weight_blocks.shape[0]
    current = volume
    for turn_index in range(view_order.shape[0]):
        view_index = view_order[turn_index]
        voxel_list = lax.dynamic_index_in_dim(tile_voxel, view_index, 0, keepdims=False)[0]
        column_list = lax.dynamic_index_in_dim(tile_column, view_index, 0, keepdims=False)[0]
        block_list = lax.dynamic_index_in_dim(tile_block, view_index, 0, keepdims=False)[0]
        live_count = lax.dynamic_index_in_dim(entry_count, view_index, 0, keepdims=False)[0, 0]
        entries = voxel_list.shape[0]
        live = (jnp.arange(entries, dtype=jnp.int32) < live_count)[:, None]
        detector = voxel_list // plane_tiles * tiles_u + column_list
        voxel_tiles = current.astype(jnp.bfloat16).reshape(-1, group_rows)
        pick_voxel = one_hot(voxel_list, voxel_tiles.shape[0])
        pick_detector = one_hot(detector, slab_tiles)
        pick_block = jnp.where(live, one_hot(block_list, n_blocks), 0)
        blocks_column = block_list[:, None]

        cells = jnp.dot(pick_voxel, voxel_tiles, preferred_element_type=jnp.float32)
        product = block_apply(cells.astype(jnp.bfloat16), blocks_column, weight_blocks, True)
        product = jnp.where(live, product, 0.0)
        projection = lax.dot_general(
            pick_detector.astype(jnp.float32), product, (((0,), (0,)), ((), ())),
            precision=lax.Precision.HIGHEST)
        detector_blocks = lax.dot_general(
            pick_detector, pick_block, (((0,), (0,)), ((), ())), preferred_element_type=jnp.float32)
        ray_sum = jnp.dot(detector_blocks, row_weight, precision=lax.Precision.HIGHEST)
        target = lax.dynamic_index_in_dim(measured, view_index, 0, keepdims=False).reshape(
            slab_tiles, group_rows
        )
        n_gx = lax.axis_size("gx")
        joined = jnp.concatenate([projection, ray_sum], axis=1).astype(jnp.bfloat16)
        joined = vector_sum(joined.reshape(n_gx, slab_tiles // n_gx, 2 * group_rows))
        joined = joined.reshape(slab_tiles, 2 * group_rows).astype(jnp.float32)
        projection, ray_sum = joined[:, :group_rows], joined[:, group_rows:]
        residual = ((target - projection) / (ray_sum + 1.0)).astype(jnp.bfloat16)

        pixels = jnp.dot(pick_detector, residual, preferred_element_type=jnp.float32)
        product = block_apply(pixels.astype(jnp.bfloat16), blocks_column, weight_blocks, False)
        product = jnp.where(live, product, 0.0)
        change = lax.dot_general(
            pick_voxel.astype(jnp.float32), product, (((0,), (0,)), ((), ())),
            precision=lax.Precision.HIGHEST)
        voxel_blocks = lax.dot_general(
            pick_voxel, pick_block, (((0,), (0,)), ((), ())), preferred_element_type=jnp.float32)
        voxel_sum = jnp.dot(voxel_blocks, col_weight, precision=lax.Precision.HIGHEST)
        current = current + (change / (voxel_sum + 1.0)).reshape(current.shape)
    art_volume = jnp.maximum(current, 0.0)
    difference = art_volume - volume
    change_part = jnp.sum(difference * difference)
    stages = scalar_stages(lax.axis_size("gz"), lax.axis_size("gx"))
    totals, halo = tv_exchange(pack_pair(0.0, change_part), art_volume, stages)
    change_total = totals[0, 1]
    padded = padded_from(art_volume, halo)
    smooth = art_volume
    for sweep_index in range(TV_STEPS):
        slope = tv_grad(pad_depth(padded))
        slope_part = jnp.sum(slope * slope)
        totals, halo = tv_exchange(pack_pair(slope_part, 0.0), slope, stages)
        slope_total = totals[0, 0]
        scale_now = step_gain * jnp.sqrt(change_total) / jnp.sqrt(slope_total + norm_floor)
        smooth = smooth - scale_now * slope
        if sweep_index + 1 < TV_STEPS:
            padded = padded - scale_now * padded_from(slope, halo)
    return smooth


def solution(mesh):
    return jax.shard_map(
        body,
        mesh=mesh,
        in_specs=(
            P("gz", "gx", None),
            P(None, "gz", None),
            P(),
            P(),
            P(None, "gz", "gx"),
            P(None, "gz", "gx"),
            P(None, "gz", "gx"),
            P(None, "gz", "gx"),
        ),
        out_specs=P("gz", "gx", None),
        check_vma=False,
    )
```

```python
import functools

import jax
import jax.numpy as jnp
from jax import lax
from jax.experimental import pallas as pl
from jax.experimental.pallas import tpu as pltpu
from jax.sharding import PartitionSpec as P

TV_STEPS = 4


smooth_floor = 0.01
step_gain = 0.25
norm_floor = 1e-06
group_rows = 128


MESH = pl.DeviceIdType.MESH


def _peer(axis, position):
    if axis == "gz":
        return (position, lax.axis_index("gx"))
    return (lax.axis_index("gz"), position)


def vector_sum_kernel(n, x_ref, o_ref, recv, red, gath, ssem1, rsem1, ssem2, rsem2):
    me = lax.axis_index("gx")
    barrier = pltpu.get_barrier_semaphore()
    for d in range(1, n):
        pl.semaphore_signal(barrier, inc=1, device_id=_peer("gx", lax.rem(me + d, n)), device_id_type=MESH)
    pl.semaphore_wait(barrier, n - 1)
    sends = []
    for d in range(1, n):
        dst = lax.rem(me + d, n)
        copy = pltpu.make_async_remote_copy(
            src_ref=x_ref.at[dst], dst_ref=recv.at[d], send_sem=ssem1.at[d], recv_sem=rsem1.at[d],
            device_id=_peer("gx", dst), device_id_type=MESH)
        copy.start()
        sends.append(copy)
    for copy in sends:
        copy.wait()
    total = x_ref[me].astype(jnp.float32)
    for d in range(1, n):
        total = total + recv[d].astype(jnp.float32)
    red[...] = total.astype(red.dtype)
    sends = []
    for d in range(1, n):
        dst = lax.rem(me + d, n)
        copy = pltpu.make_async_remote_copy(
            src_ref=red, dst_ref=gath.at[me], send_sem=ssem2.at[d], recv_sem=rsem2.at[d],
            device_id=_peer("gx", dst), device_id_type=MESH)
        copy.start()
        sends.append(copy)
    for copy in sends:
        copy.wait()
    gath[me] = red[...]
    o_ref[...] = gath[...]


def vector_sum(x):
    n, rows, cols = x.shape
    return pl.pallas_call(
        functools.partial(vector_sum_kernel, n),
        out_shape=jax.ShapeDtypeStruct(x.shape, x.dtype),
        in_specs=[pl.BlockSpec(memory_space=pltpu.VMEM)],
        out_specs=pl.BlockSpec(memory_space=pltpu.VMEM),
        scratch_shapes=[
            pltpu.VMEM(x.shape, x.dtype),
            pltpu.VMEM((rows, cols), x.dtype),
            pltpu.VMEM(x.shape, x.dtype),
            pltpu.SemaphoreType.DMA((n,)),
            pltpu.SemaphoreType.DMA((n,)),
            pltpu.SemaphoreType.DMA((n,)),
            pltpu.SemaphoreType.DMA((n,)),
        ],
        compiler_params=pltpu.CompilerParams(collective_id=1, has_side_effects=True),
    )(x)


def _stage_peers(stage):
    axis, stride, size = stage
    index = lax.axis_index(axis)
    position = lax.rem(index // stride, size)
    base = index - position * stride
    return [base + lax.rem(position + d, size) * stride for d in range(1, size)]


def scalar_sum_kernel(stages, x_ref, o_ref, buf, recv, ssem, rsem):
    barrier = pltpu.get_barrier_semaphore()
    count = 0
    for stage in stages:
        for peer in _stage_peers(stage):
            pl.semaphore_signal(barrier, inc=1, device_id=_peer(stage[0], peer), device_id_type=MESH)
            count += 1
    pl.semaphore_wait(barrier, count)
    total = x_ref[...]
    slot = 0
    for s, stage in enumerate(stages):
        axis, stride, size = stage
        position = lax.rem(lax.axis_index(axis) // stride, size)
        source = x_ref if s == 0 else buf.at[s - 1]
        recv[slot] = total
        sends = []
        for d, peer in enumerate(_stage_peers(stage), start=1):
            copy = pltpu.make_async_remote_copy(
                src_ref=source, dst_ref=recv.at[slot + d], send_sem=ssem.at[slot + d],
                recv_sem=rsem.at[slot + d], device_id=_peer(axis, peer), device_id_type=MESH)
            copy.start()
            sends.append(copy)
        for copy in sends:
            copy.wait()
        total = recv[slot + position]
        for p in range(1, size):
            total = total + recv[slot + lax.rem(position - p + size, size)]
        slot += size
        if s + 1 < len(stages):
            buf[s] = total
    o_ref[...] = total


def scalar_sum(x, stages):
    slots = sum(size for _, _, size in stages)
    return pl.pallas_call(
        functools.partial(scalar_sum_kernel, stages),
        out_shape=jax.ShapeDtypeStruct(x.shape, x.dtype),
        in_specs=[pl.BlockSpec(memory_space=pltpu.VMEM)],
        out_specs=pl.BlockSpec(memory_space=pltpu.VMEM),
        scratch_shapes=[
            pltpu.VMEM((max(len(stages) - 1, 1),) + x.shape, x.dtype),
            pltpu.VMEM((slots,) + x.shape, x.dtype),
            pltpu.SemaphoreType.DMA((slots,)),
            pltpu.SemaphoreType.DMA((slots,)),
        ],
        cost_estimate=pl.CostEstimate(flops=0, transcendentals=0, bytes_accessed=40_000_000),
        compiler_params=pltpu.CompilerParams(collective_id=2, has_side_effects=True),
    )(x)


def halo_routes(depth, width):
    count_z, count_x = lax.axis_size("gz"), lax.axis_size("gx")
    z, x = lax.axis_index("gz"), lax.axis_index("gx")
    up_z, down_z = lax.rem(z + 1, count_z), lax.rem(z + count_z - 1, count_z)
    up_x, down_x = lax.rem(x + 1, count_x), lax.rem(x + count_x - 1, count_x)
    return [
        (0, depth, (up_z, x)),
        (depth, depth, (down_z, x)),
        (2 * depth, width, (z, up_x)),
        (2 * depth + width, width, (z, down_x)),
        (2 * depth + 2 * width, 1, (up_z, down_x)),
        (2 * depth + 2 * width + 1, 1, (down_z, up_x)),
    ]


def tv_exchange_kernel(stages, shape, x_ref, f_ref, o_ref, h_ref, buf, recv, ssem, rsem, hrecv, hsend, hget):
    routes = halo_routes(*shape)
    barrier = pltpu.get_barrier_semaphore()
    count = 0
    for stage in stages:
        for peer in _stage_peers(stage):
            pl.semaphore_signal(barrier, inc=1, device_id=_peer(stage[0], peer), device_id_type=MESH)
            count += 1
    for _, _, target in routes:
        pl.semaphore_signal(barrier, inc=1, device_id=target, device_id_type=MESH)
        count += 1
    pl.semaphore_wait(barrier, count)
    halo = []
    for k, (row, rows, target) in enumerate(routes):
        copy = pltpu.make_async_remote_copy(
            src_ref=f_ref.at[pl.ds(row, rows)], dst_ref=hrecv.at[pl.ds(row, rows)],
            send_sem=hsend.at[k], recv_sem=hget.at[k], device_id=target, device_id_type=MESH)
        copy.start()
        halo.append(copy)
    total = x_ref[...]
    slot = 0
    for s, stage in enumerate(stages):
        axis, stride, size = stage
        position = lax.rem(lax.axis_index(axis) // stride, size)
        source = x_ref if s == 0 else buf.at[s - 1]
        recv[slot] = total
        sends = []
        for d, peer in enumerate(_stage_peers(stage), start=1):
            copy = pltpu.make_async_remote_copy(
                src_ref=source, dst_ref=recv.at[slot + d], send_sem=ssem.at[slot + d],
                recv_sem=rsem.at[slot + d], device_id=_peer(axis, peer), device_id_type=MESH)
            copy.start()
            sends.append(copy)
        for copy in sends:
            copy.wait()
        total = recv[slot + position]
        for p in range(1, size):
            total = total + recv[slot + lax.rem(position - p + size, size)]
        slot += size
        if s + 1 < len(stages):
            buf[s] = total
    o_ref[...] = total
    for copy in halo:
        copy.wait()
    h_ref[...] = hrecv[...]


def tv_exchange(x, cells, stages):
    faces = faces_of(cells)
    slots = sum(size for _, _, size in stages)
    return pl.pallas_call(
        functools.partial(tv_exchange_kernel, stages, (cells.shape[1], cells.shape[0])),
        out_shape=(jax.ShapeDtypeStruct(x.shape, x.dtype), jax.ShapeDtypeStruct(faces.shape, faces.dtype)),
        in_specs=[pl.BlockSpec(memory_space=pltpu.VMEM)] * 2,
        out_specs=(pl.BlockSpec(memory_space=pltpu.VMEM), pl.BlockSpec(memory_space=pltpu.VMEM)),
        scratch_shapes=[
            pltpu.VMEM((max(len(stages) - 1, 1),) + x.shape, x.dtype),
            pltpu.VMEM((slots,) + x.shape, x.dtype),
            pltpu.SemaphoreType.DMA((slots,)),
            pltpu.SemaphoreType.DMA((slots,)),
            pltpu.VMEM(faces.shape, faces.dtype),
            pltpu.SemaphoreType.DMA((6,)),
            pltpu.SemaphoreType.DMA((6,)),
        ],
        compiler_params=pltpu.CompilerParams(collective_id=3, has_side_effects=True),
    )(x, faces)


def faces_of(cells):
    return jnp.concatenate(
        [cells[-1], cells[0], cells[:, -1], cells[:, 0], cells[-1, :1], cells[0, -1:]], axis=0)


def padded_from(cells, halo):
    count_z, count_x = lax.axis_size("gz"), lax.axis_size("gx")
    z, x = lax.axis_index("gz"), lax.axis_index("gx")
    depth, width = cells.shape[1], cells.shape[0]
    low_z = jnp.where(z > 0, halo[:depth], 0.0)[None]
    high_z = jnp.where(z < count_z - 1, halo[depth:2 * depth], 0.0)[None]
    low_x = jnp.where(x > 0, halo[2 * depth:2 * depth + width], 0.0)[:, None]
    high_x = jnp.where(x < count_x - 1, halo[2 * depth + width:2 * depth + 2 * width], 0.0)[:, None]
    corner = 2 * depth + 2 * width
    low_z_high_x = jnp.where((z > 0) & (x < count_x - 1), halo[corner:corner + 1], 0.0)[None]
    high_z_low_x = jnp.where((z < count_z - 1) & (x > 0), halo[corner + 1:corner + 2], 0.0)[None]
    zero_line = jnp.zeros_like(cells[:1, :1])
    top = jnp.concatenate([zero_line, low_z, low_z_high_x], axis=1)
    middle = jnp.concatenate([low_x, cells, high_x], axis=1)
    bottom = jnp.concatenate([high_z_low_x, high_z, zero_line], axis=1)
    return jnp.concatenate([top, middle, bottom], axis=0)


def scalar_stages(n_gz, n_gx):
    stages = [("gz", 1, n_gz)]
    if n_gx % 4 == 0 and n_gx > 4:
        stages += [("gx", 1, 4), ("gx", 4, n_gx // 4)]
    else:
        stages += [("gx", 1, n_gx)]
    return [stage for stage in stages if stage[2] > 1]


def pack_pair(a, b):
    lane = lax.broadcasted_iota(jnp.int32, (8, 128), 1)
    return jnp.where(lane == 0, a, jnp.where(lane == 1, b, 0.0)).astype(jnp.float32)


def one_hot(index, size):
    return (index[:, None] == jnp.arange(size, dtype=jnp.int32)[None, :]).astype(jnp.bfloat16)


def block_apply_kernel(group, transposed, x_ref, blk_ref, w_ref, o_ref):
    o_ref[...] = jnp.zeros_like(o_ref)
    x = x_ref[...]
    chosen = blk_ref[...]
    zero = jnp.zeros_like(x)
    dims = (((1,), (1,)), ((), ())) if transposed else (((1,), (0,)), ((), ()))

    def step(p, carry):
        parts = [jnp.where(chosen == p * group + i, x, zero) for i in range(group)]
        joined = jnp.concatenate(parts, axis=1)
        o_ref[...] += lax.dot_general(joined, w_ref[p], dims, preferred_element_type=jnp.float32)
        return carry

    lax.fori_loop(0, w_ref.shape[0], step, 0)


def stack_blocks(weights, group, transposed):
    n_blocks, rows, cols = weights.shape
    if transposed:
        stacked = weights.reshape(n_blocks // group, group, rows, cols).transpose(0, 2, 1, 3)
        return stacked.reshape(n_blocks // group, rows, group * cols)
    return weights.reshape(n_blocks // group, group * rows, cols)


def block_apply(x, chosen, stacked, group, transposed):
    entries, width = x.shape
    flops = 2 * entries * width * width * group * stacked.shape[0]
    return pl.pallas_call(
        functools.partial(block_apply_kernel, group, transposed),
        out_shape=jax.ShapeDtypeStruct((entries, width), jnp.float32),
        in_specs=[pl.BlockSpec(memory_space=pltpu.VMEM)] * 3,
        out_specs=pl.BlockSpec(memory_space=pltpu.VMEM),
        cost_estimate=pl.CostEstimate(
            flops=flops, transcendentals=0, bytes_accessed=stacked.size * 2 + entries * width * 10),
    )(x, chosen, stacked)


def shift_from(block, pairs_of):
    count_z, count_x = lax.axis_size("gz"), lax.axis_size("gx")
    pairs = []
    for z in range(count_z):
        for x in range(count_x):
            target = pairs_of(z, x)
            if 0 <= target[0] < count_z and 0 <= target[1] < count_x:
                pairs.append((z * count_x + x, target[0] * count_x + target[1]))
    return lax.ppermute(block, ("gz", "gx"), pairs)


def padded_2(cells):
    zero_line = jnp.zeros_like(cells[:1, :1])
    low_z = shift_from(cells[-1:], lambda z, x: (z + 1, x))
    high_z = shift_from(cells[:1], lambda z, x: (z - 1, x))
    low_x = shift_from(cells[:, -1:], lambda z, x: (z, x + 1))
    high_x = shift_from(cells[:, :1], lambda z, x: (z, x - 1))
    low_z_high_x = shift_from(cells[-1:, :1], lambda z, x: (z + 1, x - 1))
    high_z_low_x = shift_from(cells[:1, -1:], lambda z, x: (z - 1, x + 1))
    top = jnp.concatenate([zero_line, low_z, low_z_high_x], axis=1)
    middle = jnp.concatenate([low_x, cells, high_x], axis=1)
    bottom = jnp.concatenate([high_z_low_x, high_z, zero_line], axis=1)
    return jnp.concatenate([top, middle, bottom], axis=0)


def tv_grad(padded):
    base_cells = padded[:-1, :-1, :-1]
    diff_z = padded[1:, :-1, :-1] - base_cells
    diff_x = padded[:-1, 1:, :-1] - base_cells
    diff_y = padded[:-1, :-1, 1:] - base_cells
    inverse = lax.rsqrt(diff_z * diff_z + diff_x * diff_x + diff_y * diff_y + smooth_floor)
    flow_z = diff_z * inverse
    flow_x = diff_x * inverse
    flow_y = diff_y * inverse
    flow_all = flow_z + flow_x + flow_y
    return flow_z[:-1, 1:, 1:] + flow_x[1:, :-1, 1:] + flow_y[1:, 1:, :-1] - flow_all[1:, 1:, 1:]


def pad_depth(field):
    return jnp.pad(field, ((0, 0), (0, 0), (1, 1)))


def body(
    volume, measured, weight_blocks, view_order, tile_voxel, tile_column, tile_block, entry_count
):
    depth_z, depth_x, depth_y = volume.shape
    tiles_y = depth_y // group_rows
    tiles_u = measured.shape[2] // group_rows
    slab_tiles = depth_z * tiles_u
    plane_tiles = depth_x * tiles_y
    row_weight = jnp.sum(weight_blocks, axis=2, dtype=jnp.float32)
    col_weight = jnp.sum(weight_blocks, axis=1, dtype=jnp.float32)
    n_blocks = weight_blocks.shape[0]
    group = 4 if n_blocks % 4 == 0 else 1
    forward_stack = stack_blocks(weight_blocks, group, True)
    backward_stack = stack_blocks(weight_blocks, group, False)
    current = volume
    for turn_index in range(view_order.shape[0]):
        view_index = view_order[turn_index]
        voxel_list = lax.dynamic_index_in_dim(tile_voxel, view_index, 0, keepdims=False)[0]
        column_list = lax.dynamic_index_in_dim(tile_column, view_index, 0, keepdims=False)[0]
        block_list = lax.dynamic_index_in_dim(tile_block, view_index, 0, keepdims=False)[0]
        live_count = lax.dynamic_index_in_dim(entry_count, view_index, 0, keepdims=False)[0, 0]
        entries = voxel_list.shape[0]
        live = (jnp.arange(entries, dtype=jnp.int32) < live_count)[:, None]
        detector = voxel_list // plane_tiles * tiles_u + column_list
        voxel_tiles = current.astype(jnp.bfloat16).reshape(-1, group_rows)
        pick_voxel = one_hot(voxel_list, voxel_tiles.shape[0])
        pick_detector = one_hot(detector, slab_tiles)
        pick_block = jnp.where(live, one_hot(block_list, n_blocks), 0)
        blocks_column = block_list[:, None]

        cells = jnp.dot(pick_voxel, voxel_tiles, preferred_element_type=jnp.float32)
        product = block_apply(cells.astype(jnp.bfloat16), blocks_column, forward_stack, group, True)
        product = jnp.where(live, product, 0.0)
        projection = lax.dot_general(
            pick_detector.astype(jnp.float32), product, (((0,), (0,)), ((), ())),
            precision=lax.Precision.HIGHEST)
        detector_blocks = lax.dot_general(
            pick_detector, pick_block, (((0,), (0,)), ((), ())), preferred_element_type=jnp.float32)
        ray_sum = jnp.dot(detector_blocks, row_weight, precision=lax.Precision.HIGHEST)
        target = lax.dynamic_index_in_dim(measured, view_index, 0, keepdims=False).reshape(
            slab_tiles, group_rows
        )
        n_gx = lax.axis_size("gx")
        joined = jnp.concatenate([projection, ray_sum], axis=1).astype(jnp.bfloat16)
        joined = vector_sum(joined.reshape(n_gx, slab_tiles // n_gx, 2 * group_rows))
        joined = joined.reshape(slab_tiles, 2 * group_rows).astype(jnp.float32)
        projection, ray_sum = joined[:, :group_rows], joined[:, group_rows:]
        residual = ((target - projection) / (ray_sum + 1.0)).astype(jnp.bfloat16)

        pixels = jnp.dot(pick_detector, residual, preferred_element_type=jnp.float32)
        product = block_apply(pixels.astype(jnp.bfloat16), blocks_column, backward_stack, group, False)
        product = jnp.where(live, product, 0.0)
        change = lax.dot_general(
            pick_voxel.astype(jnp.float32), product, (((0,), (0,)), ((), ())),
            precision=lax.Precision.HIGHEST)
        voxel_blocks = lax.dot_general(
            pick_voxel, pick_block, (((0,), (0,)), ((), ())), preferred_element_type=jnp.float32)
        voxel_sum = jnp.dot(voxel_blocks, col_weight, precision=lax.Precision.HIGHEST)
        current = current + (change / (voxel_sum + 1.0)).reshape(current.shape)
    art_volume = jnp.maximum(current, 0.0)
    difference = art_volume - volume
    change_part = jnp.sum(difference * difference)
    stages = scalar_stages(lax.axis_size("gz"), lax.axis_size("gx"))
    totals, halo = tv_exchange(pack_pair(0.0, change_part), art_volume, stages)
    change_total = totals[0, 1]
    padded = padded_from(art_volume, halo)
    smooth = art_volume
    for sweep_index in range(TV_STEPS):
        slope = tv_grad(pad_depth(padded))
        slope_part = jnp.sum(slope * slope)
        totals, halo = tv_exchange(pack_pair(slope_part, 0.0), slope, stages)
        slope_total = totals[0, 0]
        scale_now = step_gain * jnp.sqrt(change_total) / jnp.sqrt(slope_total + norm_floor)
        smooth = smooth - scale_now * slope
        if sweep_index + 1 < TV_STEPS:
            padded = padded - scale_now * padded_from(slope, halo)
    return smooth


def solution(mesh):
    return jax.shard_map(
        body,
        mesh=mesh,
        in_specs=(
            P("gz", "gx", None),
            P(None, "gz", None),
            P(),
            P(),
            P(None, "gz", "gx"),
            P(None, "gz", "gx"),
            P(None, "gz", "gx"),
            P(None, "gz", "gx"),
        ),
        out_specs=P("gz", "gx", None),
        check_vma=False,
    )
```

```python
import functools

import jax
import jax.numpy as jnp
from jax import lax
from jax.experimental import pallas as pl
from jax.experimental.pallas import tpu as pltpu
from jax.sharding import PartitionSpec as P

TV_STEPS = 4


smooth_floor = 0.01
step_gain = 0.25
norm_floor = 1e-06
group_rows = 128


MESH = pl.DeviceIdType.MESH


def _peer(axis, position):
    if axis == "gz":
        return (position, lax.axis_index("gx"))
    return (lax.axis_index("gz"), position)


def vector_sum_kernel(n, x_ref, o_ref, recv, red, gath, ssem1, rsem1, ssem2, rsem2):
    me = lax.axis_index("gx")
    barrier = pltpu.get_barrier_semaphore()
    for d in range(1, n):
        pl.semaphore_signal(barrier, inc=1, device_id=_peer("gx", lax.rem(me + d, n)), device_id_type=MESH)
    pl.semaphore_wait(barrier, n - 1)
    sends = []
    for d in range(1, n):
        dst = lax.rem(me + d, n)
        copy = pltpu.make_async_remote_copy(
            src_ref=x_ref.at[dst], dst_ref=recv.at[d], send_sem=ssem1.at[d], recv_sem=rsem1.at[d],
            device_id=_peer("gx", dst), device_id_type=MESH)
        copy.start()
        sends.append(copy)
    for copy in sends:
        copy.wait()
    total = x_ref[me].astype(jnp.float32)
    for d in range(1, n):
        total = total + recv[d].astype(jnp.float32)
    red[...] = total.astype(red.dtype)
    sends = []
    for d in range(1, n):
        dst = lax.rem(me + d, n)
        copy = pltpu.make_async_remote_copy(
            src_ref=red, dst_ref=gath.at[me], send_sem=ssem2.at[d], recv_sem=rsem2.at[d],
            device_id=_peer("gx", dst), device_id_type=MESH)
        copy.start()
        sends.append(copy)
    for copy in sends:
        copy.wait()
    gath[me] = red[...]
    o_ref[...] = gath[...]


def vector_sum(x):
    n, rows, cols = x.shape
    return pl.pallas_call(
        functools.partial(vector_sum_kernel, n),
        out_shape=jax.ShapeDtypeStruct(x.shape, x.dtype),
        in_specs=[pl.BlockSpec(memory_space=pltpu.VMEM)],
        out_specs=pl.BlockSpec(memory_space=pltpu.VMEM),
        scratch_shapes=[
            pltpu.VMEM(x.shape, x.dtype),
            pltpu.VMEM((rows, cols), x.dtype),
            pltpu.VMEM(x.shape, x.dtype),
            pltpu.SemaphoreType.DMA((n,)),
            pltpu.SemaphoreType.DMA((n,)),
            pltpu.SemaphoreType.DMA((n,)),
            pltpu.SemaphoreType.DMA((n,)),
        ],
        compiler_params=pltpu.CompilerParams(collective_id=1, has_side_effects=True),
    )(x)


def _stage_peers(stage):
    axis, stride, size = stage
    index = lax.axis_index(axis)
    position = lax.rem(index // stride, size)
    base = index - position * stride
    return [base + lax.rem(position + d, size) * stride for d in range(1, size)]


def scalar_sum_kernel(stages, x_ref, o_ref, buf, recv, ssem, rsem):
    barrier = pltpu.get_barrier_semaphore()
    count = 0
    for stage in stages:
        for peer in _stage_peers(stage):
            pl.semaphore_signal(barrier, inc=1, device_id=_peer(stage[0], peer), device_id_type=MESH)
            count += 1
    pl.semaphore_wait(barrier, count)
    total = x_ref[...]
    slot = 0
    for s, stage in enumerate(stages):
        axis, stride, size = stage
        position = lax.rem(lax.axis_index(axis) // stride, size)
        source = x_ref if s == 0 else buf.at[s - 1]
        recv[slot] = total
        sends = []
        for d, peer in enumerate(_stage_peers(stage), start=1):
            copy = pltpu.make_async_remote_copy(
                src_ref=source, dst_ref=recv.at[slot + d], send_sem=ssem.at[slot + d],
                recv_sem=rsem.at[slot + d], device_id=_peer(axis, peer), device_id_type=MESH)
            copy.start()
            sends.append(copy)
        for copy in sends:
            copy.wait()
        total = recv[slot + position]
        for p in range(1, size):
            total = total + recv[slot + lax.rem(position - p + size, size)]
        slot += size
        if s + 1 < len(stages):
            buf[s] = total
    o_ref[...] = total


def scalar_sum(x, stages):
    slots = sum(size for _, _, size in stages)
    return pl.pallas_call(
        functools.partial(scalar_sum_kernel, stages),
        out_shape=jax.ShapeDtypeStruct(x.shape, x.dtype),
        in_specs=[pl.BlockSpec(memory_space=pltpu.VMEM)],
        out_specs=pl.BlockSpec(memory_space=pltpu.VMEM),
        scratch_shapes=[
            pltpu.VMEM((max(len(stages) - 1, 1),) + x.shape, x.dtype),
            pltpu.VMEM((slots,) + x.shape, x.dtype),
            pltpu.SemaphoreType.DMA((slots,)),
            pltpu.SemaphoreType.DMA((slots,)),
        ],
        cost_estimate=pl.CostEstimate(flops=0, transcendentals=0, bytes_accessed=40_000_000),
        compiler_params=pltpu.CompilerParams(collective_id=2, has_side_effects=True),
    )(x)


def halo_routes(depth, width):
    count_z, count_x = lax.axis_size("gz"), lax.axis_size("gx")
    z, x = lax.axis_index("gz"), lax.axis_index("gx")
    up_z, down_z = lax.rem(z + 1, count_z), lax.rem(z + count_z - 1, count_z)
    up_x, down_x = lax.rem(x + 1, count_x), lax.rem(x + count_x - 1, count_x)
    return [
        (0, depth, (up_z, x)),
        (depth, depth, (down_z, x)),
        (2 * depth, width, (z, up_x)),
        (2 * depth + width, width, (z, down_x)),
        (2 * depth + 2 * width, 1, (up_z, down_x)),
        (2 * depth + 2 * width + 1, 1, (down_z, up_x)),
    ]


def tv_exchange_kernel(stages, shape, x_ref, f_ref, o_ref, h_ref, buf, recv, ssem, rsem, hrecv, hsend, hget):
    routes = halo_routes(*shape)
    barrier = pltpu.get_barrier_semaphore()
    count = 0
    for stage in stages:
        for peer in _stage_peers(stage):
            pl.semaphore_signal(barrier, inc=1, device_id=_peer(stage[0], peer), device_id_type=MESH)
            count += 1
    for _, _, target in routes:
        pl.semaphore_signal(barrier, inc=1, device_id=target, device_id_type=MESH)
        count += 1
    pl.semaphore_wait(barrier, count)
    halo = []
    for k, (row, rows, target) in enumerate(routes):
        copy = pltpu.make_async_remote_copy(
            src_ref=f_ref.at[pl.ds(row, rows)], dst_ref=hrecv.at[pl.ds(row, rows)],
            send_sem=hsend.at[k], recv_sem=hget.at[k], device_id=target, device_id_type=MESH)
        copy.start()
        halo.append(copy)
    total = x_ref[...]
    slot = 0
    for s, stage in enumerate(stages):
        axis, stride, size = stage
        position = lax.rem(lax.axis_index(axis) // stride, size)
        source = x_ref if s == 0 else buf.at[s - 1]
        recv[slot] = total
        sends = []
        for d, peer in enumerate(_stage_peers(stage), start=1):
            copy = pltpu.make_async_remote_copy(
                src_ref=source, dst_ref=recv.at[slot + d], send_sem=ssem.at[slot + d],
                recv_sem=rsem.at[slot + d], device_id=_peer(axis, peer), device_id_type=MESH)
            copy.start()
            sends.append(copy)
        for copy in sends:
            copy.wait()
        total = recv[slot + position]
        for p in range(1, size):
            total = total + recv[slot + lax.rem(position - p + size, size)]
        slot += size
        if s + 1 < len(stages):
            buf[s] = total
    o_ref[...] = total
    for copy in halo:
        copy.wait()
    h_ref[...] = hrecv[...]


def tv_exchange(x, cells, stages):
    faces = faces_of(cells)
    slots = sum(size for _, _, size in stages)
    return pl.pallas_call(
        functools.partial(tv_exchange_kernel, stages, (cells.shape[1], cells.shape[0])),
        out_shape=(jax.ShapeDtypeStruct(x.shape, x.dtype), jax.ShapeDtypeStruct(faces.shape, faces.dtype)),
        in_specs=[pl.BlockSpec(memory_space=pltpu.VMEM)] * 2,
        out_specs=(pl.BlockSpec(memory_space=pltpu.VMEM), pl.BlockSpec(memory_space=pltpu.VMEM)),
        scratch_shapes=[
            pltpu.VMEM((max(len(stages) - 1, 1),) + x.shape, x.dtype),
            pltpu.VMEM((slots,) + x.shape, x.dtype),
            pltpu.SemaphoreType.DMA((slots,)),
            pltpu.SemaphoreType.DMA((slots,)),
            pltpu.VMEM(faces.shape, faces.dtype),
            pltpu.SemaphoreType.DMA((6,)),
            pltpu.SemaphoreType.DMA((6,)),
        ],
        compiler_params=pltpu.CompilerParams(collective_id=3, has_side_effects=True),
    )(x, faces)


def faces_of(cells):
    return jnp.concatenate(
        [cells[-1], cells[0], cells[:, -1], cells[:, 0], cells[-1, :1], cells[0, -1:]], axis=0)


def padded_from(cells, halo):
    count_z, count_x = lax.axis_size("gz"), lax.axis_size("gx")
    z, x = lax.axis_index("gz"), lax.axis_index("gx")
    depth, width = cells.shape[1], cells.shape[0]
    low_z = jnp.where(z > 0, halo[:depth], 0.0)[None]
    high_z = jnp.where(z < count_z - 1, halo[depth:2 * depth], 0.0)[None]
    low_x = jnp.where(x > 0, halo[2 * depth:2 * depth + width], 0.0)[:, None]
    high_x = jnp.where(x < count_x - 1, halo[2 * depth + width:2 * depth + 2 * width], 0.0)[:, None]
    corner = 2 * depth + 2 * width
    low_z_high_x = jnp.where((z > 0) & (x < count_x - 1), halo[corner:corner + 1], 0.0)[None]
    high_z_low_x = jnp.where((z < count_z - 1) & (x > 0), halo[corner + 1:corner + 2], 0.0)[None]
    zero_line = jnp.zeros_like(cells[:1, :1])
    top = jnp.concatenate([zero_line, low_z, low_z_high_x], axis=1)
    middle = jnp.concatenate([low_x, cells, high_x], axis=1)
    bottom = jnp.concatenate([high_z_low_x, high_z, zero_line], axis=1)
    return jnp.concatenate([top, middle, bottom], axis=0)


def scalar_stages(n_gz, n_gx):
    stages = [("gz", 1, n_gz)]
    if n_gx % 4 == 0 and n_gx > 4:
        stages += [("gx", 1, 4), ("gx", 4, n_gx // 4)]
    else:
        stages += [("gx", 1, n_gx)]
    return [stage for stage in stages if stage[2] > 1]


def pack_pair(a, b):
    lane = lax.broadcasted_iota(jnp.int32, (8, 128), 1)
    return jnp.where(lane == 0, a, jnp.where(lane == 1, b, 0.0)).astype(jnp.float32)


def one_hot(index, size):
    return (index[:, None] == jnp.arange(size, dtype=jnp.int32)[None, :]).astype(jnp.bfloat16)


def block_apply_kernel(group, transposed, x_ref, blk_ref, w_ref, o_ref):
    o_ref[...] = jnp.zeros_like(o_ref)
    x = x_ref[...]
    chosen = blk_ref[...]
    zero = jnp.zeros_like(x)
    dims = (((1,), (1,)), ((), ())) if transposed else (((1,), (0,)), ((), ()))

    def step(p, carry):
        parts = [jnp.where(chosen == p * group + i, x, zero) for i in range(group)]
        joined = jnp.concatenate(parts, axis=1)
        weights = jnp.concatenate(
            [w_ref[p * group + i] for i in range(group)], axis=1 if transposed else 0)
        o_ref[...] += lax.dot_general(joined, weights, dims, preferred_element_type=jnp.float32)
        return carry

    lax.fori_loop(0, w_ref.shape[0] // group, step, 0)


def block_apply(x, chosen, weights, group, transposed):
    entries, width = x.shape
    flops = 2 * entries * width * width * weights.shape[0]
    return pl.pallas_call(
        functools.partial(block_apply_kernel, group, transposed),
        out_shape=jax.ShapeDtypeStruct((entries, width), jnp.float32),
        in_specs=[pl.BlockSpec(memory_space=pltpu.VMEM)] * 3,
        out_specs=pl.BlockSpec(memory_space=pltpu.VMEM),
        cost_estimate=pl.CostEstimate(
            flops=flops, transcendentals=0, bytes_accessed=weights.size * 2 + entries * width * 10),
    )(x, chosen, weights)


def shift_from(block, pairs_of):
    count_z, count_x = lax.axis_size("gz"), lax.axis_size("gx")
    pairs = []
    for z in range(count_z):
        for x in range(count_x):
            target = pairs_of(z, x)
            if 0 <= target[0] < count_z and 0 <= target[1] < count_x:
                pairs.append((z * count_x + x, target[0] * count_x + target[1]))
    return lax.ppermute(block, ("gz", "gx"), pairs)


def padded_2(cells):
    zero_line = jnp.zeros_like(cells[:1, :1])
    low_z = shift_from(cells[-1:], lambda z, x: (z + 1, x))
    high_z = shift_from(cells[:1], lambda z, x: (z - 1, x))
    low_x = shift_from(cells[:, -1:], lambda z, x: (z, x + 1))
    high_x = shift_from(cells[:, :1], lambda z, x: (z, x - 1))
    low_z_high_x = shift_from(cells[-1:, :1], lambda z, x: (z + 1, x - 1))
    high_z_low_x = shift_from(cells[:1, -1:], lambda z, x: (z - 1, x + 1))
    top = jnp.concatenate([zero_line, low_z, low_z_high_x], axis=1)
    middle = jnp.concatenate([low_x, cells, high_x], axis=1)
    bottom = jnp.concatenate([high_z_low_x, high_z, zero_line], axis=1)
    return jnp.concatenate([top, middle, bottom], axis=0)


def tv_grad(padded):
    base_cells = padded[:-1, :-1, :-1]
    diff_z = padded[1:, :-1, :-1] - base_cells
    diff_x = padded[:-1, 1:, :-1] - base_cells
    diff_y = padded[:-1, :-1, 1:] - base_cells
    inverse = lax.rsqrt(diff_z * diff_z + diff_x * diff_x + diff_y * diff_y + smooth_floor)
    flow_z = diff_z * inverse
    flow_x = diff_x * inverse
    flow_y = diff_y * inverse
    flow_all = flow_z + flow_x + flow_y
    return flow_z[:-1, 1:, 1:] + flow_x[1:, :-1, 1:] + flow_y[1:, 1:, :-1] - flow_all[1:, 1:, 1:]


def pad_depth(field):
    return jnp.pad(field, ((0, 0), (0, 0), (1, 1)))


def body(
    volume, measured, weight_blocks, view_order, tile_voxel, tile_column, tile_block, entry_count
):
    depth_z, depth_x, depth_y = volume.shape
    tiles_y = depth_y // group_rows
    tiles_u = measured.shape[2] // group_rows
    slab_tiles = depth_z * tiles_u
    plane_tiles = depth_x * tiles_y
    row_weight = jnp.sum(weight_blocks, axis=2, dtype=jnp.float32)
    col_weight = jnp.sum(weight_blocks, axis=1, dtype=jnp.float32)
    n_blocks = weight_blocks.shape[0]
    group = 4 if n_blocks % 4 == 0 else 1
    current = volume
    for turn_index in range(view_order.shape[0]):
        view_index = view_order[turn_index]
        voxel_list = lax.dynamic_index_in_dim(tile_voxel, view_index, 0, keepdims=False)[0]
        column_list = lax.dynamic_index_in_dim(tile_column, view_index, 0, keepdims=False)[0]
        block_list = lax.dynamic_index_in_dim(tile_block, view_index, 0, keepdims=False)[0]
        live_count = lax.dynamic_index_in_dim(entry_count, view_index, 0, keepdims=False)[0, 0]
        entries = voxel_list.shape[0]
        live = (jnp.arange(entries, dtype=jnp.int32) < live_count)[:, None]
        detector = voxel_list // plane_tiles * tiles_u + column_list
        voxel_tiles = current.astype(jnp.bfloat16).reshape(-1, group_rows)
        pick_voxel = one_hot(voxel_list, voxel_tiles.shape[0])
        pick_detector = one_hot(detector, slab_tiles)
        pick_block = jnp.where(live, one_hot(block_list, n_blocks), 0)
        blocks_column = block_list[:, None]

        cells = jnp.dot(pick_voxel, voxel_tiles, preferred_element_type=jnp.float32)
        product = block_apply(cells.astype(jnp.bfloat16), blocks_column, weight_blocks, group, True)
        product = jnp.where(live, product, 0.0)
        projection = lax.dot_general(
            pick_detector.astype(jnp.float32), product, (((0,), (0,)), ((), ())),
            precision=lax.Precision.HIGHEST)
        detector_blocks = lax.dot_general(
            pick_detector, pick_block, (((0,), (0,)), ((), ())), preferred_element_type=jnp.float32)
        ray_sum = jnp.dot(detector_blocks, row_weight, precision=lax.Precision.HIGHEST)
        target = lax.dynamic_index_in_dim(measured, view_index, 0, keepdims=False).reshape(
            slab_tiles, group_rows
        )
        n_gx = lax.axis_size("gx")
        joined = jnp.concatenate([projection, ray_sum], axis=1).astype(jnp.bfloat16)
        joined = vector_sum(joined.reshape(n_gx, slab_tiles // n_gx, 2 * group_rows))
        joined = joined.reshape(slab_tiles, 2 * group_rows).astype(jnp.float32)
        projection, ray_sum = joined[:, :group_rows], joined[:, group_rows:]
        residual = ((target - projection) / (ray_sum + 1.0)).astype(jnp.bfloat16)

        pixels = jnp.dot(pick_detector, residual, preferred_element_type=jnp.float32)
        product = block_apply(pixels.astype(jnp.bfloat16), blocks_column, weight_blocks, group, False)
        product = jnp.where(live, product, 0.0)
        change = lax.dot_general(
            pick_voxel.astype(jnp.float32), product, (((0,), (0,)), ((), ())),
            precision=lax.Precision.HIGHEST)
        voxel_blocks = lax.dot_general(
            pick_voxel, pick_block, (((0,), (0,)), ((), ())), preferred_element_type=jnp.float32)
        voxel_sum = jnp.dot(voxel_blocks, col_weight, precision=lax.Precision.HIGHEST)
        current = current + (change / (voxel_sum + 1.0)).reshape(current.shape)
    art_volume = jnp.maximum(current, 0.0)
    difference = art_volume - volume
    change_part = jnp.sum(difference * difference)
    stages = scalar_stages(lax.axis_size("gz"), lax.axis_size("gx"))
    totals, halo = tv_exchange(pack_pair(0.0, change_part), art_volume, stages)
    change_total = totals[0, 1]
    padded = padded_from(art_volume, halo)
    smooth = art_volume
    for sweep_index in range(TV_STEPS):
        slope = tv_grad(pad_depth(padded))
        slope_part = jnp.sum(slope * slope)
        totals, halo = tv_exchange(pack_pair(slope_part, 0.0), slope, stages)
        slope_total = totals[0, 0]
        scale_now = step_gain * jnp.sqrt(change_total) / jnp.sqrt(slope_total + norm_floor)
        smooth = smooth - scale_now * slope
        if sweep_index + 1 < TV_STEPS:
            padded = padded - scale_now * padded_from(slope, halo)
    return smooth


def solution(mesh):
    return jax.shard_map(
        body,
        mesh=mesh,
        in_specs=(
            P("gz", "gx", None),
            P(None, "gz", None),
            P(),
            P(),
            P(None, "gz", "gx"),
            P(None, "gz", "gx"),
            P(None, "gz", "gx"),
            P(None, "gz", "gx"),
        ),
        out_specs=P("gz", "gx", None),
        check_vma=False,
    )
```

```python
import functools
import math

import jax
import jax.numpy as jnp
from jax import lax
from jax.experimental import pallas as pl
from jax.experimental.pallas import tpu as pltpu
from jax.sharding import PartitionSpec as P

TV_STEPS = 4


smooth_floor = 0.01
step_gain = 0.25
norm_floor = 1e-06
group_rows = 128


MESH = pl.DeviceIdType.MESH


def _peer(axis, position):
    if axis == "gz":
        return (position, lax.axis_index("gx"))
    return (lax.axis_index("gz"), position)


def vector_sum_kernel(n, x_ref, o_ref, recv, red, gath, ssem1, rsem1, ssem2, rsem2):
    me = lax.axis_index("gx")
    barrier = pltpu.get_barrier_semaphore()
    for d in range(1, n):
        pl.semaphore_signal(barrier, inc=1, device_id=_peer("gx", lax.rem(me + d, n)), device_id_type=MESH)
    pl.semaphore_wait(barrier, n - 1)
    sends = []
    for d in range(1, n):
        dst = lax.rem(me + d, n)
        copy = pltpu.make_async_remote_copy(
            src_ref=x_ref.at[dst], dst_ref=recv.at[d], send_sem=ssem1.at[d], recv_sem=rsem1.at[d],
            device_id=_peer("gx", dst), device_id_type=MESH)
        copy.start()
        sends.append(copy)
    for copy in sends:
        copy.wait()
    total = x_ref[me].astype(jnp.float32)
    for d in range(1, n):
        total = total + recv[d].astype(jnp.float32)
    red[...] = total.astype(red.dtype)
    sends = []
    for d in range(1, n):
        dst = lax.rem(me + d, n)
        copy = pltpu.make_async_remote_copy(
            src_ref=red, dst_ref=gath.at[me], send_sem=ssem2.at[d], recv_sem=rsem2.at[d],
            device_id=_peer("gx", dst), device_id_type=MESH)
        copy.start()
        sends.append(copy)
    for copy in sends:
        copy.wait()
    gath[me] = red[...]
    o_ref[...] = gath[...]


def vector_sum(x):
    n, rows, cols = x.shape
    return pl.pallas_call(
        functools.partial(vector_sum_kernel, n),
        out_shape=jax.ShapeDtypeStruct(x.shape, x.dtype),
        in_specs=[pl.BlockSpec(memory_space=pltpu.VMEM)],
        out_specs=pl.BlockSpec(memory_space=pltpu.VMEM),
        scratch_shapes=[
            pltpu.VMEM(x.shape, x.dtype),
            pltpu.VMEM((rows, cols), x.dtype),
            pltpu.VMEM(x.shape, x.dtype),
            pltpu.SemaphoreType.DMA((n,)),
            pltpu.SemaphoreType.DMA((n,)),
            pltpu.SemaphoreType.DMA((n,)),
            pltpu.SemaphoreType.DMA((n,)),
        ],
        compiler_params=pltpu.CompilerParams(collective_id=1, has_side_effects=True),
    )(x)


def _stage_peers(stage):
    if isinstance(stage[0], str):
        stage = [stage]
    index = {axis: lax.axis_index(axis) for axis, _, _ in stage}
    digits = [lax.rem(index[axis] // stride, size) for axis, stride, size in stage]
    total = 1
    position = 0
    for (_, _, size), digit in zip(stage, digits):
        position = position * size + digit
        total *= size
    peers = []
    for d in range(1, total):
        q = lax.rem(position + d, total)
        coords = dict(index)
        rest = total
        for (axis, stride, size), digit in zip(stage, digits):
            rest //= size
            coords[axis] = coords[axis] + (lax.rem(q // rest, size) - digit) * stride
        peers.append((coords.get("gz", lax.axis_index("gz")), coords.get("gx", lax.axis_index("gx"))))
    return position, total, peers


def halo_routes(depth, width):
    count_z, count_x = lax.axis_size("gz"), lax.axis_size("gx")
    z, x = lax.axis_index("gz"), lax.axis_index("gx")
    up_z, down_z = lax.rem(z + 1, count_z), lax.rem(z + count_z - 1, count_z)
    up_x, down_x = lax.rem(x + 1, count_x), lax.rem(x + count_x - 1, count_x)
    return [
        (0, depth, (up_z, x)),
        (depth, depth, (down_z, x)),
        (2 * depth, width, (z, up_x)),
        (2 * depth + width, width, (z, down_x)),
        (2 * depth + 2 * width, 1, (up_z, down_x)),
        (2 * depth + 2 * width + 1, 1, (down_z, up_x)),
    ]


def tv_exchange_kernel(stages, shape, x_ref, f_ref, o_ref, h_ref, buf, recv, ssem, rsem, hrecv, hsend, hget):
    routes = halo_routes(*shape)
    plan = [_stage_peers(stage) for stage in stages]
    barrier = pltpu.get_barrier_semaphore()
    count = 0
    for _, _, peers in plan:
        for peer in peers:
            pl.semaphore_signal(barrier, inc=1, device_id=peer, device_id_type=MESH)
            count += 1
    for _, _, target in routes:
        pl.semaphore_signal(barrier, inc=1, device_id=target, device_id_type=MESH)
        count += 1
    pl.semaphore_wait(barrier, count)
    halo = []
    for k, (row, rows, target) in enumerate(routes):
        copy = pltpu.make_async_remote_copy(
            src_ref=f_ref.at[pl.ds(row, rows)], dst_ref=hrecv.at[pl.ds(row, rows)],
            send_sem=hsend.at[k], recv_sem=hget.at[k], device_id=target, device_id_type=MESH)
        copy.start()
        halo.append(copy)
    total = x_ref[...]
    slot = 0
    for s, (position, size, peers) in enumerate(plan):
        source = x_ref if s == 0 else buf.at[s - 1]
        recv[slot] = total
        sends = []
        for d, peer in enumerate(peers, start=1):
            copy = pltpu.make_async_remote_copy(
                src_ref=source, dst_ref=recv.at[slot + d], send_sem=ssem.at[slot + d],
                recv_sem=rsem.at[slot + d], device_id=peer, device_id_type=MESH)
            copy.start()
            sends.append(copy)
        for copy in sends:
            copy.wait()
        total = recv[slot + position]
        for p in range(1, size):
            total = total + recv[slot + lax.rem(position - p + size, size)]
        slot += size
        if s + 1 < len(plan):
            buf[s] = total
    o_ref[...] = total
    for copy in halo:
        copy.wait()
    h_ref[...] = hrecv[...]


def tv_exchange(x, cells, stages):
    faces = faces_of(cells)
    slots = sum(math.prod(size for _, _, size in stage) for stage in stages)
    return pl.pallas_call(
        functools.partial(tv_exchange_kernel, stages, (cells.shape[1], cells.shape[0])),
        out_shape=(jax.ShapeDtypeStruct(x.shape, x.dtype), jax.ShapeDtypeStruct(faces.shape, faces.dtype)),
        in_specs=[pl.BlockSpec(memory_space=pltpu.VMEM)] * 2,
        out_specs=(pl.BlockSpec(memory_space=pltpu.VMEM), pl.BlockSpec(memory_space=pltpu.VMEM)),
        scratch_shapes=[
            pltpu.VMEM((max(len(stages) - 1, 1),) + x.shape, x.dtype),
            pltpu.VMEM((slots,) + x.shape, x.dtype),
            pltpu.SemaphoreType.DMA((slots,)),
            pltpu.SemaphoreType.DMA((slots,)),
            pltpu.VMEM(faces.shape, faces.dtype),
            pltpu.SemaphoreType.DMA((6,)),
            pltpu.SemaphoreType.DMA((6,)),
        ],
        compiler_params=pltpu.CompilerParams(collective_id=3, has_side_effects=True),
    )(x, faces)


def faces_of(cells):
    return jnp.concatenate(
        [cells[-1], cells[0], cells[:, -1], cells[:, 0], cells[-1, :1], cells[0, -1:]], axis=0)


def padded_from(cells, halo):
    count_z, count_x = lax.axis_size("gz"), lax.axis_size("gx")
    z, x = lax.axis_index("gz"), lax.axis_index("gx")
    depth, width = cells.shape[1], cells.shape[0]
    low_z = jnp.where(z > 0, halo[:depth], 0.0)[None]
    high_z = jnp.where(z < count_z - 1, halo[depth:2 * depth], 0.0)[None]
    low_x = jnp.where(x > 0, halo[2 * depth:2 * depth + width], 0.0)[:, None]
    high_x = jnp.where(x < count_x - 1, halo[2 * depth + width:2 * depth + 2 * width], 0.0)[:, None]
    corner = 2 * depth + 2 * width
    low_z_high_x = jnp.where((z > 0) & (x < count_x - 1), halo[corner:corner + 1], 0.0)[None]
    high_z_low_x = jnp.where((z < count_z - 1) & (x > 0), halo[corner + 1:corner + 2], 0.0)[None]
    zero_line = jnp.zeros_like(cells[:1, :1])
    top = jnp.concatenate([zero_line, low_z, low_z_high_x], axis=1)
    middle = jnp.concatenate([low_x, cells, high_x], axis=1)
    bottom = jnp.concatenate([high_z_low_x, high_z, zero_line], axis=1)
    return jnp.concatenate([top, middle, bottom], axis=0)


def scalar_stages(n_gz, n_gx):
    if n_gx % 4 == 0 and n_gx > 4:
        return [[("gz", 1, n_gz), ("gx", 1, 4)], [("gx", 4, n_gx // 4)]]
    return [[("gz", 1, n_gz)], [("gx", 1, n_gx)]]


def pack_pair(a, b):
    lane = lax.broadcasted_iota(jnp.int32, (8, 128), 1)
    return jnp.where(lane == 0, a, jnp.where(lane == 1, b, 0.0)).astype(jnp.float32)


def one_hot(index, size):
    return (index[:, None] == jnp.arange(size, dtype=jnp.int32)[None, :]).astype(jnp.bfloat16)


def block_apply_kernel(group, transposed, x_ref, blk_ref, w_ref, o_ref):
    o_ref[...] = jnp.zeros_like(o_ref)
    x = x_ref[...]
    chosen = blk_ref[...]
    zero = jnp.zeros_like(x)
    dims = (((1,), (1,)), ((), ())) if transposed else (((1,), (0,)), ((), ()))

    def step(p, carry):
        parts = [jnp.where(chosen == p * group + i, x, zero) for i in range(group)]
        joined = jnp.concatenate(parts, axis=1)
        weights = jnp.concatenate(
            [w_ref[p * group + i] for i in range(group)], axis=1 if transposed else 0)
        o_ref[...] += lax.dot_general(joined, weights, dims, preferred_element_type=jnp.float32)
        return carry

    lax.fori_loop(0, w_ref.shape[0] // group, step, 0)


def block_apply(x, chosen, weights, group, transposed):
    entries, width = x.shape
    flops = 2 * entries * width * width * weights.shape[0]
    return pl.pallas_call(
        functools.partial(block_apply_kernel, group, transposed),
        out_shape=jax.ShapeDtypeStruct((entries, width), jnp.float32),
        in_specs=[pl.BlockSpec(memory_space=pltpu.VMEM)] * 3,
        out_specs=pl.BlockSpec(memory_space=pltpu.VMEM),
        cost_estimate=pl.CostEstimate(
            flops=flops, transcendentals=0, bytes_accessed=weights.size * 2 + entries * width * 10),
    )(x, chosen, weights)


def shift_from(block, pairs_of):
    count_z, count_x = lax.axis_size("gz"), lax.axis_size("gx")
    pairs = []
    for z in range(count_z):
        for x in range(count_x):
            target = pairs_of(z, x)
            if 0 <= target[0] < count_z and 0 <= target[1] < count_x:
                pairs.append((z * count_x + x, target[0] * count_x + target[1]))
    return lax.ppermute(block, ("gz", "gx"), pairs)


def padded_2(cells):
    zero_line = jnp.zeros_like(cells[:1, :1])
    low_z = shift_from(cells[-1:], lambda z, x: (z + 1, x))
    high_z = shift_from(cells[:1], lambda z, x: (z - 1, x))
    low_x = shift_from(cells[:, -1:], lambda z, x: (z, x + 1))
    high_x = shift_from(cells[:, :1], lambda z, x: (z, x - 1))
    low_z_high_x = shift_from(cells[-1:, :1], lambda z, x: (z + 1, x - 1))
    high_z_low_x = shift_from(cells[:1, -1:], lambda z, x: (z - 1, x + 1))
    top = jnp.concatenate([zero_line, low_z, low_z_high_x], axis=1)
    middle = jnp.concatenate([low_x, cells, high_x], axis=1)
    bottom = jnp.concatenate([high_z_low_x, high_z, zero_line], axis=1)
    return jnp.concatenate([top, middle, bottom], axis=0)


def tv_grad(padded):
    base_cells = padded[:-1, :-1, :-1]
    diff_z = padded[1:, :-1, :-1] - base_cells
    diff_x = padded[:-1, 1:, :-1] - base_cells
    diff_y = padded[:-1, :-1, 1:] - base_cells
    inverse = lax.rsqrt(diff_z * diff_z + diff_x * diff_x + diff_y * diff_y + smooth_floor)
    flow_z = diff_z * inverse
    flow_x = diff_x * inverse
    flow_y = diff_y * inverse
    flow_all = flow_z + flow_x + flow_y
    return flow_z[:-1, 1:, 1:] + flow_x[1:, :-1, 1:] + flow_y[1:, 1:, :-1] - flow_all[1:, 1:, 1:]


def pad_depth(field):
    return jnp.pad(field, ((0, 0), (0, 0), (1, 1)))


def body(
    volume, measured, weight_blocks, view_order, tile_voxel, tile_column, tile_block, entry_count
):
    depth_z, depth_x, depth_y = volume.shape
    tiles_y = depth_y // group_rows
    tiles_u = measured.shape[2] // group_rows
    slab_tiles = depth_z * tiles_u
    plane_tiles = depth_x * tiles_y
    row_weight = jnp.sum(weight_blocks, axis=2, dtype=jnp.float32)
    col_weight = jnp.sum(weight_blocks, axis=1, dtype=jnp.float32)
    n_blocks = weight_blocks.shape[0]
    group = 4 if n_blocks % 4 == 0 else 1
    current = volume
    for turn_index in range(view_order.shape[0]):
        view_index = view_order[turn_index]
        voxel_list = lax.dynamic_index_in_dim(tile_voxel, view_index, 0, keepdims=False)[0]
        column_list = lax.dynamic_index_in_dim(tile_column, view_index, 0, keepdims=False)[0]
        block_list = lax.dynamic_index_in_dim(tile_block, view_index, 0, keepdims=False)[0]
        live_count = lax.dynamic_index_in_dim(entry_count, view_index, 0, keepdims=False)[0, 0]
        entries = voxel_list.shape[0]
        live = (jnp.arange(entries, dtype=jnp.int32) < live_count)[:, None]
        detector = voxel_list // plane_tiles * tiles_u + column_list
        voxel_tiles = current.astype(jnp.bfloat16).reshape(-1, group_rows)
        pick_voxel = one_hot(voxel_list, voxel_tiles.shape[0])
        pick_detector = one_hot(detector, slab_tiles)
        pick_block = jnp.where(live, one_hot(block_list, n_blocks), 0)
        blocks_column = block_list[:, None]

        cells = jnp.dot(pick_voxel, voxel_tiles, preferred_element_type=jnp.float32)
        product = block_apply(cells.astype(jnp.bfloat16), blocks_column, weight_blocks, group, True)
        product = jnp.where(live, product, 0.0)
        projection = lax.dot_general(
            pick_detector.astype(jnp.float32), product, (((0,), (0,)), ((), ())),
            precision=lax.Precision.HIGHEST)
        detector_blocks = lax.dot_general(
            pick_detector, pick_block, (((0,), (0,)), ((), ())), preferred_element_type=jnp.float32)
        ray_sum = jnp.dot(detector_blocks, row_weight, precision=lax.Precision.HIGHEST)
        target = lax.dynamic_index_in_dim(measured, view_index, 0, keepdims=False).reshape(
            slab_tiles, group_rows
        )
        n_gx = lax.axis_size("gx")
        joined = jnp.concatenate([projection, ray_sum], axis=1).astype(jnp.bfloat16)
        joined = vector_sum(joined.reshape(n_gx, slab_tiles // n_gx, 2 * group_rows))
        joined = joined.reshape(slab_tiles, 2 * group_rows).astype(jnp.float32)
        projection, ray_sum = joined[:, :group_rows], joined[:, group_rows:]
        residual = ((target - projection) / (ray_sum + 1.0)).astype(jnp.bfloat16)

        pixels = jnp.dot(pick_detector, residual, preferred_element_type=jnp.float32)
        product = block_apply(pixels.astype(jnp.bfloat16), blocks_column, weight_blocks, group, False)
        product = jnp.where(live, product, 0.0)
        change = lax.dot_general(
            pick_voxel.astype(jnp.float32), product, (((0,), (0,)), ((), ())),
            precision=lax.Precision.HIGHEST)
        voxel_blocks = lax.dot_general(
            pick_voxel, pick_block, (((0,), (0,)), ((), ())), preferred_element_type=jnp.float32)
        voxel_sum = jnp.dot(voxel_blocks, col_weight, precision=lax.Precision.HIGHEST)
        current = current + (change / (voxel_sum + 1.0)).reshape(current.shape)
    art_volume = jnp.maximum(current, 0.0)
    difference = art_volume - volume
    change_part = jnp.sum(difference * difference)
    stages = scalar_stages(lax.axis_size("gz"), lax.axis_size("gx"))
    totals, halo = tv_exchange(pack_pair(0.0, change_part), art_volume, stages)
    change_total = totals[0, 1]
    padded = padded_from(art_volume, halo)
    smooth = art_volume
    for sweep_index in range(TV_STEPS):
        slope = tv_grad(pad_depth(padded))
        slope_part = jnp.sum(slope * slope)
        totals, halo = tv_exchange(pack_pair(slope_part, 0.0), slope, stages)
        slope_total = totals[0, 0]
        scale_now = step_gain * jnp.sqrt(change_total) / jnp.sqrt(slope_total + norm_floor)
        smooth = smooth - scale_now * slope
        if sweep_index + 1 < TV_STEPS:
            padded = padded - scale_now * padded_from(slope, halo)
    return smooth


def solution(mesh):
    return jax.shard_map(
        body,
        mesh=mesh,
        in_specs=(
            P("gz", "gx", None),
            P(None, "gz", None),
            P(),
            P(),
            P(None, "gz", "gx"),
            P(None, "gz", "gx"),
            P(None, "gz", "gx"),
            P(None, "gz", "gx"),
        ),
        out_specs=P("gz", "gx", None),
        check_vma=False,
    )
```

```python
import functools
import math

import jax
import jax.numpy as jnp
from jax import lax
from jax.experimental import pallas as pl
from jax.experimental.pallas import tpu as pltpu
from jax.sharding import PartitionSpec as P

TV_STEPS = 4


smooth_floor = 0.01
step_gain = 0.25
norm_floor = 1e-06
group_rows = 128


MESH = pl.DeviceIdType.MESH


def _peer(axis, position):
    if axis == "gz":
        return (position, lax.axis_index("gx"))
    return (lax.axis_index("gz"), position)


def vector_sum_kernel(n, x_ref, o_ref, recv, red, gath, ssem1, rsem1, ssem2, rsem2):
    me = lax.axis_index("gx")
    barrier = pltpu.get_barrier_semaphore()
    for d in range(1, n):
        pl.semaphore_signal(barrier, inc=1, device_id=_peer("gx", lax.rem(me + d, n)), device_id_type=MESH)
    pl.semaphore_wait(barrier, n - 1)

    def scatter_copy(d):
        dst = lax.rem(me + d, n)
        return pltpu.make_async_remote_copy(
            src_ref=x_ref.at[dst], dst_ref=recv.at[d], send_sem=ssem1.at[d], recv_sem=rsem1.at[d],
            device_id=_peer("gx", dst), device_id_type=MESH)

    def gather_copy(d):
        dst = lax.rem(me + d, n)
        return pltpu.make_async_remote_copy(
            src_ref=red, dst_ref=gath.at[me], send_sem=ssem2.at[d], recv_sem=rsem2.at[d],
            device_id=_peer("gx", dst), device_id_type=MESH)

    @pl.loop(1, n)
    def _(d):
        scatter_copy(d).start()

    @pl.loop(1, n)
    def _(d):
        scatter_copy(d).wait()

    total = lax.fori_loop(
        1, n, lambda d, acc: acc + recv[d].astype(jnp.float32), x_ref[me].astype(jnp.float32))
    red[...] = total.astype(red.dtype)

    @pl.loop(1, n)
    def _(d):
        gather_copy(d).start()

    @pl.loop(1, n)
    def _(d):
        gather_copy(d).wait()

    gath[me] = red[...]
    o_ref[...] = gath[...]


def vector_sum(x):
    n, rows, cols = x.shape
    return pl.pallas_call(
        functools.partial(vector_sum_kernel, n),
        out_shape=jax.ShapeDtypeStruct(x.shape, x.dtype),
        in_specs=[pl.BlockSpec(memory_space=pltpu.VMEM)],
        out_specs=pl.BlockSpec(memory_space=pltpu.VMEM),
        scratch_shapes=[
            pltpu.VMEM(x.shape, x.dtype),
            pltpu.VMEM((rows, cols), x.dtype),
            pltpu.VMEM(x.shape, x.dtype),
            pltpu.SemaphoreType.DMA((n,)),
            pltpu.SemaphoreType.DMA((n,)),
            pltpu.SemaphoreType.DMA((n,)),
            pltpu.SemaphoreType.DMA((n,)),
        ],
        compiler_params=pltpu.CompilerParams(collective_id=1, has_side_effects=True),
    )(x)


def _stage_peers(stage):
    if isinstance(stage[0], str):
        stage = [stage]
    index = {axis: lax.axis_index(axis) for axis, _, _ in stage}
    digits = [lax.rem(index[axis] // stride, size) for axis, stride, size in stage]
    total = 1
    position = 0
    for (_, _, size), digit in zip(stage, digits):
        position = position * size + digit
        total *= size
    peers = []
    for d in range(1, total):
        q = lax.rem(position + d, total)
        coords = dict(index)
        rest = total
        for (axis, stride, size), digit in zip(stage, digits):
            rest //= size
            coords[axis] = coords[axis] + (lax.rem(q // rest, size) - digit) * stride
        peers.append((coords.get("gz", lax.axis_index("gz")), coords.get("gx", lax.axis_index("gx"))))
    return position, total, peers


def halo_routes(depth, width):
    count_z, count_x = lax.axis_size("gz"), lax.axis_size("gx")
    z, x = lax.axis_index("gz"), lax.axis_index("gx")
    up_z, down_z = lax.rem(z + 1, count_z), lax.rem(z + count_z - 1, count_z)
    up_x, down_x = lax.rem(x + 1, count_x), lax.rem(x + count_x - 1, count_x)
    return [
        (0, depth, (up_z, x)),
        (depth, depth, (down_z, x)),
        (2 * depth, width, (z, up_x)),
        (2 * depth + width, width, (z, down_x)),
        (2 * depth + 2 * width, 1, (up_z, down_x)),
        (2 * depth + 2 * width + 1, 1, (down_z, up_x)),
    ]


def tv_exchange_kernel(stages, shape, x_ref, f_ref, o_ref, h_ref, buf, recv, ssem, rsem, hrecv, hsend, hget):
    routes = halo_routes(*shape)
    plan = [_stage_peers(stage) for stage in stages]
    barrier = pltpu.get_barrier_semaphore()
    count = 0
    for _, _, peers in plan:
        for peer in peers:
            pl.semaphore_signal(barrier, inc=1, device_id=peer, device_id_type=MESH)
            count += 1
    for _, _, target in routes:
        pl.semaphore_signal(barrier, inc=1, device_id=target, device_id_type=MESH)
        count += 1
    pl.semaphore_wait(barrier, count)
    halo = []
    for k, (row, rows, target) in enumerate(routes):
        copy = pltpu.make_async_remote_copy(
            src_ref=f_ref.at[pl.ds(row, rows)], dst_ref=hrecv.at[pl.ds(row, rows)],
            send_sem=hsend.at[k], recv_sem=hget.at[k], device_id=target, device_id_type=MESH)
        copy.start()
        halo.append(copy)
    total = x_ref[...]
    slot = 0
    for s, (position, size, peers) in enumerate(plan):
        source = x_ref if s == 0 else buf.at[s - 1]
        recv[slot] = total
        sends = []
        for d, peer in enumerate(peers, start=1):
            copy = pltpu.make_async_remote_copy(
                src_ref=source, dst_ref=recv.at[slot + d], send_sem=ssem.at[slot + d],
                recv_sem=rsem.at[slot + d], device_id=peer, device_id_type=MESH)
            copy.start()
            sends.append(copy)
        for copy in sends:
            copy.wait()
        total = recv[slot + position]
        for p in range(1, size):
            total = total + recv[slot + lax.rem(position - p + size, size)]
        slot += size
        if s + 1 < len(plan):
            buf[s] = total
    o_ref[...] = total
    for copy in halo:
        copy.wait()
    h_ref[...] = hrecv[...]


def tv_exchange(x, cells, stages):
    faces = faces_of(cells)
    slots = sum(math.prod(size for _, _, size in stage) for stage in stages)
    return pl.pallas_call(
        functools.partial(tv_exchange_kernel, stages, (cells.shape[1], cells.shape[0])),
        out_shape=(jax.ShapeDtypeStruct(x.shape, x.dtype), jax.ShapeDtypeStruct(faces.shape, faces.dtype)),
        in_specs=[pl.BlockSpec(memory_space=pltpu.VMEM)] * 2,
        out_specs=(pl.BlockSpec(memory_space=pltpu.VMEM), pl.BlockSpec(memory_space=pltpu.VMEM)),
        scratch_shapes=[
            pltpu.VMEM((max(len(stages) - 1, 1),) + x.shape, x.dtype),
            pltpu.VMEM((slots,) + x.shape, x.dtype),
            pltpu.SemaphoreType.DMA((slots,)),
            pltpu.SemaphoreType.DMA((slots,)),
            pltpu.VMEM(faces.shape, faces.dtype),
            pltpu.SemaphoreType.DMA((6,)),
            pltpu.SemaphoreType.DMA((6,)),
        ],
        compiler_params=pltpu.CompilerParams(collective_id=3, has_side_effects=True),
    )(x, faces)


def halo_exchange_kernel(shape, f_ref, h_ref, hrecv, hsend, hget):
    routes = halo_routes(*shape)
    barrier = pltpu.get_barrier_semaphore()
    for _, _, target in routes:
        pl.semaphore_signal(barrier, inc=1, device_id=target, device_id_type=MESH)
    pl.semaphore_wait(barrier, len(routes))
    halo = []
    for k, (row, rows, target) in enumerate(routes):
        copy = pltpu.make_async_remote_copy(
            src_ref=f_ref.at[pl.ds(row, rows)], dst_ref=hrecv.at[pl.ds(row, rows)],
            send_sem=hsend.at[k], recv_sem=hget.at[k], device_id=target, device_id_type=MESH)
        copy.start()
        halo.append(copy)
    for copy in halo:
        copy.wait()
    h_ref[...] = hrecv[...]


def halo_exchange(cells):
    faces = faces_of(cells)
    return pl.pallas_call(
        functools.partial(halo_exchange_kernel, (cells.shape[1], cells.shape[0])),
        out_shape=jax.ShapeDtypeStruct(faces.shape, faces.dtype),
        in_specs=[pl.BlockSpec(memory_space=pltpu.VMEM)],
        out_specs=pl.BlockSpec(memory_space=pltpu.VMEM),
        scratch_shapes=[
            pltpu.VMEM(faces.shape, faces.dtype),
            pltpu.SemaphoreType.DMA((6,)),
            pltpu.SemaphoreType.DMA((6,)),
        ],
        compiler_params=pltpu.CompilerParams(collective_id=4, has_side_effects=True),
    )(faces)


def faces_of(cells):
    return jnp.concatenate(
        [cells[-1], cells[0], cells[:, -1], cells[:, 0], cells[-1, :1], cells[0, -1:]], axis=0)


def padded_from(cells, halo):
    count_z, count_x = lax.axis_size("gz"), lax.axis_size("gx")
    z, x = lax.axis_index("gz"), lax.axis_index("gx")
    depth, width = cells.shape[1], cells.shape[0]
    low_z = jnp.where(z > 0, halo[:depth], 0.0)[None]
    high_z = jnp.where(z < count_z - 1, halo[depth:2 * depth], 0.0)[None]
    low_x = jnp.where(x > 0, halo[2 * depth:2 * depth + width], 0.0)[:, None]
    high_x = jnp.where(x < count_x - 1, halo[2 * depth + width:2 * depth + 2 * width], 0.0)[:, None]
    corner = 2 * depth + 2 * width
    low_z_high_x = jnp.where((z > 0) & (x < count_x - 1), halo[corner:corner + 1], 0.0)[None]
    high_z_low_x = jnp.where((z < count_z - 1) & (x > 0), halo[corner + 1:corner + 2], 0.0)[None]
    zero_line = jnp.zeros_like(cells[:1, :1])
    top = jnp.concatenate([zero_line, low_z, low_z_high_x], axis=1)
    middle = jnp.concatenate([low_x, cells, high_x], axis=1)
    bottom = jnp.concatenate([high_z_low_x, high_z, zero_line], axis=1)
    return jnp.concatenate([top, middle, bottom], axis=0)


def scalar_stages(n_gz, n_gx):
    if n_gx % 4 == 0 and n_gx > 4:
        return [[("gz", 1, n_gz), ("gx", 1, 4)], [("gx", 4, n_gx // 4)]]
    return [[("gz", 1, n_gz)], [("gx", 1, n_gx)]]


def pack_pair(a, b):
    lane = lax.broadcasted_iota(jnp.int32, (8, 128), 1)
    return jnp.where(lane == 0, a, jnp.where(lane == 1, b, 0.0)).astype(jnp.float32)


def one_hot(index, size):
    return (index[:, None] == jnp.arange(size, dtype=jnp.int32)[None, :]).astype(jnp.bfloat16)


def block_apply_kernel(group, transposed, x_ref, blk_ref, w_ref, o_ref):
    o_ref[...] = jnp.zeros_like(o_ref)
    x = x_ref[...]
    chosen = blk_ref[...]
    zero = jnp.zeros_like(x)
    dims = (((1,), (1,)), ((), ())) if transposed else (((1,), (0,)), ((), ()))

    def step(p, carry):
        parts = [jnp.where(chosen == p * group + i, x, zero) for i in range(group)]
        joined = jnp.concatenate(parts, axis=1)
        weights = jnp.concatenate(
            [w_ref[p * group + i] for i in range(group)], axis=1 if transposed else 0)
        o_ref[...] += lax.dot_general(joined, weights, dims, preferred_element_type=jnp.float32)
        return carry

    lax.fori_loop(0, w_ref.shape[0] // group, step, 0)


def block_apply(x, chosen, weights, group, transposed):
    entries, width = x.shape
    flops = 2 * entries * width * width * weights.shape[0]
    return pl.pallas_call(
        functools.partial(block_apply_kernel, group, transposed),
        out_shape=jax.ShapeDtypeStruct((entries, width), jnp.float32),
        in_specs=[pl.BlockSpec(memory_space=pltpu.VMEM)] * 3,
        out_specs=pl.BlockSpec(memory_space=pltpu.VMEM),
        cost_estimate=pl.CostEstimate(
            flops=flops, transcendentals=0, bytes_accessed=weights.size * 2 + entries * width * 10),
    )(x, chosen, weights)


def shift_from(block, pairs_of):
    count_z, count_x = lax.axis_size("gz"), lax.axis_size("gx")
    pairs = []
    for z in range(count_z):
        for x in range(count_x):
            target = pairs_of(z, x)
            if 0 <= target[0] < count_z and 0 <= target[1] < count_x:
                pairs.append((z * count_x + x, target[0] * count_x + target[1]))
    return lax.ppermute(block, ("gz", "gx"), pairs)


def padded_2(cells):
    zero_line = jnp.zeros_like(cells[:1, :1])
    low_z = shift_from(cells[-1:], lambda z, x: (z + 1, x))
    high_z = shift_from(cells[:1], lambda z, x: (z - 1, x))
    low_x = shift_from(cells[:, -1:], lambda z, x: (z, x + 1))
    high_x = shift_from(cells[:, :1], lambda z, x: (z, x - 1))
    low_z_high_x = shift_from(cells[-1:, :1], lambda z, x: (z + 1, x - 1))
    high_z_low_x = shift_from(cells[:1, -1:], lambda z, x: (z - 1, x + 1))
    top = jnp.concatenate([zero_line, low_z, low_z_high_x], axis=1)
    middle = jnp.concatenate([low_x, cells, high_x], axis=1)
    bottom = jnp.concatenate([high_z_low_x, high_z, zero_line], axis=1)
    return jnp.concatenate([top, middle, bottom], axis=0)


def tv_grad(padded):
    base_cells = padded[:-1, :-1, :-1]
    diff_z = padded[1:, :-1, :-1] - base_cells
    diff_x = padded[:-1, 1:, :-1] - base_cells
    diff_y = padded[:-1, :-1, 1:] - base_cells
    inverse = lax.rsqrt(diff_z * diff_z + diff_x * diff_x + diff_y * diff_y + smooth_floor)
    flow_z = diff_z * inverse
    flow_x = diff_x * inverse
    flow_y = diff_y * inverse
    flow_all = flow_z + flow_x + flow_y
    return flow_z[:-1, 1:, 1:] + flow_x[1:, :-1, 1:] + flow_y[1:, 1:, :-1] - flow_all[1:, 1:, 1:]


def pad_depth(field):
    return jnp.pad(field, ((0, 0), (0, 0), (1, 1)))


def body(
    volume, measured, weight_blocks, view_order, tile_voxel, tile_column, tile_block, entry_count
):
    depth_z, depth_x, depth_y = volume.shape
    tiles_y = depth_y // group_rows
    tiles_u = measured.shape[2] // group_rows
    slab_tiles = depth_z * tiles_u
    plane_tiles = depth_x * tiles_y
    row_weight = jnp.sum(weight_blocks, axis=2, dtype=jnp.float32)
    col_weight = jnp.sum(weight_blocks, axis=1, dtype=jnp.float32)
    n_blocks = weight_blocks.shape[0]
    group = 4 if n_blocks % 4 == 0 else 1
    current = volume
    for turn_index in range(view_order.shape[0]):
        view_index = view_order[turn_index]
        voxel_list = lax.dynamic_index_in_dim(tile_voxel, view_index, 0, keepdims=False)[0]
        column_list = lax.dynamic_index_in_dim(tile_column, view_index, 0, keepdims=False)[0]
        block_list = lax.dynamic_index_in_dim(tile_block, view_index, 0, keepdims=False)[0]
        live_count = lax.dynamic_index_in_dim(entry_count, view_index, 0, keepdims=False)[0, 0]
        entries = voxel_list.shape[0]
        live = (jnp.arange(entries, dtype=jnp.int32) < live_count)[:, None]
        detector = voxel_list // plane_tiles * tiles_u + column_list
        voxel_tiles = current.astype(jnp.bfloat16).reshape(-1, group_rows)
        pick_voxel = one_hot(voxel_list, voxel_tiles.shape[0])
        pick_detector = one_hot(detector, slab_tiles)
        pick_block = jnp.where(live, one_hot(block_list, n_blocks), 0)
        blocks_column = block_list[:, None]

        cells = jnp.dot(pick_voxel, voxel_tiles, preferred_element_type=jnp.float32)
        product = block_apply(cells.astype(jnp.bfloat16), blocks_column, weight_blocks, group, True)
        product = jnp.where(live, product, 0.0)
        projection = lax.dot_general(
            pick_detector.astype(jnp.float32), product, (((0,), (0,)), ((), ())),
            precision=lax.Precision.HIGHEST)
        detector_blocks = lax.dot_general(
            pick_detector, pick_block, (((0,), (0,)), ((), ())), preferred_element_type=jnp.float32)
        ray_sum = jnp.dot(detector_blocks, row_weight, precision=lax.Precision.HIGHEST)
        target = lax.dynamic_index_in_dim(measured, view_index, 0, keepdims=False).reshape(
            slab_tiles, group_rows
        )
        n_gx = lax.axis_size("gx")
        joined = jnp.concatenate([projection, ray_sum], axis=1).astype(jnp.bfloat16)
        joined = vector_sum(joined.reshape(n_gx, slab_tiles // n_gx, 2 * group_rows))
        joined = joined.reshape(slab_tiles, 2 * group_rows).astype(jnp.float32)
        projection, ray_sum = joined[:, :group_rows], joined[:, group_rows:]
        residual = ((target - projection) / (ray_sum + 1.0)).astype(jnp.bfloat16)

        pixels = jnp.dot(pick_detector, residual, preferred_element_type=jnp.float32)
        product = block_apply(pixels.astype(jnp.bfloat16), blocks_column, weight_blocks, group, False)
        product = jnp.where(live, product, 0.0)
        change = lax.dot_general(
            pick_voxel.astype(jnp.float32), product, (((0,), (0,)), ((), ())),
            precision=lax.Precision.HIGHEST)
        voxel_blocks = lax.dot_general(
            pick_voxel, pick_block, (((0,), (0,)), ((), ())), preferred_element_type=jnp.float32)
        voxel_sum = jnp.dot(voxel_blocks, col_weight, precision=lax.Precision.HIGHEST)
        current = current + (change / (voxel_sum + 1.0)).reshape(current.shape)
    art_volume = jnp.maximum(current, 0.0)
    difference = art_volume - volume
    change_part = jnp.sum(difference * difference)
    stages = scalar_stages(lax.axis_size("gz"), lax.axis_size("gx"))
    padded = padded_from(art_volume, halo_exchange(art_volume))
    change_total = None
    smooth = art_volume
    for sweep_index in range(TV_STEPS):
        slope = tv_grad(pad_depth(padded))
        slope_part = jnp.sum(slope * slope)
        totals, halo = tv_exchange(
            pack_pair(slope_part, change_part if sweep_index == 0 else 0.0), slope, stages)
        if sweep_index == 0:
            change_total = totals[0, 1]
        slope_total = totals[0, 0]
        scale_now = step_gain * jnp.sqrt(change_total) / jnp.sqrt(slope_total + norm_floor)
        smooth = smooth - scale_now * slope
        if sweep_index + 1 < TV_STEPS:
            padded = padded - scale_now * padded_from(slope, halo)
    return smooth


def solution(mesh):
    return jax.shard_map(
        body,
        mesh=mesh,
        in_specs=(
            P("gz", "gx", None),
            P(None, "gz", None),
            P(),
            P(),
            P(None, "gz", "gx"),
            P(None, "gz", "gx"),
            P(None, "gz", "gx"),
            P(None, "gz", "gx"),
        ),
        out_specs=P("gz", "gx", None),
        check_vma=False,
    )
```

```python
import functools
import math

import jax
import jax.numpy as jnp
from jax import lax
from jax.experimental import pallas as pl
from jax.experimental.pallas import tpu as pltpu
from jax.sharding import PartitionSpec as P

TV_STEPS = 4


smooth_floor = 0.01
step_gain = 0.25
norm_floor = 1e-06
group_rows = 128


MESH = pl.DeviceIdType.MESH


def _peer(axis, position):
    if axis == "gz":
        return (position, lax.axis_index("gx"))
    return (lax.axis_index("gz"), position)


def vector_sum_kernel(n, x_ref, o_ref, recv, red, gath, ssem1, rsem1, ssem2, rsem2):
    me = lax.axis_index("gx")
    barrier = pltpu.get_barrier_semaphore()
    for d in range(1, n):
        pl.semaphore_signal(barrier, inc=1, device_id=_peer("gx", lax.rem(me + d, n)), device_id_type=MESH)
    pl.semaphore_wait(barrier, n - 1)

    def scatter_copy(d):
        dst = lax.rem(me + d, n)
        return pltpu.make_async_remote_copy(
            src_ref=x_ref.at[dst], dst_ref=recv.at[d], send_sem=ssem1.at[d], recv_sem=rsem1.at[d],
            device_id=_peer("gx", dst), device_id_type=MESH)

    def gather_copy(d):
        dst = lax.rem(me + d, n)
        return pltpu.make_async_remote_copy(
            src_ref=red, dst_ref=gath.at[me], send_sem=ssem2.at[d], recv_sem=rsem2.at[d],
            device_id=_peer("gx", dst), device_id_type=MESH)

    @pl.loop(1, n)
    def _(d):
        scatter_copy(d).start()

    @pl.loop(1, n)
    def _(d):
        scatter_copy(d).wait()

    total = lax.fori_loop(
        1, n, lambda d, acc: acc + recv[d].astype(jnp.float32), x_ref[me].astype(jnp.float32))
    red[...] = total.astype(red.dtype)

    @pl.loop(1, n)
    def _(d):
        gather_copy(d).start()

    @pl.loop(1, n)
    def _(d):
        gather_copy(d).wait()

    gath[me] = red[...]
    o_ref[...] = gath[...]


def vector_sum(x):
    n, rows, cols = x.shape
    return pl.pallas_call(
        functools.partial(vector_sum_kernel, n),
        out_shape=jax.ShapeDtypeStruct(x.shape, x.dtype),
        in_specs=[pl.BlockSpec(memory_space=pltpu.VMEM)],
        out_specs=pl.BlockSpec(memory_space=pltpu.VMEM),
        scratch_shapes=[
            pltpu.VMEM(x.shape, x.dtype),
            pltpu.VMEM((rows, cols), x.dtype),
            pltpu.VMEM(x.shape, x.dtype),
            pltpu.SemaphoreType.DMA((n,)),
            pltpu.SemaphoreType.DMA((n,)),
            pltpu.SemaphoreType.DMA((n,)),
            pltpu.SemaphoreType.DMA((n,)),
        ],
        compiler_params=pltpu.CompilerParams(collective_id=1, has_side_effects=True),
    )(x)


def _stage_peers(stage):
    if isinstance(stage[0], str):
        stage = [stage]
    index = {axis: lax.axis_index(axis) for axis, _, _ in stage}
    digits = [lax.rem(index[axis] // stride, size) for axis, stride, size in stage]
    total = 1
    position = 0
    for (_, _, size), digit in zip(stage, digits):
        position = position * size + digit
        total *= size
    peers = []
    for d in range(1, total):
        q = lax.rem(position + d, total)
        coords = dict(index)
        rest = total
        for (axis, stride, size), digit in zip(stage, digits):
            rest //= size
            coords[axis] = coords[axis] + (lax.rem(q // rest, size) - digit) * stride
        peers.append((coords.get("gz", lax.axis_index("gz")), coords.get("gx", lax.axis_index("gx"))))
    return position, total, peers


def fill_faces(c_ref, faces, depth, width):
    faces[pl.ds(0, depth)] = c_ref[width - 1]
    faces[pl.ds(depth, depth)] = c_ref[0]
    faces[pl.ds(2 * depth, width)] = c_ref[:, depth - 1, :]
    faces[pl.ds(2 * depth + width, width)] = c_ref[:, 0, :]
    faces[pl.ds(2 * depth + 2 * width, 1)] = c_ref[width - 1, pl.ds(0, 1), :]
    faces[pl.ds(2 * depth + 2 * width + 1, 1)] = c_ref[0, pl.ds(depth - 1, 1), :]


def halo_routes(depth, width):
    count_z, count_x = lax.axis_size("gz"), lax.axis_size("gx")
    z, x = lax.axis_index("gz"), lax.axis_index("gx")
    up_z, down_z = lax.rem(z + 1, count_z), lax.rem(z + count_z - 1, count_z)
    up_x, down_x = lax.rem(x + 1, count_x), lax.rem(x + count_x - 1, count_x)
    return [
        (0, depth, (up_z, x)),
        (depth, depth, (down_z, x)),
        (2 * depth, width, (z, up_x)),
        (2 * depth + width, width, (z, down_x)),
        (2 * depth + 2 * width, 1, (up_z, down_x)),
        (2 * depth + 2 * width + 1, 1, (down_z, up_x)),
    ]


def tv_exchange_kernel(stages, shape, x_ref, c_ref, o_ref, h_ref, buf, recv, ssem, rsem, hrecv, hsend, hget, f_ref):
    routes = halo_routes(*shape)
    fill_faces(c_ref, f_ref, *shape)
    plan = [_stage_peers(stage) for stage in stages]
    barrier = pltpu.get_barrier_semaphore()
    count = 0
    for _, _, peers in plan:
        for peer in peers:
            pl.semaphore_signal(barrier, inc=1, device_id=peer, device_id_type=MESH)
            count += 1
    for _, _, target in routes:
        pl.semaphore_signal(barrier, inc=1, device_id=target, device_id_type=MESH)
        count += 1
    pl.semaphore_wait(barrier, count)
    halo = []
    for k, (row, rows, target) in enumerate(routes):
        copy = pltpu.make_async_remote_copy(
            src_ref=f_ref.at[pl.ds(row, rows)], dst_ref=hrecv.at[pl.ds(row, rows)],
            send_sem=hsend.at[k], recv_sem=hget.at[k], device_id=target, device_id_type=MESH)
        copy.start()
        halo.append(copy)
    total = x_ref[...]
    slot = 0
    for s, (position, size, peers) in enumerate(plan):
        source = x_ref if s == 0 else buf.at[s - 1]
        recv[slot] = total
        sends = []
        for d, peer in enumerate(peers, start=1):
            copy = pltpu.make_async_remote_copy(
                src_ref=source, dst_ref=recv.at[slot + d], send_sem=ssem.at[slot + d],
                recv_sem=rsem.at[slot + d], device_id=peer, device_id_type=MESH)
            copy.start()
            sends.append(copy)
        for copy in sends:
            copy.wait()
        total = recv[slot + position]
        for p in range(1, size):
            total = total + recv[slot + lax.rem(position - p + size, size)]
        slot += size
        if s + 1 < len(plan):
            buf[s] = total
    o_ref[...] = total
    for copy in halo:
        copy.wait()
    h_ref[...] = hrecv[...]


def tv_exchange(x, cells, stages):
    width, depth, lanes = cells.shape
    rows = 2 * depth + 2 * width + 2
    slots = sum(math.prod(size for _, _, size in stage) for stage in stages)
    return pl.pallas_call(
        functools.partial(tv_exchange_kernel, stages, (depth, width)),
        out_shape=(jax.ShapeDtypeStruct(x.shape, x.dtype), jax.ShapeDtypeStruct((rows, lanes), cells.dtype)),
        in_specs=[pl.BlockSpec(memory_space=pltpu.VMEM)] * 2,
        out_specs=(pl.BlockSpec(memory_space=pltpu.VMEM), pl.BlockSpec(memory_space=pltpu.VMEM)),
        scratch_shapes=[
            pltpu.VMEM((max(len(stages) - 1, 1),) + x.shape, x.dtype),
            pltpu.VMEM((slots,) + x.shape, x.dtype),
            pltpu.SemaphoreType.DMA((slots,)),
            pltpu.SemaphoreType.DMA((slots,)),
            pltpu.VMEM((rows, lanes), cells.dtype),
            pltpu.SemaphoreType.DMA((6,)),
            pltpu.SemaphoreType.DMA((6,)),
            pltpu.VMEM((rows, lanes), cells.dtype),
        ],
        compiler_params=pltpu.CompilerParams(collective_id=3, has_side_effects=True),
    )(x, cells)


def halo_exchange_kernel(shape, c_ref, h_ref, hrecv, hsend, hget, f_ref):
    routes = halo_routes(*shape)
    fill_faces(c_ref, f_ref, *shape)
    barrier = pltpu.get_barrier_semaphore()
    for _, _, target in routes:
        pl.semaphore_signal(barrier, inc=1, device_id=target, device_id_type=MESH)
    pl.semaphore_wait(barrier, len(routes))
    halo = []
    for k, (row, rows, target) in enumerate(routes):
        copy = pltpu.make_async_remote_copy(
            src_ref=f_ref.at[pl.ds(row, rows)], dst_ref=hrecv.at[pl.ds(row, rows)],
            send_sem=hsend.at[k], recv_sem=hget.at[k], device_id=target, device_id_type=MESH)
        copy.start()
        halo.append(copy)
    for copy in halo:
        copy.wait()
    h_ref[...] = hrecv[...]


def halo_exchange(cells):
    width, depth, lanes = cells.shape
    rows = 2 * depth + 2 * width + 2
    return pl.pallas_call(
        functools.partial(halo_exchange_kernel, (depth, width)),
        out_shape=jax.ShapeDtypeStruct((rows, lanes), cells.dtype),
        in_specs=[pl.BlockSpec(memory_space=pltpu.VMEM)],
        out_specs=pl.BlockSpec(memory_space=pltpu.VMEM),
        scratch_shapes=[
            pltpu.VMEM((rows, lanes), cells.dtype),
            pltpu.SemaphoreType.DMA((6,)),
            pltpu.SemaphoreType.DMA((6,)),
            pltpu.VMEM((rows, lanes), cells.dtype),
        ],
        compiler_params=pltpu.CompilerParams(collective_id=4, has_side_effects=True),
    )(cells)


def faces_of(cells):
    return jnp.concatenate(
        [cells[-1], cells[0], cells[:, -1], cells[:, 0], cells[-1, :1], cells[0, -1:]], axis=0)


def padded_from(cells, halo):
    count_z, count_x = lax.axis_size("gz"), lax.axis_size("gx")
    z, x = lax.axis_index("gz"), lax.axis_index("gx")
    depth, width = cells.shape[1], cells.shape[0]
    low_z = jnp.where(z > 0, halo[:depth], 0.0)[None]
    high_z = jnp.where(z < count_z - 1, halo[depth:2 * depth], 0.0)[None]
    low_x = jnp.where(x > 0, halo[2 * depth:2 * depth + width], 0.0)[:, None]
    high_x = jnp.where(x < count_x - 1, halo[2 * depth + width:2 * depth + 2 * width], 0.0)[:, None]
    corner = 2 * depth + 2 * width
    low_z_high_x = jnp.where((z > 0) & (x < count_x - 1), halo[corner:corner + 1], 0.0)[None]
    high_z_low_x = jnp.where((z < count_z - 1) & (x > 0), halo[corner + 1:corner + 2], 0.0)[None]
    zero_line = jnp.zeros_like(cells[:1, :1])
    top = jnp.concatenate([zero_line, low_z, low_z_high_x], axis=1)
    middle = jnp.concatenate([low_x, cells, high_x], axis=1)
    bottom = jnp.concatenate([high_z_low_x, high_z, zero_line], axis=1)
    return jnp.concatenate([top, middle, bottom], axis=0)


def scalar_stages(n_gz, n_gx):
    if n_gx % 4 == 0 and n_gx > 4:
        return [[("gz", 1, n_gz), ("gx", 1, 4)], [("gx", 4, n_gx // 4)]]
    return [[("gz", 1, n_gz)], [("gx", 1, n_gx)]]


def pack_pair(a, b):
    lane = lax.broadcasted_iota(jnp.int32, (8, 128), 1)
    return jnp.where(lane == 0, a, jnp.where(lane == 1, b, 0.0)).astype(jnp.float32)


def one_hot(index, size):
    return (index[:, None] == jnp.arange(size, dtype=jnp.int32)[None, :]).astype(jnp.bfloat16)


def block_apply_kernel(group, transposed, x_ref, blk_ref, w_ref, o_ref):
    o_ref[...] = jnp.zeros_like(o_ref)
    x = x_ref[...]
    chosen = blk_ref[...]
    zero = jnp.zeros_like(x)
    dims = (((1,), (1,)), ((), ())) if transposed else (((1,), (0,)), ((), ()))

    def step(p, carry):
        parts = [jnp.where(chosen == p * group + i, x, zero) for i in range(group)]
        joined = jnp.concatenate(parts, axis=1)
        weights = jnp.concatenate(
            [w_ref[p * group + i] for i in range(group)], axis=1 if transposed else 0)
        o_ref[...] += lax.dot_general(joined, weights, dims, preferred_element_type=jnp.float32)
        return carry

    lax.fori_loop(0, w_ref.shape[0] // group, step, 0)


def block_apply(x, chosen, weights, group, transposed):
    entries, width = x.shape
    flops = 2 * entries * width * width * weights.shape[0]
    return pl.pallas_call(
        functools.partial(block_apply_kernel, group, transposed),
        out_shape=jax.ShapeDtypeStruct((entries, width), jnp.float32),
        in_specs=[pl.BlockSpec(memory_space=pltpu.VMEM)] * 3,
        out_specs=pl.BlockSpec(memory_space=pltpu.VMEM),
        cost_estimate=pl.CostEstimate(
            flops=flops, transcendentals=0, bytes_accessed=weights.size * 2 + entries * width * 10),
    )(x, chosen, weights)


def shift_from(block, pairs_of):
    count_z, count_x = lax.axis_size("gz"), lax.axis_size("gx")
    pairs = []
    for z in range(count_z):
        for x in range(count_x):
            target = pairs_of(z, x)
            if 0 <= target[0] < count_z and 0 <= target[1] < count_x:
                pairs.append((z * count_x + x, target[0] * count_x + target[1]))
    return lax.ppermute(block, ("gz", "gx"), pairs)


def padded_2(cells):
    zero_line = jnp.zeros_like(cells[:1, :1])
    low_z = shift_from(cells[-1:], lambda z, x: (z + 1, x))
    high_z = shift_from(cells[:1], lambda z, x: (z - 1, x))
    low_x = shift_from(cells[:, -1:], lambda z, x: (z, x + 1))
    high_x = shift_from(cells[:, :1], lambda z, x: (z, x - 1))
    low_z_high_x = shift_from(cells[-1:, :1], lambda z, x: (z + 1, x - 1))
    high_z_low_x = shift_from(cells[:1, -1:], lambda z, x: (z - 1, x + 1))
    top = jnp.concatenate([zero_line, low_z, low_z_high_x], axis=1)
    middle = jnp.concatenate([low_x, cells, high_x], axis=1)
    bottom = jnp.concatenate([high_z_low_x, high_z, zero_line], axis=1)
    return jnp.concatenate([top, middle, bottom], axis=0)


def tv_grad(padded):
    base_cells = padded[:-1, :-1, :-1]
    diff_z = padded[1:, :-1, :-1] - base_cells
    diff_x = padded[:-1, 1:, :-1] - base_cells
    diff_y = padded[:-1, :-1, 1:] - base_cells
    inverse = lax.rsqrt(diff_z * diff_z + diff_x * diff_x + diff_y * diff_y + smooth_floor)
    flow_z = diff_z * inverse
    flow_x = diff_x * inverse
    flow_y = diff_y * inverse
    flow_all = flow_z + flow_x + flow_y
    return flow_z[:-1, 1:, 1:] + flow_x[1:, :-1, 1:] + flow_y[1:, 1:, :-1] - flow_all[1:, 1:, 1:]


def pad_depth(field):
    return jnp.pad(field, ((0, 0), (0, 0), (1, 1)))


def body(
    volume, measured, weight_blocks, view_order, tile_voxel, tile_column, tile_block, entry_count
):
    depth_z, depth_x, depth_y = volume.shape
    tiles_y = depth_y // group_rows
    tiles_u = measured.shape[2] // group_rows
    slab_tiles = depth_z * tiles_u
    plane_tiles = depth_x * tiles_y
    row_weight = jnp.sum(weight_blocks, axis=2, dtype=jnp.float32)
    col_weight = jnp.sum(weight_blocks, axis=1, dtype=jnp.float32)
    n_blocks = weight_blocks.shape[0]
    group = 4 if n_blocks % 4 == 0 else 1
    current = volume
    for turn_index in range(view_order.shape[0]):
        view_index = view_order[turn_index]
        voxel_list = lax.dynamic_index_in_dim(tile_voxel, view_index, 0, keepdims=False)[0]
        column_list = lax.dynamic_index_in_dim(tile_column, view_index, 0, keepdims=False)[0]
        block_list = lax.dynamic_index_in_dim(tile_block, view_index, 0, keepdims=False)[0]
        live_count = lax.dynamic_index_in_dim(entry_count, view_index, 0, keepdims=False)[0, 0]
        entries = voxel_list.shape[0]
        live = (jnp.arange(entries, dtype=jnp.int32) < live_count)[:, None]
        detector = voxel_list // plane_tiles * tiles_u + column_list
        voxel_tiles = current.astype(jnp.bfloat16).reshape(-1, group_rows)
        pick_voxel = one_hot(voxel_list, voxel_tiles.shape[0])
        pick_detector = one_hot(detector, slab_tiles)
        pick_block = jnp.where(live, one_hot(block_list, n_blocks), 0)
        blocks_column = block_list[:, None]

        cells = jnp.dot(pick_voxel, voxel_tiles, preferred_element_type=jnp.float32)
        product = block_apply(cells.astype(jnp.bfloat16), blocks_column, weight_blocks, group, True)
        product = jnp.where(live, product, 0.0)
        projection = lax.dot_general(
            pick_detector.astype(jnp.float32), product, (((0,), (0,)), ((), ())),
            precision=lax.Precision.HIGHEST)
        detector_blocks = lax.dot_general(
            pick_detector, pick_block, (((0,), (0,)), ((), ())), preferred_element_type=jnp.float32)
        ray_sum = jnp.dot(detector_blocks, row_weight, precision=lax.Precision.HIGHEST)
        target = lax.dynamic_index_in_dim(measured, view_index, 0, keepdims=False).reshape(
            slab_tiles, group_rows
        )
        n_gx = lax.axis_size("gx")
        joined = jnp.concatenate([projection, ray_sum], axis=1).astype(jnp.bfloat16)
        joined = vector_sum(joined.reshape(n_gx, slab_tiles // n_gx, 2 * group_rows))
        joined = joined.reshape(slab_tiles, 2 * group_rows).astype(jnp.float32)
        projection, ray_sum = joined[:, :group_rows], joined[:, group_rows:]
        residual = ((target - projection) / (ray_sum + 1.0)).astype(jnp.bfloat16)

        pixels = jnp.dot(pick_detector, residual, preferred_element_type=jnp.float32)
        product = block_apply(pixels.astype(jnp.bfloat16), blocks_column, weight_blocks, group, False)
        product = jnp.where(live, product, 0.0)
        change = lax.dot_general(
            pick_voxel.astype(jnp.float32), product, (((0,), (0,)), ((), ())),
            precision=lax.Precision.HIGHEST)
        voxel_blocks = lax.dot_general(
            pick_voxel, pick_block, (((0,), (0,)), ((), ())), preferred_element_type=jnp.float32)
        voxel_sum = jnp.dot(voxel_blocks, col_weight, precision=lax.Precision.HIGHEST)
        current = current + (change / (voxel_sum + 1.0)).reshape(current.shape)
    art_volume = jnp.maximum(current, 0.0)
    difference = art_volume - volume
    change_part = jnp.sum(difference * difference)
    stages = scalar_stages(lax.axis_size("gz"), lax.axis_size("gx"))
    padded = padded_from(art_volume, halo_exchange(art_volume))
    change_total = None
    smooth = art_volume
    for sweep_index in range(TV_STEPS):
        slope = tv_grad(pad_depth(padded))
        slope_part = jnp.sum(slope * slope)
        totals, halo = tv_exchange(
            pack_pair(slope_part, change_part if sweep_index == 0 else 0.0), slope, stages)
        if sweep_index == 0:
            change_total = totals[0, 1]
        slope_total = totals[0, 0]
        scale_now = step_gain * jnp.sqrt(change_total) / jnp.sqrt(slope_total + norm_floor)
        smooth = smooth - scale_now * slope
        if sweep_index + 1 < TV_STEPS:
            padded = padded - scale_now * padded_from(slope, halo)
    return smooth


def solution(mesh):
    return jax.shard_map(
        body,
        mesh=mesh,
        in_specs=(
            P("gz", "gx", None),
            P(None, "gz", None),
            P(),
            P(),
            P(None, "gz", "gx"),
            P(None, "gz", "gx"),
            P(None, "gz", "gx"),
            P(None, "gz", "gx"),
        ),
        out_specs=P("gz", "gx", None),
        check_vma=False,
    )
```

```python
import functools
import math

import jax
import jax.numpy as jnp
from jax import lax
from jax.experimental import pallas as pl
from jax.experimental.pallas import tpu as pltpu
from jax.sharding import PartitionSpec as P

TV_STEPS = 4


smooth_floor = 0.01
step_gain = 0.25
norm_floor = 1e-06
group_rows = 128


MESH = pl.DeviceIdType.MESH


def _peer(axis, position):
    if axis == "gz":
        return (position, lax.axis_index("gx"))
    return (lax.axis_index("gz"), position)


def vector_sum_kernel(n, x_ref, o_ref, recv, red, gath, ssem1, rsem1, ssem2, rsem2):
    me = lax.axis_index("gx")
    barrier = pltpu.get_barrier_semaphore()
    for d in range(1, n):
        pl.semaphore_signal(barrier, inc=1, device_id=_peer("gx", lax.rem(me + d, n)), device_id_type=MESH)
    pl.semaphore_wait(barrier, n - 1)

    def scatter_copy(d):
        dst = lax.rem(me + d, n)
        return pltpu.make_async_remote_copy(
            src_ref=x_ref.at[dst], dst_ref=recv.at[d], send_sem=ssem1.at[d], recv_sem=rsem1.at[d],
            device_id=_peer("gx", dst), device_id_type=MESH)

    def gather_copy(d):
        dst = lax.rem(me + d, n)
        return pltpu.make_async_remote_copy(
            src_ref=red, dst_ref=gath.at[me], send_sem=ssem2.at[d], recv_sem=rsem2.at[d],
            device_id=_peer("gx", dst), device_id_type=MESH)

    @pl.loop(1, n)
    def _(d):
        scatter_copy(d).start()

    @pl.loop(1, n)
    def _(d):
        scatter_copy(d).wait()

    total = lax.fori_loop(
        1, n, lambda d, acc: acc + recv[d].astype(jnp.float32), x_ref[me].astype(jnp.float32))
    red[...] = total.astype(red.dtype)

    @pl.loop(1, n)
    def _(d):
        gather_copy(d).start()

    @pl.loop(1, n)
    def _(d):
        gather_copy(d).wait()

    gath[me] = red[...]
    o_ref[...] = gath[...]


def vector_sum(x):
    n, rows, cols = x.shape
    return pl.pallas_call(
        functools.partial(vector_sum_kernel, n),
        out_shape=jax.ShapeDtypeStruct(x.shape, x.dtype),
        in_specs=[pl.BlockSpec(memory_space=pltpu.VMEM)],
        out_specs=pl.BlockSpec(memory_space=pltpu.VMEM),
        scratch_shapes=[
            pltpu.VMEM(x.shape, x.dtype),
            pltpu.VMEM((rows, cols), x.dtype),
            pltpu.VMEM(x.shape, x.dtype),
            pltpu.SemaphoreType.DMA((n,)),
            pltpu.SemaphoreType.DMA((n,)),
            pltpu.SemaphoreType.DMA((n,)),
            pltpu.SemaphoreType.DMA((n,)),
        ],
        compiler_params=pltpu.CompilerParams(collective_id=1, has_side_effects=True),
    )(x)


def _stage_peers(stage):
    if isinstance(stage[0], str):
        stage = [stage]
    index = {axis: lax.axis_index(axis) for axis, _, _ in stage}
    digits = [lax.rem(index[axis] // stride, size) for axis, stride, size in stage]
    total = 1
    position = 0
    for (_, _, size), digit in zip(stage, digits):
        position = position * size + digit
        total *= size
    peers = []
    for d in range(1, total):
        q = lax.rem(position + d, total)
        coords = dict(index)
        rest = total
        for (axis, stride, size), digit in zip(stage, digits):
            rest //= size
            coords[axis] = coords[axis] + (lax.rem(q // rest, size) - digit) * stride
        peers.append((coords.get("gz", lax.axis_index("gz")), coords.get("gx", lax.axis_index("gx"))))
    return position, total, peers


def fill_faces(c_ref, faces, depth, width):
    faces[pl.ds(0, depth)] = c_ref[width - 1]
    faces[pl.ds(depth, depth)] = c_ref[0]
    faces[pl.ds(2 * depth, width)] = c_ref[:, depth - 1, :]
    faces[pl.ds(2 * depth + width, width)] = c_ref[:, 0, :]
    faces[pl.ds(2 * depth + 2 * width, 1)] = c_ref[width - 1, pl.ds(0, 1), :]
    faces[pl.ds(2 * depth + 2 * width + 1, 1)] = c_ref[0, pl.ds(depth - 1, 1), :]


def write_halo(h_ref, hrecv, depth, width):
    count_z, count_x = lax.axis_size("gz"), lax.axis_size("gx")
    z, x = lax.axis_index("gz"), lax.axis_index("gx")
    corner = 2 * depth + 2 * width
    parts = [
        (0, depth, z > 0),
        (depth, depth, z < count_z - 1),
        (2 * depth, width, x > 0),
        (2 * depth + width, width, x < count_x - 1),
        (corner, 1, (z > 0) & (x < count_x - 1)),
        (corner + 1, 1, (z < count_z - 1) & (x > 0)),
    ]
    for row, rows, keep in parts:
        values = hrecv[pl.ds(row, rows)]
        h_ref[pl.ds(row, rows)] = jnp.where(keep, values, jnp.zeros_like(values))


def halo_routes(depth, width):
    count_z, count_x = lax.axis_size("gz"), lax.axis_size("gx")
    z, x = lax.axis_index("gz"), lax.axis_index("gx")
    up_z, down_z = lax.rem(z + 1, count_z), lax.rem(z + count_z - 1, count_z)
    up_x, down_x = lax.rem(x + 1, count_x), lax.rem(x + count_x - 1, count_x)
    return [
        (0, depth, (up_z, x)),
        (depth, depth, (down_z, x)),
        (2 * depth, width, (z, up_x)),
        (2 * depth + width, width, (z, down_x)),
        (2 * depth + 2 * width, 1, (up_z, down_x)),
        (2 * depth + 2 * width + 1, 1, (down_z, up_x)),
    ]


def tv_exchange_kernel(stages, shape, x_ref, c_ref, o_ref, h_ref, buf, recv, ssem, rsem, hrecv, hsend, hget, f_ref):
    routes = halo_routes(*shape)
    fill_faces(c_ref, f_ref, *shape)
    plan = [_stage_peers(stage) for stage in stages]
    barrier = pltpu.get_barrier_semaphore()
    count = 0
    for _, _, peers in plan:
        for peer in peers:
            pl.semaphore_signal(barrier, inc=1, device_id=peer, device_id_type=MESH)
            count += 1
    for _, _, target in routes:
        pl.semaphore_signal(barrier, inc=1, device_id=target, device_id_type=MESH)
        count += 1
    pl.semaphore_wait(barrier, count)
    halo = []
    for k, (row, rows, target) in enumerate(routes):
        copy = pltpu.make_async_remote_copy(
            src_ref=f_ref.at[pl.ds(row, rows)], dst_ref=hrecv.at[pl.ds(row, rows)],
            send_sem=hsend.at[k], recv_sem=hget.at[k], device_id=target, device_id_type=MESH)
        copy.start()
        halo.append(copy)
    total = x_ref[...]
    slot = 0
    for s, (position, size, peers) in enumerate(plan):
        source = x_ref if s == 0 else buf.at[s - 1]
        recv[slot] = total
        sends = []
        for d, peer in enumerate(peers, start=1):
            copy = pltpu.make_async_remote_copy(
                src_ref=source, dst_ref=recv.at[slot + d], send_sem=ssem.at[slot + d],
                recv_sem=rsem.at[slot + d], device_id=peer, device_id_type=MESH)
            copy.start()
            sends.append(copy)
        for copy in sends:
            copy.wait()
        total = recv[slot + position]
        for p in range(1, size):
            total = total + recv[slot + lax.rem(position - p + size, size)]
        slot += size
        if s + 1 < len(plan):
            buf[s] = total
    o_ref[...] = total
    for copy in halo:
        copy.wait()
    write_halo(h_ref, hrecv, *shape)


def tv_exchange(x, cells, stages):
    width, depth, lanes = cells.shape
    rows = 2 * depth + 2 * width + 2
    slots = sum(math.prod(size for _, _, size in stage) for stage in stages)
    return pl.pallas_call(
        functools.partial(tv_exchange_kernel, stages, (depth, width)),
        out_shape=(jax.ShapeDtypeStruct(x.shape, x.dtype), jax.ShapeDtypeStruct((rows, lanes), cells.dtype)),
        in_specs=[pl.BlockSpec(memory_space=pltpu.VMEM)] * 2,
        out_specs=(pl.BlockSpec(memory_space=pltpu.VMEM), pl.BlockSpec(memory_space=pltpu.VMEM)),
        scratch_shapes=[
            pltpu.VMEM((max(len(stages) - 1, 1),) + x.shape, x.dtype),
            pltpu.VMEM((slots,) + x.shape, x.dtype),
            pltpu.SemaphoreType.DMA((slots,)),
            pltpu.SemaphoreType.DMA((slots,)),
            pltpu.VMEM((rows, lanes), cells.dtype),
            pltpu.SemaphoreType.DMA((6,)),
            pltpu.SemaphoreType.DMA((6,)),
            pltpu.VMEM((rows, lanes), cells.dtype),
        ],
        compiler_params=pltpu.CompilerParams(collective_id=3, has_side_effects=True),
    )(x, cells)


def halo_exchange_kernel(shape, c_ref, h_ref, hrecv, hsend, hget, f_ref):
    routes = halo_routes(*shape)
    fill_faces(c_ref, f_ref, *shape)
    barrier = pltpu.get_barrier_semaphore()
    for _, _, target in routes:
        pl.semaphore_signal(barrier, inc=1, device_id=target, device_id_type=MESH)
    pl.semaphore_wait(barrier, len(routes))
    halo = []
    for k, (row, rows, target) in enumerate(routes):
        copy = pltpu.make_async_remote_copy(
            src_ref=f_ref.at[pl.ds(row, rows)], dst_ref=hrecv.at[pl.ds(row, rows)],
            send_sem=hsend.at[k], recv_sem=hget.at[k], device_id=target, device_id_type=MESH)
        copy.start()
        halo.append(copy)
    for copy in halo:
        copy.wait()
    write_halo(h_ref, hrecv, *shape)


def halo_exchange(cells):
    width, depth, lanes = cells.shape
    rows = 2 * depth + 2 * width + 2
    return pl.pallas_call(
        functools.partial(halo_exchange_kernel, (depth, width)),
        out_shape=jax.ShapeDtypeStruct((rows, lanes), cells.dtype),
        in_specs=[pl.BlockSpec(memory_space=pltpu.VMEM)],
        out_specs=pl.BlockSpec(memory_space=pltpu.VMEM),
        scratch_shapes=[
            pltpu.VMEM((rows, lanes), cells.dtype),
            pltpu.SemaphoreType.DMA((6,)),
            pltpu.SemaphoreType.DMA((6,)),
            pltpu.VMEM((rows, lanes), cells.dtype),
        ],
        compiler_params=pltpu.CompilerParams(collective_id=4, has_side_effects=True),
    )(cells)


def faces_of(cells):
    return jnp.concatenate(
        [cells[-1], cells[0], cells[:, -1], cells[:, 0], cells[-1, :1], cells[0, -1:]], axis=0)


def padded_from(cells, halo):
    depth, width = cells.shape[1], cells.shape[0]
    low_z = halo[:depth][None]
    high_z = halo[depth:2 * depth][None]
    low_x = halo[2 * depth:2 * depth + width][:, None]
    high_x = halo[2 * depth + width:2 * depth + 2 * width][:, None]
    corner = 2 * depth + 2 * width
    low_z_high_x = halo[corner:corner + 1][None]
    high_z_low_x = halo[corner + 1:corner + 2][None]
    zero_line = jnp.zeros_like(cells[:1, :1])
    top = jnp.concatenate([zero_line, low_z, low_z_high_x], axis=1)
    middle = jnp.concatenate([low_x, cells, high_x], axis=1)
    bottom = jnp.concatenate([high_z_low_x, high_z, zero_line], axis=1)
    return jnp.concatenate([top, middle, bottom], axis=0)


def scalar_stages(n_gz, n_gx):
    if n_gx % 4 == 0 and n_gx > 4:
        return [[("gz", 1, n_gz), ("gx", 1, 4)], [("gx", 4, n_gx // 4)]]
    return [[("gz", 1, n_gz)], [("gx", 1, n_gx)]]


def pack_pair(a, b):
    lane = lax.broadcasted_iota(jnp.int32, (8, 128), 1)
    return jnp.where(lane == 0, a, jnp.where(lane == 1, b, 0.0)).astype(jnp.float32)


def one_hot(index, size):
    return (index[:, None] == jnp.arange(size, dtype=jnp.int32)[None, :]).astype(jnp.bfloat16)


def block_apply_kernel(group, transposed, x_ref, blk_ref, w_ref, o_ref):
    o_ref[...] = jnp.zeros_like(o_ref)
    x = x_ref[...]
    chosen = blk_ref[...]
    zero = jnp.zeros_like(x)
    dims = (((1,), (1,)), ((), ())) if transposed else (((1,), (0,)), ((), ()))

    def step(p, carry):
        parts = [jnp.where(chosen == p * group + i, x, zero) for i in range(group)]
        joined = jnp.concatenate(parts, axis=1)
        weights = jnp.concatenate(
            [w_ref[p * group + i] for i in range(group)], axis=1 if transposed else 0)
        o_ref[...] += lax.dot_general(joined, weights, dims, preferred_element_type=jnp.float32)
        return carry

    lax.fori_loop(0, w_ref.shape[0] // group, step, 0)


def block_apply(x, chosen, weights, group, transposed):
    entries, width = x.shape
    flops = 2 * entries * width * width * weights.shape[0]
    return pl.pallas_call(
        functools.partial(block_apply_kernel, group, transposed),
        out_shape=jax.ShapeDtypeStruct((entries, width), jnp.float32),
        in_specs=[pl.BlockSpec(memory_space=pltpu.VMEM)] * 3,
        out_specs=pl.BlockSpec(memory_space=pltpu.VMEM),
        cost_estimate=pl.CostEstimate(
            flops=flops, transcendentals=0, bytes_accessed=weights.size * 2 + entries * width * 10),
    )(x, chosen, weights)


def shift_from(block, pairs_of):
    count_z, count_x = lax.axis_size("gz"), lax.axis_size("gx")
    pairs = []
    for z in range(count_z):
        for x in range(count_x):
            target = pairs_of(z, x)
            if 0 <= target[0] < count_z and 0 <= target[1] < count_x:
                pairs.append((z * count_x + x, target[0] * count_x + target[1]))
    return lax.ppermute(block, ("gz", "gx"), pairs)


def padded_2(cells):
    zero_line = jnp.zeros_like(cells[:1, :1])
    low_z = shift_from(cells[-1:], lambda z, x: (z + 1, x))
    high_z = shift_from(cells[:1], lambda z, x: (z - 1, x))
    low_x = shift_from(cells[:, -1:], lambda z, x: (z, x + 1))
    high_x = shift_from(cells[:, :1], lambda z, x: (z, x - 1))
    low_z_high_x = shift_from(cells[-1:, :1], lambda z, x: (z + 1, x - 1))
    high_z_low_x = shift_from(cells[:1, -1:], lambda z, x: (z - 1, x + 1))
    top = jnp.concatenate([zero_line, low_z, low_z_high_x], axis=1)
    middle = jnp.concatenate([low_x, cells, high_x], axis=1)
    bottom = jnp.concatenate([high_z_low_x, high_z, zero_line], axis=1)
    return jnp.concatenate([top, middle, bottom], axis=0)


def tv_grad(padded):
    base_cells = padded[:-1, :-1, :-1]
    diff_z = padded[1:, :-1, :-1] - base_cells
    diff_x = padded[:-1, 1:, :-1] - base_cells
    diff_y = padded[:-1, :-1, 1:] - base_cells
    inverse = lax.rsqrt(diff_z * diff_z + diff_x * diff_x + diff_y * diff_y + smooth_floor)
    flow_z = diff_z * inverse
    flow_x = diff_x * inverse
    flow_y = diff_y * inverse
    flow_all = flow_z + flow_x + flow_y
    return flow_z[:-1, 1:, 1:] + flow_x[1:, :-1, 1:] + flow_y[1:, 1:, :-1] - flow_all[1:, 1:, 1:]


def pad_depth(field):
    return jnp.pad(field, ((0, 0), (0, 0), (1, 1)))


def body(
    volume, measured, weight_blocks, view_order, tile_voxel, tile_column, tile_block, entry_count
):
    depth_z, depth_x, depth_y = volume.shape
    tiles_y = depth_y // group_rows
    tiles_u = measured.shape[2] // group_rows
    slab_tiles = depth_z * tiles_u
    plane_tiles = depth_x * tiles_y
    row_weight = jnp.sum(weight_blocks, axis=2, dtype=jnp.float32)
    col_weight = jnp.sum(weight_blocks, axis=1, dtype=jnp.float32)
    n_blocks = weight_blocks.shape[0]
    group = 4 if n_blocks % 4 == 0 else 1
    current = volume
    for turn_index in range(view_order.shape[0]):
        view_index = view_order[turn_index]
        voxel_list = lax.dynamic_index_in_dim(tile_voxel, view_index, 0, keepdims=False)[0]
        column_list = lax.dynamic_index_in_dim(tile_column, view_index, 0, keepdims=False)[0]
        block_list = lax.dynamic_index_in_dim(tile_block, view_index, 0, keepdims=False)[0]
        live_count = lax.dynamic_index_in_dim(entry_count, view_index, 0, keepdims=False)[0, 0]
        entries = voxel_list.shape[0]
        live = (jnp.arange(entries, dtype=jnp.int32) < live_count)[:, None]
        detector = voxel_list // plane_tiles * tiles_u + column_list
        voxel_tiles = current.astype(jnp.bfloat16).reshape(-1, group_rows)
        pick_voxel = one_hot(voxel_list, voxel_tiles.shape[0])
        pick_detector = one_hot(detector, slab_tiles)
        pick_block = jnp.where(live, one_hot(block_list, n_blocks), 0)
        blocks_column = block_list[:, None]

        cells = jnp.dot(pick_voxel, voxel_tiles, preferred_element_type=jnp.float32)
        product = block_apply(cells.astype(jnp.bfloat16), blocks_column, weight_blocks, group, True)
        product = jnp.where(live, product, 0.0)
        projection = lax.dot_general(
            pick_detector.astype(jnp.float32), product, (((0,), (0,)), ((), ())),
            precision=lax.Precision.HIGHEST)
        detector_blocks = lax.dot_general(
            pick_detector, pick_block, (((0,), (0,)), ((), ())), preferred_element_type=jnp.float32)
        ray_sum = jnp.dot(detector_blocks, row_weight, precision=lax.Precision.HIGHEST)
        target = lax.dynamic_index_in_dim(measured, view_index, 0, keepdims=False).reshape(
            slab_tiles, group_rows
        )
        n_gx = lax.axis_size("gx")
        joined = jnp.concatenate([projection, ray_sum], axis=1).astype(jnp.bfloat16)
        joined = vector_sum(joined.reshape(n_gx, slab_tiles // n_gx, 2 * group_rows))
        joined = joined.reshape(slab_tiles, 2 * group_rows).astype(jnp.float32)
        projection, ray_sum = joined[:, :group_rows], joined[:, group_rows:]
        residual = ((target - projection) / (ray_sum + 1.0)).astype(jnp.bfloat16)

        pixels = jnp.dot(pick_detector, residual, preferred_element_type=jnp.float32)
        product = block_apply(pixels.astype(jnp.bfloat16), blocks_column, weight_blocks, group, False)
        product = jnp.where(live, product, 0.0)
        change = lax.dot_general(
            pick_voxel.astype(jnp.float32), product, (((0,), (0,)), ((), ())),
            precision=lax.Precision.HIGHEST)
        voxel_blocks = lax.dot_general(
            pick_voxel, pick_block, (((0,), (0,)), ((), ())), preferred_element_type=jnp.float32)
        voxel_sum = jnp.dot(voxel_blocks, col_weight, precision=lax.Precision.HIGHEST)
        current = current + (change / (voxel_sum + 1.0)).reshape(current.shape)
    art_volume = jnp.maximum(current, 0.0)
    difference = art_volume - volume
    change_part = jnp.sum(difference * difference)
    stages = scalar_stages(lax.axis_size("gz"), lax.axis_size("gx"))
    padded = padded_from(art_volume, halo_exchange(art_volume))
    change_total = None
    smooth = art_volume
    for sweep_index in range(TV_STEPS):
        slope = tv_grad(pad_depth(padded))
        slope_part = jnp.sum(slope * slope)
        totals, halo = tv_exchange(
            pack_pair(slope_part, change_part if sweep_index == 0 else 0.0), slope, stages)
        if sweep_index == 0:
            change_total = totals[0, 1]
        slope_total = totals[0, 0]
        scale_now = step_gain * jnp.sqrt(change_total) / jnp.sqrt(slope_total + norm_floor)
        smooth = smooth - scale_now * slope
        if sweep_index + 1 < TV_STEPS:
            padded = padded - scale_now * padded_from(slope, halo)
    return smooth


def solution(mesh):
    return jax.shard_map(
        body,
        mesh=mesh,
        in_specs=(
            P("gz", "gx", None),
            P(None, "gz", None),
            P(),
            P(),
            P(None, "gz", "gx"),
            P(None, "gz", "gx"),
            P(None, "gz", "gx"),
            P(None, "gz", "gx"),
        ),
        out_specs=P("gz", "gx", None),
        check_vma=False,
    )
```

```python
import functools
import math

import jax
import jax.numpy as jnp
from jax import lax
from jax.experimental import pallas as pl
from jax.experimental.pallas import tpu as pltpu
from jax.sharding import PartitionSpec as P

TV_STEPS = 4


smooth_floor = 0.01
step_gain = 0.25
norm_floor = 1e-06
group_rows = 128


MESH = pl.DeviceIdType.MESH


def _peer(axis, position):
    if axis == "gz":
        return (position, lax.axis_index("gx"))
    return (lax.axis_index("gz"), position)


def vector_sum_kernel(n, x_ref, o_ref, recv, red, gath, ssem1, rsem1, ssem2, rsem2):
    me = lax.axis_index("gx")
    barrier = pltpu.get_barrier_semaphore()
    for d in range(1, n):
        pl.semaphore_signal(barrier, inc=1, device_id=_peer("gx", lax.rem(me + d, n)), device_id_type=MESH)
    pl.semaphore_wait(barrier, n - 1)

    def scatter_copy(d):
        dst = lax.rem(me + d, n)
        return pltpu.make_async_remote_copy(
            src_ref=x_ref.at[dst], dst_ref=recv.at[d], send_sem=ssem1.at[d], recv_sem=rsem1.at[d],
            device_id=_peer("gx", dst), device_id_type=MESH)

    def gather_copy(d):
        dst = lax.rem(me + d, n)
        return pltpu.make_async_remote_copy(
            src_ref=red, dst_ref=gath.at[me], send_sem=ssem2.at[d], recv_sem=rsem2.at[d],
            device_id=_peer("gx", dst), device_id_type=MESH)

    @pl.loop(1, n)
    def _(d):
        scatter_copy(d).start()

    @pl.loop(1, n)
    def _(d):
        scatter_copy(d).wait()

    total = lax.fori_loop(
        1, n, lambda d, acc: acc + recv[d].astype(jnp.float32), x_ref[me].astype(jnp.float32))
    red[...] = total.astype(red.dtype)

    @pl.loop(1, n)
    def _(d):
        gather_copy(d).start()

    @pl.loop(1, n)
    def _(d):
        gather_copy(d).wait()

    gath[me] = red[...]
    o_ref[...] = gath[...]


def vector_sum(x):
    n, rows, cols = x.shape
    return pl.pallas_call(
        functools.partial(vector_sum_kernel, n),
        out_shape=jax.ShapeDtypeStruct(x.shape, x.dtype),
        in_specs=[pl.BlockSpec(memory_space=pltpu.VMEM)],
        out_specs=pl.BlockSpec(memory_space=pltpu.VMEM),
        scratch_shapes=[
            pltpu.VMEM(x.shape, x.dtype),
            pltpu.VMEM((rows, cols), x.dtype),
            pltpu.VMEM(x.shape, x.dtype),
            pltpu.SemaphoreType.DMA((n,)),
            pltpu.SemaphoreType.DMA((n,)),
            pltpu.SemaphoreType.DMA((n,)),
            pltpu.SemaphoreType.DMA((n,)),
        ],
        compiler_params=pltpu.CompilerParams(collective_id=1, has_side_effects=True),
    )(x)


def _stage_peers(stage):
    if isinstance(stage[0], str):
        stage = [stage]
    index = {axis: lax.axis_index(axis) for axis, _, _ in stage}
    digits = [lax.rem(index[axis] // stride, size) for axis, stride, size in stage]
    total = 1
    position = 0
    for (_, _, size), digit in zip(stage, digits):
        position = position * size + digit
        total *= size
    peers = []
    for d in range(1, total):
        q = lax.rem(position + d, total)
        coords = dict(index)
        rest = total
        for (axis, stride, size), digit in zip(stage, digits):
            rest //= size
            coords[axis] = coords[axis] + (lax.rem(q // rest, size) - digit) * stride
        peers.append((coords.get("gz", lax.axis_index("gz")), coords.get("gx", lax.axis_index("gx"))))
    return position, total, peers


def fill_faces(c_ref, faces, depth, width):
    faces[pl.ds(0, depth)] = c_ref[width - 1]
    faces[pl.ds(depth, depth)] = c_ref[0]
    faces[pl.ds(2 * depth, width)] = c_ref[:, depth - 1, :]
    faces[pl.ds(2 * depth + width, width)] = c_ref[:, 0, :]
    faces[pl.ds(2 * depth + 2 * width, 1)] = c_ref[width - 1, pl.ds(0, 1), :]
    faces[pl.ds(2 * depth + 2 * width + 1, 1)] = c_ref[0, pl.ds(depth - 1, 1), :]


def write_halo(h_ref, hrecv, depth, width):
    count_z, count_x = lax.axis_size("gz"), lax.axis_size("gx")
    z, x = lax.axis_index("gz"), lax.axis_index("gx")
    corner = 2 * depth + 2 * width
    parts = [
        (0, depth, z > 0),
        (depth, depth, z < count_z - 1),
        (2 * depth, width, x > 0),
        (2 * depth + width, width, x < count_x - 1),
        (corner, 1, (z > 0) & (x < count_x - 1)),
        (corner + 1, 1, (z < count_z - 1) & (x > 0)),
    ]
    for row, rows, keep in parts:
        values = hrecv[pl.ds(row, rows)]
        h_ref[pl.ds(row, rows)] = jnp.where(keep, values, jnp.zeros_like(values))


def halo_routes(depth, width):
    count_z, count_x = lax.axis_size("gz"), lax.axis_size("gx")
    z, x = lax.axis_index("gz"), lax.axis_index("gx")
    up_z, down_z = lax.rem(z + 1, count_z), lax.rem(z + count_z - 1, count_z)
    up_x, down_x = lax.rem(x + 1, count_x), lax.rem(x + count_x - 1, count_x)
    return [
        (0, depth, (up_z, x)),
        (depth, depth, (down_z, x)),
        (2 * depth, width, (z, up_x)),
        (2 * depth + width, width, (z, down_x)),
        (2 * depth + 2 * width, 1, (up_z, down_x)),
        (2 * depth + 2 * width + 1, 1, (down_z, up_x)),
    ]


def tv_exchange_kernel(stages, shape, x_ref, c_ref, o_ref, h_ref, buf, recv, ssem, rsem, hrecv, hsend, hget, f_ref):
    routes = halo_routes(*shape)
    fill_faces(c_ref, f_ref, *shape)
    plan = [_stage_peers(stage) for stage in stages]
    barrier = pltpu.get_barrier_semaphore()
    count = 0
    for _, _, peers in plan:
        for peer in peers:
            pl.semaphore_signal(barrier, inc=1, device_id=peer, device_id_type=MESH)
            count += 1
    for _, _, target in routes:
        pl.semaphore_signal(barrier, inc=1, device_id=target, device_id_type=MESH)
        count += 1
    pl.semaphore_wait(barrier, count)
    halo = []
    for k, (row, rows, target) in enumerate(routes):
        copy = pltpu.make_async_remote_copy(
            src_ref=f_ref.at[pl.ds(row, rows)], dst_ref=hrecv.at[pl.ds(row, rows)],
            send_sem=hsend.at[k], recv_sem=hget.at[k], device_id=target, device_id_type=MESH)
        copy.start()
        halo.append(copy)
    total = x_ref[...]
    slot = 0
    for s, (position, size, peers) in enumerate(plan):
        source = x_ref if s == 0 else buf.at[s - 1]
        recv[slot] = total
        sends = []
        for d, peer in enumerate(peers, start=1):
            copy = pltpu.make_async_remote_copy(
                src_ref=source, dst_ref=recv.at[slot + d], send_sem=ssem.at[slot + d],
                recv_sem=rsem.at[slot + d], device_id=peer, device_id_type=MESH)
            copy.start()
            sends.append(copy)
        for copy in sends:
            copy.wait()
        total = recv[slot + position]
        for p in range(1, size):
            total = total + recv[slot + lax.rem(position - p + size, size)]
        slot += size
        if s + 1 < len(plan):
            buf[s] = total
    o_ref[...] = total
    for copy in halo:
        copy.wait()
    write_halo(h_ref, hrecv, *shape)


def tv_exchange(x, cells, stages):
    width, depth, lanes = cells.shape
    rows = 2 * depth + 2 * width + 2
    slots = sum(math.prod(size for _, _, size in stage) for stage in stages)
    return pl.pallas_call(
        functools.partial(tv_exchange_kernel, stages, (depth, width)),
        out_shape=(jax.ShapeDtypeStruct(x.shape, x.dtype), jax.ShapeDtypeStruct((rows, lanes), cells.dtype)),
        in_specs=[pl.BlockSpec(memory_space=pltpu.VMEM)] * 2,
        out_specs=(pl.BlockSpec(memory_space=pltpu.VMEM), pl.BlockSpec(memory_space=pltpu.VMEM)),
        scratch_shapes=[
            pltpu.VMEM((max(len(stages) - 1, 1),) + x.shape, x.dtype),
            pltpu.VMEM((slots,) + x.shape, x.dtype),
            pltpu.SemaphoreType.DMA((slots,)),
            pltpu.SemaphoreType.DMA((slots,)),
            pltpu.VMEM((rows, lanes), cells.dtype),
            pltpu.SemaphoreType.DMA((6,)),
            pltpu.SemaphoreType.DMA((6,)),
            pltpu.VMEM((rows, lanes), cells.dtype),
        ],
        compiler_params=pltpu.CompilerParams(collective_id=3, has_side_effects=True),
    )(x, cells)


def halo_exchange_kernel(shape, c_ref, h_ref, hrecv, hsend, hget, f_ref):
    routes = halo_routes(*shape)
    fill_faces(c_ref, f_ref, *shape)
    barrier = pltpu.get_barrier_semaphore()
    for _, _, target in routes:
        pl.semaphore_signal(barrier, inc=1, device_id=target, device_id_type=MESH)
    pl.semaphore_wait(barrier, len(routes))
    halo = []
    for k, (row, rows, target) in enumerate(routes):
        copy = pltpu.make_async_remote_copy(
            src_ref=f_ref.at[pl.ds(row, rows)], dst_ref=hrecv.at[pl.ds(row, rows)],
            send_sem=hsend.at[k], recv_sem=hget.at[k], device_id=target, device_id_type=MESH)
        copy.start()
        halo.append(copy)
    for copy in halo:
        copy.wait()
    write_halo(h_ref, hrecv, *shape)


def halo_exchange(cells):
    width, depth, lanes = cells.shape
    rows = 2 * depth + 2 * width + 2
    return pl.pallas_call(
        functools.partial(halo_exchange_kernel, (depth, width)),
        out_shape=jax.ShapeDtypeStruct((rows, lanes), cells.dtype),
        in_specs=[pl.BlockSpec(memory_space=pltpu.VMEM)],
        out_specs=pl.BlockSpec(memory_space=pltpu.VMEM),
        scratch_shapes=[
            pltpu.VMEM((rows, lanes), cells.dtype),
            pltpu.SemaphoreType.DMA((6,)),
            pltpu.SemaphoreType.DMA((6,)),
            pltpu.VMEM((rows, lanes), cells.dtype),
        ],
        compiler_params=pltpu.CompilerParams(collective_id=4, has_side_effects=True),
    )(cells)


def faces_of(cells):
    return jnp.concatenate(
        [cells[-1], cells[0], cells[:, -1], cells[:, 0], cells[-1, :1], cells[0, -1:]], axis=0)


def padded_from(cells, halo):
    depth, width = cells.shape[1], cells.shape[0]
    low_z = halo[:depth][None]
    high_z = halo[depth:2 * depth][None]
    low_x = halo[2 * depth:2 * depth + width][:, None]
    high_x = halo[2 * depth + width:2 * depth + 2 * width][:, None]
    corner = 2 * depth + 2 * width
    low_z_high_x = halo[corner:corner + 1][None]
    high_z_low_x = halo[corner + 1:corner + 2][None]
    zero_line = jnp.zeros_like(cells[:1, :1])
    top = jnp.concatenate([zero_line, low_z, low_z_high_x], axis=1)
    middle = jnp.concatenate([low_x, cells, high_x], axis=1)
    bottom = jnp.concatenate([high_z_low_x, high_z, zero_line], axis=1)
    return jnp.concatenate([top, middle, bottom], axis=0)


def scalar_stages(n_gz, n_gx):
    if n_gx % 4 == 0 and n_gx > 4:
        return [[("gz", 1, n_gz), ("gx", 1, 4)], [("gx", 4, n_gx // 4)]]
    return [[("gz", 1, n_gz)], [("gx", 1, n_gx)]]


def pack_pair(a, b):
    lane = lax.broadcasted_iota(jnp.int32, (8, 128), 1)
    return jnp.where(lane == 0, a, jnp.where(lane == 1, b, 0.0)).astype(jnp.float32)


def one_hot(index, size):
    return (index[:, None] == jnp.arange(size, dtype=jnp.int32)[None, :]).astype(jnp.bfloat16)


def block_apply_kernel(group, transposed, x_ref, blk_ref, w_ref, o_ref):
    o_ref[...] = jnp.zeros_like(o_ref)
    x = x_ref[...]
    chosen = blk_ref[...]
    zero = jnp.zeros_like(x)
    dims = (((1,), (1,)), ((), ())) if transposed else (((1,), (0,)), ((), ()))

    def step(p, carry):
        parts = [jnp.where(chosen == p * group + i, x, zero) for i in range(group)]
        joined = jnp.concatenate(parts, axis=1)
        weights = jnp.concatenate(
            [w_ref[p * group + i] for i in range(group)], axis=1 if transposed else 0)
        o_ref[...] += lax.dot_general(joined, weights, dims, preferred_element_type=jnp.float32)
        return carry

    lax.fori_loop(0, w_ref.shape[0] // group, step, 0)


def block_apply(x, chosen, weights, group, transposed):
    entries, width = x.shape
    flops = 2 * entries * width * width * weights.shape[0]
    return pl.pallas_call(
        functools.partial(block_apply_kernel, group, transposed),
        out_shape=jax.ShapeDtypeStruct((entries, width), jnp.float32),
        in_specs=[pl.BlockSpec(memory_space=pltpu.VMEM)] * 3,
        out_specs=pl.BlockSpec(memory_space=pltpu.VMEM),
        cost_estimate=pl.CostEstimate(
            flops=flops, transcendentals=0, bytes_accessed=weights.size * 2 + entries * width * 10),
    )(x, chosen, weights)


def shift_from(block, pairs_of):
    count_z, count_x = lax.axis_size("gz"), lax.axis_size("gx")
    pairs = []
    for z in range(count_z):
        for x in range(count_x):
            target = pairs_of(z, x)
            if 0 <= target[0] < count_z and 0 <= target[1] < count_x:
                pairs.append((z * count_x + x, target[0] * count_x + target[1]))
    return lax.ppermute(block, ("gz", "gx"), pairs)


def padded_2(cells):
    zero_line = jnp.zeros_like(cells[:1, :1])
    low_z = shift_from(cells[-1:], lambda z, x: (z + 1, x))
    high_z = shift_from(cells[:1], lambda z, x: (z - 1, x))
    low_x = shift_from(cells[:, -1:], lambda z, x: (z, x + 1))
    high_x = shift_from(cells[:, :1], lambda z, x: (z, x - 1))
    low_z_high_x = shift_from(cells[-1:, :1], lambda z, x: (z + 1, x - 1))
    high_z_low_x = shift_from(cells[:1, -1:], lambda z, x: (z - 1, x + 1))
    top = jnp.concatenate([zero_line, low_z, low_z_high_x], axis=1)
    middle = jnp.concatenate([low_x, cells, high_x], axis=1)
    bottom = jnp.concatenate([high_z_low_x, high_z, zero_line], axis=1)
    return jnp.concatenate([top, middle, bottom], axis=0)


def tv_grad(padded):
    base_cells = padded[:-1, :-1, :-1]
    diff_z = padded[1:, :-1, :-1] - base_cells
    diff_x = padded[:-1, 1:, :-1] - base_cells
    diff_y = padded[:-1, :-1, 1:] - base_cells
    inverse = lax.rsqrt(diff_z * diff_z + diff_x * diff_x + diff_y * diff_y + smooth_floor)
    flow_z = diff_z * inverse
    flow_x = diff_x * inverse
    flow_y = diff_y * inverse
    flow_all = flow_z + flow_x + flow_y
    return flow_z[:-1, 1:, 1:] + flow_x[1:, :-1, 1:] + flow_y[1:, 1:, :-1] - flow_all[1:, 1:, 1:]


def pad_depth(field):
    return jnp.pad(field, ((0, 0), (0, 0), (1, 1)))


def body(
    volume, measured, weight_blocks, view_order, tile_voxel, tile_column, tile_block, entry_count
):
    depth_z, depth_x, depth_y = volume.shape
    tiles_y = depth_y // group_rows
    tiles_u = measured.shape[2] // group_rows
    slab_tiles = depth_z * tiles_u
    plane_tiles = depth_x * tiles_y
    row_weight = jnp.sum(weight_blocks, axis=2, dtype=jnp.float32)
    col_weight = jnp.sum(weight_blocks, axis=1, dtype=jnp.float32)
    n_blocks = weight_blocks.shape[0]
    group = 8 if n_blocks % 8 == 0 else 1
    current = volume
    for turn_index in range(view_order.shape[0]):
        view_index = view_order[turn_index]
        voxel_list = lax.dynamic_index_in_dim(tile_voxel, view_index, 0, keepdims=False)[0]
        column_list = lax.dynamic_index_in_dim(tile_column, view_index, 0, keepdims=False)[0]
        block_list = lax.dynamic_index_in_dim(tile_block, view_index, 0, keepdims=False)[0]
        live_count = lax.dynamic_index_in_dim(entry_count, view_index, 0, keepdims=False)[0, 0]
        entries = voxel_list.shape[0]
        live = (jnp.arange(entries, dtype=jnp.int32) < live_count)[:, None]
        detector = voxel_list // plane_tiles * tiles_u + column_list
        voxel_tiles = current.astype(jnp.bfloat16).reshape(-1, group_rows)
        pick_voxel = one_hot(voxel_list, voxel_tiles.shape[0])
        pick_detector = one_hot(detector, slab_tiles)
        pick_block = jnp.where(live, one_hot(block_list, n_blocks), 0)
        blocks_column = block_list[:, None]

        cells = jnp.dot(pick_voxel, voxel_tiles, preferred_element_type=jnp.float32)
        product = block_apply(cells.astype(jnp.bfloat16), blocks_column, weight_blocks, group, True)
        product = jnp.where(live, product, 0.0)
        projection = lax.dot_general(
            pick_detector.astype(jnp.float32), product, (((0,), (0,)), ((), ())),
            precision=lax.Precision.HIGHEST)
        detector_blocks = lax.dot_general(
            pick_detector, pick_block, (((0,), (0,)), ((), ())), preferred_element_type=jnp.float32)
        ray_sum = jnp.dot(detector_blocks, row_weight, precision=lax.Precision.HIGHEST)
        target = lax.dynamic_index_in_dim(measured, view_index, 0, keepdims=False).reshape(
            slab_tiles, group_rows
        )
        n_gx = lax.axis_size("gx")
        joined = jnp.concatenate([projection, ray_sum], axis=1).astype(jnp.bfloat16)
        joined = vector_sum(joined.reshape(n_gx, slab_tiles // n_gx, 2 * group_rows))
        joined = joined.reshape(slab_tiles, 2 * group_rows).astype(jnp.float32)
        projection, ray_sum = joined[:, :group_rows], joined[:, group_rows:]
        residual = ((target - projection) / (ray_sum + 1.0)).astype(jnp.bfloat16)

        pixels = jnp.dot(pick_detector, residual, preferred_element_type=jnp.float32)
        product = block_apply(pixels.astype(jnp.bfloat16), blocks_column, weight_blocks, group, False)
        product = jnp.where(live, product, 0.0)
        change = lax.dot_general(
            pick_voxel.astype(jnp.float32), product, (((0,), (0,)), ((), ())),
            precision=lax.Precision.HIGHEST)
        voxel_blocks = lax.dot_general(
            pick_voxel, pick_block, (((0,), (0,)), ((), ())), preferred_element_type=jnp.float32)
        voxel_sum = jnp.dot(voxel_blocks, col_weight, precision=lax.Precision.HIGHEST)
        current = current + (change / (voxel_sum + 1.0)).reshape(current.shape)
    art_volume = jnp.maximum(current, 0.0)
    difference = art_volume - volume
    change_part = jnp.sum(difference * difference)
    stages = scalar_stages(lax.axis_size("gz"), lax.axis_size("gx"))
    padded = padded_from(art_volume, halo_exchange(art_volume))
    change_total = None
    smooth = art_volume
    for sweep_index in range(TV_STEPS):
        slope = tv_grad(pad_depth(padded))
        slope_part = jnp.sum(slope * slope)
        totals, halo = tv_exchange(
            pack_pair(slope_part, change_part if sweep_index == 0 else 0.0), slope, stages)
        if sweep_index == 0:
            change_total = totals[0, 1]
        slope_total = totals[0, 0]
        scale_now = step_gain * jnp.sqrt(change_total) / jnp.sqrt(slope_total + norm_floor)
        smooth = smooth - scale_now * slope
        if sweep_index + 1 < TV_STEPS:
            padded = padded - scale_now * padded_from(slope, halo)
    return smooth


def solution(mesh):
    return jax.shard_map(
        body,
        mesh=mesh,
        in_specs=(
            P("gz", "gx", None),
            P(None, "gz", None),
            P(),
            P(),
            P(None, "gz", "gx"),
            P(None, "gz", "gx"),
            P(None, "gz", "gx"),
            P(None, "gz", "gx"),
        ),
        out_specs=P("gz", "gx", None),
        check_vma=False,
    )
```

```python
import functools
import math

import jax
import jax.numpy as jnp
from jax import lax
from jax.experimental import pallas as pl
from jax.experimental.pallas import tpu as pltpu
from jax.sharding import PartitionSpec as P

TV_STEPS = 4


smooth_floor = 0.01
step_gain = 0.25
norm_floor = 1e-06
group_rows = 128


MESH = pl.DeviceIdType.MESH


def _peer(axis, position):
    if axis == "gz":
        return (position, lax.axis_index("gx"))
    return (lax.axis_index("gz"), position)


def vector_sum_kernel(n, x_ref, o_ref, recv, red, gath, ssem1, rsem1, ssem2, rsem2):
    me = lax.axis_index("gx")
    barrier = pltpu.get_barrier_semaphore()
    for d in range(1, n):
        pl.semaphore_signal(barrier, inc=1, device_id=_peer("gx", lax.rem(me + d, n)), device_id_type=MESH)
    pl.semaphore_wait(barrier, n - 1)

    def scatter_copy(d):
        dst = lax.rem(me + d, n)
        return pltpu.make_async_remote_copy(
            src_ref=x_ref.at[dst], dst_ref=recv.at[d], send_sem=ssem1.at[d], recv_sem=rsem1.at[d],
            device_id=_peer("gx", dst), device_id_type=MESH)

    def gather_copy(d):
        dst = lax.rem(me + d, n)
        return pltpu.make_async_remote_copy(
            src_ref=red, dst_ref=gath.at[me], send_sem=ssem2.at[d], recv_sem=rsem2.at[d],
            device_id=_peer("gx", dst), device_id_type=MESH)

    @pl.loop(1, n)
    def _(d):
        scatter_copy(d).start()

    @pl.loop(1, n)
    def _(d):
        scatter_copy(d).wait()

    total = lax.fori_loop(
        1, n, lambda d, acc: acc + recv[d].astype(jnp.float32), x_ref[me].astype(jnp.float32))
    red[...] = total.astype(red.dtype)

    @pl.loop(1, n)
    def _(d):
        gather_copy(d).start()

    @pl.loop(1, n)
    def _(d):
        gather_copy(d).wait()

    gath[me] = red[...]
    o_ref[...] = gath[...]


def vector_sum(x):
    n, rows, cols = x.shape
    return pl.pallas_call(
        functools.partial(vector_sum_kernel, n),
        out_shape=jax.ShapeDtypeStruct(x.shape, x.dtype),
        in_specs=[pl.BlockSpec(memory_space=pltpu.VMEM)],
        out_specs=pl.BlockSpec(memory_space=pltpu.VMEM),
        scratch_shapes=[
            pltpu.VMEM(x.shape, x.dtype),
            pltpu.VMEM((rows, cols), x.dtype),
            pltpu.VMEM(x.shape, x.dtype),
            pltpu.SemaphoreType.DMA((n,)),
            pltpu.SemaphoreType.DMA((n,)),
            pltpu.SemaphoreType.DMA((n,)),
            pltpu.SemaphoreType.DMA((n,)),
        ],
        compiler_params=pltpu.CompilerParams(collective_id=1, has_side_effects=True),
    )(x)


def _stage_peers(stage):
    if isinstance(stage[0], str):
        stage = [stage]
    index = {axis: lax.axis_index(axis) for axis, _, _ in stage}
    digits = [lax.rem(index[axis] // stride, size) for axis, stride, size in stage]
    total = 1
    position = 0
    for (_, _, size), digit in zip(stage, digits):
        position = position * size + digit
        total *= size
    peers = []
    for d in range(1, total):
        q = lax.rem(position + d, total)
        coords = dict(index)
        rest = total
        for (axis, stride, size), digit in zip(stage, digits):
            rest //= size
            coords[axis] = coords[axis] + (lax.rem(q // rest, size) - digit) * stride
        peers.append((coords.get("gz", lax.axis_index("gz")), coords.get("gx", lax.axis_index("gx"))))
    return position, total, peers


def fill_faces(c_ref, faces, depth, width):
    faces[pl.ds(0, depth)] = c_ref[width - 1]
    faces[pl.ds(depth, depth)] = c_ref[0]
    faces[pl.ds(2 * depth, width)] = c_ref[:, depth - 1, :]
    faces[pl.ds(2 * depth + width, width)] = c_ref[:, 0, :]
    faces[pl.ds(2 * depth + 2 * width, 1)] = c_ref[width - 1, pl.ds(0, 1), :]
    faces[pl.ds(2 * depth + 2 * width + 1, 1)] = c_ref[0, pl.ds(depth - 1, 1), :]


def write_halo(h_ref, hrecv, depth, width):
    count_z, count_x = lax.axis_size("gz"), lax.axis_size("gx")
    z, x = lax.axis_index("gz"), lax.axis_index("gx")
    corner = 2 * depth + 2 * width
    parts = [
        (0, depth, z > 0),
        (depth, depth, z < count_z - 1),
        (2 * depth, width, x > 0),
        (2 * depth + width, width, x < count_x - 1),
        (corner, 1, (z > 0) & (x < count_x - 1)),
        (corner + 1, 1, (z < count_z - 1) & (x > 0)),
    ]
    for row, rows, keep in parts:
        values = hrecv[pl.ds(row, rows)]
        h_ref[pl.ds(row, rows)] = jnp.where(keep, values, jnp.zeros_like(values))


def halo_routes(depth, width):
    count_z, count_x = lax.axis_size("gz"), lax.axis_size("gx")
    z, x = lax.axis_index("gz"), lax.axis_index("gx")
    up_z, down_z = lax.rem(z + 1, count_z), lax.rem(z + count_z - 1, count_z)
    up_x, down_x = lax.rem(x + 1, count_x), lax.rem(x + count_x - 1, count_x)
    return [
        (0, depth, (up_z, x)),
        (depth, depth, (down_z, x)),
        (2 * depth, width, (z, up_x)),
        (2 * depth + width, width, (z, down_x)),
        (2 * depth + 2 * width, 1, (up_z, down_x)),
        (2 * depth + 2 * width + 1, 1, (down_z, up_x)),
    ]


def tv_exchange_kernel(stages, shape, x_ref, c_ref, o_ref, h_ref, buf, recv, ssem, rsem, hrecv, hsend, hget, f_ref):
    routes = halo_routes(*shape)
    fill_faces(c_ref, f_ref, *shape)
    plan = [_stage_peers(stage) for stage in stages]
    barrier = pltpu.get_barrier_semaphore()
    count = 0
    for _, _, peers in plan:
        for peer in peers:
            pl.semaphore_signal(barrier, inc=1, device_id=peer, device_id_type=MESH)
            count += 1
    for _, _, target in routes:
        pl.semaphore_signal(barrier, inc=1, device_id=target, device_id_type=MESH)
        count += 1
    pl.semaphore_wait(barrier, count)
    halo = []
    for k, (row, rows, target) in enumerate(routes):
        copy = pltpu.make_async_remote_copy(
            src_ref=f_ref.at[pl.ds(row, rows)], dst_ref=hrecv.at[pl.ds(row, rows)],
            send_sem=hsend.at[k], recv_sem=hget.at[k], device_id=target, device_id_type=MESH)
        copy.start()
        halo.append(copy)
    total = x_ref[...]
    slot = 0
    for s, (position, size, peers) in enumerate(plan):
        source = x_ref if s == 0 else buf.at[s - 1]
        recv[slot] = total
        sends = []
        for d, peer in enumerate(peers, start=1):
            copy = pltpu.make_async_remote_copy(
                src_ref=source, dst_ref=recv.at[slot + d], send_sem=ssem.at[slot + d],
                recv_sem=rsem.at[slot + d], device_id=peer, device_id_type=MESH)
            copy.start()
            sends.append(copy)
        for copy in sends:
            copy.wait()
        total = recv[slot + position]
        for p in range(1, size):
            total = total + recv[slot + lax.rem(position - p + size, size)]
        slot += size
        if s + 1 < len(plan):
            buf[s] = total
    o_ref[...] = total
    for copy in halo:
        copy.wait()
    write_halo(h_ref, hrecv, *shape)


def tv_exchange(x, cells, stages):
    width, depth, lanes = cells.shape
    rows = 2 * depth + 2 * width + 2
    slots = sum(math.prod(size for _, _, size in stage) for stage in stages)
    return pl.pallas_call(
        functools.partial(tv_exchange_kernel, stages, (depth, width)),
        out_shape=(jax.ShapeDtypeStruct(x.shape, x.dtype), jax.ShapeDtypeStruct((rows, lanes), cells.dtype)),
        in_specs=[pl.BlockSpec(memory_space=pltpu.VMEM)] * 2,
        out_specs=(pl.BlockSpec(memory_space=pltpu.VMEM), pl.BlockSpec(memory_space=pltpu.VMEM)),
        scratch_shapes=[
            pltpu.VMEM((max(len(stages) - 1, 1),) + x.shape, x.dtype),
            pltpu.VMEM((slots,) + x.shape, x.dtype),
            pltpu.SemaphoreType.DMA((slots,)),
            pltpu.SemaphoreType.DMA((slots,)),
            pltpu.VMEM((rows, lanes), cells.dtype),
            pltpu.SemaphoreType.DMA((6,)),
            pltpu.SemaphoreType.DMA((6,)),
            pltpu.VMEM((rows, lanes), cells.dtype),
        ],
        compiler_params=pltpu.CompilerParams(collective_id=3, has_side_effects=True),
    )(x, cells)


def halo_exchange_kernel(shape, c_ref, h_ref, hrecv, hsend, hget, f_ref):
    routes = halo_routes(*shape)
    fill_faces(c_ref, f_ref, *shape)
    barrier = pltpu.get_barrier_semaphore()
    for _, _, target in routes:
        pl.semaphore_signal(barrier, inc=1, device_id=target, device_id_type=MESH)
    pl.semaphore_wait(barrier, len(routes))
    halo = []
    for k, (row, rows, target) in enumerate(routes):
        copy = pltpu.make_async_remote_copy(
            src_ref=f_ref.at[pl.ds(row, rows)], dst_ref=hrecv.at[pl.ds(row, rows)],
            send_sem=hsend.at[k], recv_sem=hget.at[k], device_id=target, device_id_type=MESH)
        copy.start()
        halo.append(copy)
    for copy in halo:
        copy.wait()
    write_halo(h_ref, hrecv, *shape)


def halo_exchange(cells):
    width, depth, lanes = cells.shape
    rows = 2 * depth + 2 * width + 2
    return pl.pallas_call(
        functools.partial(halo_exchange_kernel, (depth, width)),
        out_shape=jax.ShapeDtypeStruct((rows, lanes), cells.dtype),
        in_specs=[pl.BlockSpec(memory_space=pltpu.VMEM)],
        out_specs=pl.BlockSpec(memory_space=pltpu.VMEM),
        scratch_shapes=[
            pltpu.VMEM((rows, lanes), cells.dtype),
            pltpu.SemaphoreType.DMA((6,)),
            pltpu.SemaphoreType.DMA((6,)),
            pltpu.VMEM((rows, lanes), cells.dtype),
        ],
        compiler_params=pltpu.CompilerParams(collective_id=4, has_side_effects=True),
    )(cells)


def faces_of(cells):
    return jnp.concatenate(
        [cells[-1], cells[0], cells[:, -1], cells[:, 0], cells[-1, :1], cells[0, -1:]], axis=0)


def padded_from(cells, halo):
    depth, width = cells.shape[1], cells.shape[0]
    low_z = halo[:depth][None]
    high_z = halo[depth:2 * depth][None]
    low_x = halo[2 * depth:2 * depth + width][:, None]
    high_x = halo[2 * depth + width:2 * depth + 2 * width][:, None]
    corner = 2 * depth + 2 * width
    low_z_high_x = halo[corner:corner + 1][None]
    high_z_low_x = halo[corner + 1:corner + 2][None]
    zero_line = jnp.zeros_like(cells[:1, :1])
    top = jnp.concatenate([zero_line, low_z, low_z_high_x], axis=1)
    middle = jnp.concatenate([low_x, cells, high_x], axis=1)
    bottom = jnp.concatenate([high_z_low_x, high_z, zero_line], axis=1)
    return jnp.concatenate([top, middle, bottom], axis=0)


def scalar_stages(n_gz, n_gx):
    if n_gx % 4 == 0 and n_gx > 4:
        return [[("gz", 1, n_gz), ("gx", 1, 4)], [("gx", 4, n_gx // 4)]]
    return [[("gz", 1, n_gz)], [("gx", 1, n_gx)]]


def pack_pair(a, b):
    lane = lax.broadcasted_iota(jnp.int32, (8, 128), 1)
    return jnp.where(lane == 0, a, jnp.where(lane == 1, b, 0.0)).astype(jnp.float32)


def one_hot(index, size):
    return (index[:, None] == jnp.arange(size, dtype=jnp.int32)[None, :]).astype(jnp.bfloat16)


def block_apply_kernel(group, transposed, x_ref, blk_ref, w_ref, o_ref):
    o_ref[...] = jnp.zeros_like(o_ref)
    x = x_ref[...]
    chosen = blk_ref[...]
    zero = jnp.zeros_like(x)
    dims = (((1,), (1,)), ((), ())) if transposed else (((1,), (0,)), ((), ()))

    def step(p, carry):
        parts = [jnp.where(chosen == p * group + i, x, zero) for i in range(group)]
        joined = jnp.concatenate(parts, axis=1)
        weights = jnp.concatenate(
            [w_ref[p * group + i] for i in range(group)], axis=1 if transposed else 0)
        o_ref[...] += lax.dot_general(joined, weights, dims, preferred_element_type=jnp.float32)
        return carry

    lax.fori_loop(0, w_ref.shape[0] // group, step, 0)


def block_apply(x, chosen, weights, group, transposed):
    entries, width = x.shape
    flops = 2 * entries * width * width * weights.shape[0]
    return pl.pallas_call(
        functools.partial(block_apply_kernel, group, transposed),
        out_shape=jax.ShapeDtypeStruct((entries, width), jnp.float32),
        in_specs=[pl.BlockSpec(memory_space=pltpu.VMEM)] * 3,
        out_specs=pl.BlockSpec(memory_space=pltpu.VMEM),
        cost_estimate=pl.CostEstimate(
            flops=flops, transcendentals=0, bytes_accessed=weights.size * 2 + entries * width * 10),
    )(x, chosen, weights)


def shift_from(block, pairs_of):
    count_z, count_x = lax.axis_size("gz"), lax.axis_size("gx")
    pairs = []
    for z in range(count_z):
        for x in range(count_x):
            target = pairs_of(z, x)
            if 0 <= target[0] < count_z and 0 <= target[1] < count_x:
                pairs.append((z * count_x + x, target[0] * count_x + target[1]))
    return lax.ppermute(block, ("gz", "gx"), pairs)


def padded_2(cells):
    zero_line = jnp.zeros_like(cells[:1, :1])
    low_z = shift_from(cells[-1:], lambda z, x: (z + 1, x))
    high_z = shift_from(cells[:1], lambda z, x: (z - 1, x))
    low_x = shift_from(cells[:, -1:], lambda z, x: (z, x + 1))
    high_x = shift_from(cells[:, :1], lambda z, x: (z, x - 1))
    low_z_high_x = shift_from(cells[-1:, :1], lambda z, x: (z + 1, x - 1))
    high_z_low_x = shift_from(cells[:1, -1:], lambda z, x: (z - 1, x + 1))
    top = jnp.concatenate([zero_line, low_z, low_z_high_x], axis=1)
    middle = jnp.concatenate([low_x, cells, high_x], axis=1)
    bottom = jnp.concatenate([high_z_low_x, high_z, zero_line], axis=1)
    return jnp.concatenate([top, middle, bottom], axis=0)


def tv_grad(padded):
    base_cells = padded[:-1, :-1, :-1]
    diff_z = padded[1:, :-1, :-1] - base_cells
    diff_x = padded[:-1, 1:, :-1] - base_cells
    diff_y = padded[:-1, :-1, 1:] - base_cells
    inverse = lax.rsqrt(diff_z * diff_z + diff_x * diff_x + diff_y * diff_y + smooth_floor)
    flow_z = diff_z * inverse
    flow_x = diff_x * inverse
    flow_y = diff_y * inverse
    flow_all = flow_z + flow_x + flow_y
    return flow_z[:-1, 1:, 1:] + flow_x[1:, :-1, 1:] + flow_y[1:, 1:, :-1] - flow_all[1:, 1:, 1:]


def pad_depth(field):
    return jnp.pad(field, ((0, 0), (0, 0), (1, 1)))


def body(
    volume, measured, weight_blocks, view_order, tile_voxel, tile_column, tile_block, entry_count
):
    depth_z, depth_x, depth_y = volume.shape
    tiles_y = depth_y // group_rows
    tiles_u = measured.shape[2] // group_rows
    slab_tiles = depth_z * tiles_u
    plane_tiles = depth_x * tiles_y
    row_weight = jnp.sum(weight_blocks, axis=2, dtype=jnp.float32)
    col_weight = jnp.sum(weight_blocks, axis=1, dtype=jnp.float32)
    n_blocks = weight_blocks.shape[0]
    group = 16 if n_blocks % 16 == 0 else 1
    current = volume
    for turn_index in range(view_order.shape[0]):
        view_index = view_order[turn_index]
        voxel_list = lax.dynamic_index_in_dim(tile_voxel, view_index, 0, keepdims=False)[0]
        column_list = lax.dynamic_index_in_dim(tile_column, view_index, 0, keepdims=False)[0]
        block_list = lax.dynamic_index_in_dim(tile_block, view_index, 0, keepdims=False)[0]
        live_count = lax.dynamic_index_in_dim(entry_count, view_index, 0, keepdims=False)[0, 0]
        entries = voxel_list.shape[0]
        live = (jnp.arange(entries, dtype=jnp.int32) < live_count)[:, None]
        detector = voxel_list // plane_tiles * tiles_u + column_list
        voxel_tiles = current.astype(jnp.bfloat16).reshape(-1, group_rows)
        pick_voxel = one_hot(voxel_list, voxel_tiles.shape[0])
        pick_detector = one_hot(detector, slab_tiles)
        pick_block = jnp.where(live, one_hot(block_list, n_blocks), 0)
        blocks_column = block_list[:, None]

        cells = jnp.dot(pick_voxel, voxel_tiles, preferred_element_type=jnp.float32)
        product = block_apply(cells.astype(jnp.bfloat16), blocks_column, weight_blocks, group, True)
        product = jnp.where(live, product, 0.0)
        projection = lax.dot_general(
            pick_detector.astype(jnp.float32), product, (((0,), (0,)), ((), ())),
            precision=lax.Precision.HIGHEST)
        detector_blocks = lax.dot_general(
            pick_detector, pick_block, (((0,), (0,)), ((), ())), preferred_element_type=jnp.float32)
        ray_sum = jnp.dot(detector_blocks, row_weight, precision=lax.Precision.HIGHEST)
        target = lax.dynamic_index_in_dim(measured, view_index, 0, keepdims=False).reshape(
            slab_tiles, group_rows
        )
        n_gx = lax.axis_size("gx")
        joined = jnp.concatenate([projection, ray_sum], axis=1).astype(jnp.bfloat16)
        joined = vector_sum(joined.reshape(n_gx, slab_tiles // n_gx, 2 * group_rows))
        joined = joined.reshape(slab_tiles, 2 * group_rows).astype(jnp.float32)
        projection, ray_sum = joined[:, :group_rows], joined[:, group_rows:]
        residual = ((target - projection) / (ray_sum + 1.0)).astype(jnp.bfloat16)

        pixels = jnp.dot(pick_detector, residual, preferred_element_type=jnp.float32)
        product = block_apply(pixels.astype(jnp.bfloat16), blocks_column, weight_blocks, group, False)
        product = jnp.where(live, product, 0.0)
        change = lax.dot_general(
            pick_voxel.astype(jnp.float32), product, (((0,), (0,)), ((), ())),
            precision=lax.Precision.HIGHEST)
        voxel_blocks = lax.dot_general(
            pick_voxel, pick_block, (((0,), (0,)), ((), ())), preferred_element_type=jnp.float32)
        voxel_sum = jnp.dot(voxel_blocks, col_weight, precision=lax.Precision.HIGHEST)
        current = current + (change / (voxel_sum + 1.0)).reshape(current.shape)
    art_volume = jnp.maximum(current, 0.0)
    difference = art_volume - volume
    change_part = jnp.sum(difference * difference)
    stages = scalar_stages(lax.axis_size("gz"), lax.axis_size("gx"))
    padded = padded_from(art_volume, halo_exchange(art_volume))
    change_total = None
    smooth = art_volume
    for sweep_index in range(TV_STEPS):
        slope = tv_grad(pad_depth(padded))
        slope_part = jnp.sum(slope * slope)
        totals, halo = tv_exchange(
            pack_pair(slope_part, change_part if sweep_index == 0 else 0.0), slope, stages)
        if sweep_index == 0:
            change_total = totals[0, 1]
        slope_total = totals[0, 0]
        scale_now = step_gain * jnp.sqrt(change_total) / jnp.sqrt(slope_total + norm_floor)
        smooth = smooth - scale_now * slope
        if sweep_index + 1 < TV_STEPS:
            padded = padded - scale_now * padded_from(slope, halo)
    return smooth


def solution(mesh):
    return jax.shard_map(
        body,
        mesh=mesh,
        in_specs=(
            P("gz", "gx", None),
            P(None, "gz", None),
            P(),
            P(),
            P(None, "gz", "gx"),
            P(None, "gz", "gx"),
            P(None, "gz", "gx"),
            P(None, "gz", "gx"),
        ),
        out_specs=P("gz", "gx", None),
        check_vma=False,
    )
```

```python
import functools
import math

import jax
import jax.numpy as jnp
from jax import lax
from jax.experimental import pallas as pl
from jax.experimental.pallas import tpu as pltpu
from jax.sharding import PartitionSpec as P

TV_STEPS = 4


smooth_floor = 0.01
step_gain = 0.25
norm_floor = 1e-06
group_rows = 128


MESH = pl.DeviceIdType.MESH


def _peer(axis, position):
    if axis == "gz":
        return (position, lax.axis_index("gx"))
    return (lax.axis_index("gz"), position)


def vector_sum_kernel(n, x_ref, o_ref, recv, red, gath, ssem1, rsem1, ssem2, rsem2):
    me = lax.axis_index("gx")
    barrier = pltpu.get_barrier_semaphore()
    @pl.loop(1, n)
    def _(d):
        pl.semaphore_signal(barrier, inc=1, device_id=_peer("gx", lax.rem(me + d, n)), device_id_type=MESH)

    pl.semaphore_wait(barrier, n - 1)

    def scatter_copy(d):
        dst = lax.rem(me + d, n)
        return pltpu.make_async_remote_copy(
            src_ref=x_ref.at[dst], dst_ref=recv.at[d], send_sem=ssem1.at[d], recv_sem=rsem1.at[d],
            device_id=_peer("gx", dst), device_id_type=MESH)

    def gather_copy(d):
        dst = lax.rem(me + d, n)
        return pltpu.make_async_remote_copy(
            src_ref=red, dst_ref=gath.at[me], send_sem=ssem2.at[d], recv_sem=rsem2.at[d],
            device_id=_peer("gx", dst), device_id_type=MESH)

    @pl.loop(1, n)
    def _(d):
        scatter_copy(d).start()

    @pl.loop(1, n)
    def _(d):
        scatter_copy(d).wait()

    total = lax.fori_loop(
        1, n, lambda d, acc: acc + recv[d].astype(jnp.float32), x_ref[me].astype(jnp.float32))
    red[...] = total.astype(red.dtype)

    @pl.loop(1, n)
    def _(d):
        gather_copy(d).start()

    @pl.loop(1, n)
    def _(d):
        gather_copy(d).wait()

    gath[me] = red[...]
    o_ref[...] = gath[...]


def vector_sum(x):
    n, rows, cols = x.shape
    return pl.pallas_call(
        functools.partial(vector_sum_kernel, n),
        out_shape=jax.ShapeDtypeStruct(x.shape, x.dtype),
        in_specs=[pl.BlockSpec(memory_space=pltpu.VMEM)],
        out_specs=pl.BlockSpec(memory_space=pltpu.VMEM),
        scratch_shapes=[
            pltpu.VMEM(x.shape, x.dtype),
            pltpu.VMEM((rows, cols), x.dtype),
            pltpu.VMEM(x.shape, x.dtype),
            pltpu.SemaphoreType.DMA((n,)),
            pltpu.SemaphoreType.DMA((n,)),
            pltpu.SemaphoreType.DMA((n,)),
            pltpu.SemaphoreType.DMA((n,)),
        ],
        compiler_params=pltpu.CompilerParams(collective_id=1, has_side_effects=True),
    )(x)


def _stage_peers(stage):
    if isinstance(stage[0], str):
        stage = [stage]
    index = {axis: lax.axis_index(axis) for axis, _, _ in stage}
    digits = [lax.rem(index[axis] // stride, size) for axis, stride, size in stage]
    total = 1
    position = 0
    for (_, _, size), digit in zip(stage, digits):
        position = position * size + digit
        total *= size
    peers = []
    for d in range(1, total):
        q = lax.rem(position + d, total)
        coords = dict(index)
        rest = total
        for (axis, stride, size), digit in zip(stage, digits):
            rest //= size
            coords[axis] = coords[axis] + (lax.rem(q // rest, size) - digit) * stride
        peers.append((coords.get("gz", lax.axis_index("gz")), coords.get("gx", lax.axis_index("gx"))))
    return position, total, peers


def fill_faces(c_ref, faces, depth, width):
    faces[pl.ds(0, depth)] = c_ref[width - 1]
    faces[pl.ds(depth, depth)] = c_ref[0]
    faces[pl.ds(2 * depth, width)] = c_ref[:, depth - 1, :]
    faces[pl.ds(2 * depth + width, width)] = c_ref[:, 0, :]
    faces[pl.ds(2 * depth + 2 * width, 1)] = c_ref[width - 1, pl.ds(0, 1), :]
    faces[pl.ds(2 * depth + 2 * width + 1, 1)] = c_ref[0, pl.ds(depth - 1, 1), :]


def write_halo(h_ref, hrecv, depth, width):
    count_z, count_x = lax.axis_size("gz"), lax.axis_size("gx")
    z, x = lax.axis_index("gz"), lax.axis_index("gx")
    corner = 2 * depth + 2 * width
    parts = [
        (0, depth, z > 0),
        (depth, depth, z < count_z - 1),
        (2 * depth, width, x > 0),
        (2 * depth + width, width, x < count_x - 1),
        (corner, 1, (z > 0) & (x < count_x - 1)),
        (corner + 1, 1, (z < count_z - 1) & (x > 0)),
    ]
    for row, rows, keep in parts:
        values = hrecv[pl.ds(row, rows)]
        h_ref[pl.ds(row, rows)] = jnp.where(keep, values, jnp.zeros_like(values))


def halo_routes(depth, width):
    count_z, count_x = lax.axis_size("gz"), lax.axis_size("gx")
    z, x = lax.axis_index("gz"), lax.axis_index("gx")
    up_z, down_z = lax.rem(z + 1, count_z), lax.rem(z + count_z - 1, count_z)
    up_x, down_x = lax.rem(x + 1, count_x), lax.rem(x + count_x - 1, count_x)
    return [
        (0, depth, (up_z, x)),
        (depth, depth, (down_z, x)),
        (2 * depth, width, (z, up_x)),
        (2 * depth + width, width, (z, down_x)),
        (2 * depth + 2 * width, 1, (up_z, down_x)),
        (2 * depth + 2 * width + 1, 1, (down_z, up_x)),
    ]


def _stage_info(stage):
    index = {axis: lax.axis_index(axis) for axis, _, _ in stage}
    digits = [lax.rem(index[axis] // stride, size) for axis, stride, size in stage]
    total = 1
    position = 0
    for (_, _, size), digit in zip(stage, digits):
        position = position * size + digit
        total *= size

    def peer(d):
        q = lax.rem(position + d, total)
        coords = dict(index)
        rest = total
        for (axis, stride, size), digit in zip(stage, digits):
            rest //= size
            coords[axis] = coords[axis] + (lax.rem(q // rest, size) - digit) * stride
        return (coords.get("gz", lax.axis_index("gz")), coords.get("gx", lax.axis_index("gx")))

    return position, total, peer


def tv_exchange_kernel(stages, shape, x_ref, c_ref, o_ref, h_ref, buf, recv, ssem, rsem, hrecv, hsend, hget, f_ref):
    routes = halo_routes(*shape)
    fill_faces(c_ref, f_ref, *shape)
    plan = [_stage_info(stage) for stage in stages]
    barrier = pltpu.get_barrier_semaphore()
    count = 0
    for _, size, peer in plan:

        @pl.loop(1, size)
        def _(d):
            pl.semaphore_signal(barrier, inc=1, device_id=peer(d), device_id_type=MESH)

        count += size - 1
    for _, _, target in routes:
        pl.semaphore_signal(barrier, inc=1, device_id=target, device_id_type=MESH)
        count += 1
    pl.semaphore_wait(barrier, count)
    halo = []
    for k, (row, rows, target) in enumerate(routes):
        copy = pltpu.make_async_remote_copy(
            src_ref=f_ref.at[pl.ds(row, rows)], dst_ref=hrecv.at[pl.ds(row, rows)],
            send_sem=hsend.at[k], recv_sem=hget.at[k], device_id=target, device_id_type=MESH)
        copy.start()
        halo.append(copy)
    slot = 0
    for s, (position, size, peer) in enumerate(plan):
        source = x_ref if s == 0 else buf.at[s - 1]
        recv[slot] = x_ref[...] if s == 0 else buf[s - 1]

        def sum_copy(d, source=source, slot=slot, peer=peer):
            return pltpu.make_async_remote_copy(
                src_ref=source, dst_ref=recv.at[slot + d], send_sem=ssem.at[slot + d],
                recv_sem=rsem.at[slot + d], device_id=peer(d), device_id_type=MESH)

        @pl.loop(1, size)
        def _(d):
            sum_copy(d).start()

        @pl.loop(1, size)
        def _(d):
            sum_copy(d).wait()

        total = lax.fori_loop(
            1, size,
            lambda p, acc, slot=slot, position=position, size=size:
                acc + recv[slot + lax.rem(position - p + size, size)],
            recv[slot + position])
        slot += size
        if s + 1 < len(plan):
            buf[s] = total
    o_ref[...] = total
    for copy in halo:
        copy.wait()
    write_halo(h_ref, hrecv, *shape)


def tv_exchange(x, cells, stages):
    width, depth, lanes = cells.shape
    rows = 2 * depth + 2 * width + 2
    slots = sum(math.prod(size for _, _, size in stage) for stage in stages)
    return pl.pallas_call(
        functools.partial(tv_exchange_kernel, stages, (depth, width)),
        out_shape=(jax.ShapeDtypeStruct(x.shape, x.dtype), jax.ShapeDtypeStruct((rows, lanes), cells.dtype)),
        in_specs=[pl.BlockSpec(memory_space=pltpu.VMEM)] * 2,
        out_specs=(pl.BlockSpec(memory_space=pltpu.VMEM), pl.BlockSpec(memory_space=pltpu.VMEM)),
        scratch_shapes=[
            pltpu.VMEM((max(len(stages) - 1, 1),) + x.shape, x.dtype),
            pltpu.VMEM((slots,) + x.shape, x.dtype),
            pltpu.SemaphoreType.DMA((slots,)),
            pltpu.SemaphoreType.DMA((slots,)),
            pltpu.VMEM((rows, lanes), cells.dtype),
            pltpu.SemaphoreType.DMA((6,)),
            pltpu.SemaphoreType.DMA((6,)),
            pltpu.VMEM((rows, lanes), cells.dtype),
        ],
        compiler_params=pltpu.CompilerParams(collective_id=3, has_side_effects=True),
    )(x, cells)


def halo_exchange_kernel(shape, c_ref, h_ref, hrecv, hsend, hget, f_ref):
    routes = halo_routes(*shape)
    fill_faces(c_ref, f_ref, *shape)
    barrier = pltpu.get_barrier_semaphore()
    for _, _, target in routes:
        pl.semaphore_signal(barrier, inc=1, device_id=target, device_id_type=MESH)
    pl.semaphore_wait(barrier, len(routes))
    halo = []
    for k, (row, rows, target) in enumerate(routes):
        copy = pltpu.make_async_remote_copy(
            src_ref=f_ref.at[pl.ds(row, rows)], dst_ref=hrecv.at[pl.ds(row, rows)],
            send_sem=hsend.at[k], recv_sem=hget.at[k], device_id=target, device_id_type=MESH)
        copy.start()
        halo.append(copy)
    for copy in halo:
        copy.wait()
    write_halo(h_ref, hrecv, *shape)


def halo_exchange(cells):
    width, depth, lanes = cells.shape
    rows = 2 * depth + 2 * width + 2
    return pl.pallas_call(
        functools.partial(halo_exchange_kernel, (depth, width)),
        out_shape=jax.ShapeDtypeStruct((rows, lanes), cells.dtype),
        in_specs=[pl.BlockSpec(memory_space=pltpu.VMEM)],
        out_specs=pl.BlockSpec(memory_space=pltpu.VMEM),
        scratch_shapes=[
            pltpu.VMEM((rows, lanes), cells.dtype),
            pltpu.SemaphoreType.DMA((6,)),
            pltpu.SemaphoreType.DMA((6,)),
            pltpu.VMEM((rows, lanes), cells.dtype),
        ],
        compiler_params=pltpu.CompilerParams(collective_id=4, has_side_effects=True),
    )(cells)


def faces_of(cells):
    return jnp.concatenate(
        [cells[-1], cells[0], cells[:, -1], cells[:, 0], cells[-1, :1], cells[0, -1:]], axis=0)


def padded_from(cells, halo):
    depth, width = cells.shape[1], cells.shape[0]
    low_z = halo[:depth][None]
    high_z = halo[depth:2 * depth][None]
    low_x = halo[2 * depth:2 * depth + width][:, None]
    high_x = halo[2 * depth + width:2 * depth + 2 * width][:, None]
    corner = 2 * depth + 2 * width
    low_z_high_x = halo[corner:corner + 1][None]
    high_z_low_x = halo[corner + 1:corner + 2][None]
    zero_line = jnp.zeros_like(cells[:1, :1])
    top = jnp.concatenate([zero_line, low_z, low_z_high_x], axis=1)
    middle = jnp.concatenate([low_x, cells, high_x], axis=1)
    bottom = jnp.concatenate([high_z_low_x, high_z, zero_line], axis=1)
    return jnp.concatenate([top, middle, bottom], axis=0)


def scalar_stages(n_gz, n_gx):
    if n_gx % 4 == 0 and n_gx > 4:
        return [[("gz", 1, n_gz), ("gx", 1, 4)], [("gx", 4, n_gx // 4)]]
    return [[("gz", 1, n_gz)], [("gx", 1, n_gx)]]


def pack_pair(a, b):
    lane = lax.broadcasted_iota(jnp.int32, (8, 128), 1)
    return jnp.where(lane == 0, a, jnp.where(lane == 1, b, 0.0)).astype(jnp.float32)


def one_hot(index, size):
    return (index[:, None] == jnp.arange(size, dtype=jnp.int32)[None, :]).astype(jnp.bfloat16)


def block_apply_kernel(group, transposed, x_ref, blk_ref, w_ref, o_ref):
    o_ref[...] = jnp.zeros_like(o_ref)
    x = x_ref[...]
    chosen = blk_ref[...]
    zero = jnp.zeros_like(x)
    dims = (((1,), (1,)), ((), ())) if transposed else (((1,), (0,)), ((), ()))

    def step(p, carry):
        parts = [jnp.where(chosen == p * group + i, x, zero) for i in range(group)]
        joined = jnp.concatenate(parts, axis=1)
        weights = jnp.concatenate(
            [w_ref[p * group + i] for i in range(group)], axis=1 if transposed else 0)
        o_ref[...] += lax.dot_general(joined, weights, dims, preferred_element_type=jnp.float32)
        return carry

    lax.fori_loop(0, w_ref.shape[0] // group, step, 0)


def block_apply(x, chosen, weights, group, transposed):
    entries, width = x.shape
    flops = 2 * entries * width * width * weights.shape[0]
    return pl.pallas_call(
        functools.partial(block_apply_kernel, group, transposed),
        out_shape=jax.ShapeDtypeStruct((entries, width), jnp.float32),
        in_specs=[pl.BlockSpec(memory_space=pltpu.VMEM)] * 3,
        out_specs=pl.BlockSpec(memory_space=pltpu.VMEM),
        cost_estimate=pl.CostEstimate(
            flops=flops, transcendentals=0, bytes_accessed=weights.size * 2 + entries * width * 10),
    )(x, chosen, weights)


def shift_from(block, pairs_of):
    count_z, count_x = lax.axis_size("gz"), lax.axis_size("gx")
    pairs = []
    for z in range(count_z):
        for x in range(count_x):
            target = pairs_of(z, x)
            if 0 <= target[0] < count_z and 0 <= target[1] < count_x:
                pairs.append((z * count_x + x, target[0] * count_x + target[1]))
    return lax.ppermute(block, ("gz", "gx"), pairs)


def padded_2(cells):
    zero_line = jnp.zeros_like(cells[:1, :1])
    low_z = shift_from(cells[-1:], lambda z, x: (z + 1, x))
    high_z = shift_from(cells[:1], lambda z, x: (z - 1, x))
    low_x = shift_from(cells[:, -1:], lambda z, x: (z, x + 1))
    high_x = shift_from(cells[:, :1], lambda z, x: (z, x - 1))
    low_z_high_x = shift_from(cells[-1:, :1], lambda z, x: (z + 1, x - 1))
    high_z_low_x = shift_from(cells[:1, -1:], lambda z, x: (z - 1, x + 1))
    top = jnp.concatenate([zero_line, low_z, low_z_high_x], axis=1)
    middle = jnp.concatenate([low_x, cells, high_x], axis=1)
    bottom = jnp.concatenate([high_z_low_x, high_z, zero_line], axis=1)
    return jnp.concatenate([top, middle, bottom], axis=0)


def tv_grad(padded):
    base_cells = padded[:-1, :-1, :-1]
    diff_z = padded[1:, :-1, :-1] - base_cells
    diff_x = padded[:-1, 1:, :-1] - base_cells
    diff_y = padded[:-1, :-1, 1:] - base_cells
    inverse = lax.rsqrt(diff_z * diff_z + diff_x * diff_x + diff_y * diff_y + smooth_floor)
    flow_z = diff_z * inverse
    flow_x = diff_x * inverse
    flow_y = diff_y * inverse
    flow_all = flow_z + flow_x + flow_y
    return flow_z[:-1, 1:, 1:] + flow_x[1:, :-1, 1:] + flow_y[1:, 1:, :-1] - flow_all[1:, 1:, 1:]


def pad_depth(field):
    return jnp.pad(field, ((0, 0), (0, 0), (1, 1)))


def body(
    volume, measured, weight_blocks, view_order, tile_voxel, tile_column, tile_block, entry_count
):
    depth_z, depth_x, depth_y = volume.shape
    tiles_y = depth_y // group_rows
    tiles_u = measured.shape[2] // group_rows
    slab_tiles = depth_z * tiles_u
    plane_tiles = depth_x * tiles_y
    row_weight = jnp.sum(weight_blocks, axis=2, dtype=jnp.float32)
    col_weight = jnp.sum(weight_blocks, axis=1, dtype=jnp.float32)
    n_blocks = weight_blocks.shape[0]
    group = 8 if n_blocks % 8 == 0 else 1
    current = volume
    for turn_index in range(view_order.shape[0]):
        view_index = view_order[turn_index]
        voxel_list = lax.dynamic_index_in_dim(tile_voxel, view_index, 0, keepdims=False)[0]
        column_list = lax.dynamic_index_in_dim(tile_column, view_index, 0, keepdims=False)[0]
        block_list = lax.dynamic_index_in_dim(tile_block, view_index, 0, keepdims=False)[0]
        live_count = lax.dynamic_index_in_dim(entry_count, view_index, 0, keepdims=False)[0, 0]
        entries = voxel_list.shape[0]
        live = (jnp.arange(entries, dtype=jnp.int32) < live_count)[:, None]
        detector = voxel_list // plane_tiles * tiles_u + column_list
        voxel_tiles = current.astype(jnp.bfloat16).reshape(-1, group_rows)
        pick_voxel = one_hot(voxel_list, voxel_tiles.shape[0])
        pick_detector = one_hot(detector, slab_tiles)
        pick_block = jnp.where(live, one_hot(block_list, n_blocks), 0)
        blocks_column = block_list[:, None]

        cells = jnp.dot(pick_voxel, voxel_tiles, preferred_element_type=jnp.float32)
        product = block_apply(cells.astype(jnp.bfloat16), blocks_column, weight_blocks, group, True)
        product = jnp.where(live, product, 0.0)
        projection = lax.dot_general(
            pick_detector.astype(jnp.float32), product, (((0,), (0,)), ((), ())),
            precision=lax.Precision.HIGHEST)
        detector_blocks = lax.dot_general(
            pick_detector, pick_block, (((0,), (0,)), ((), ())), preferred_element_type=jnp.float32)
        ray_sum = jnp.dot(detector_blocks, row_weight, precision=lax.Precision.HIGHEST)
        target = lax.dynamic_index_in_dim(measured, view_index, 0, keepdims=False).reshape(
            slab_tiles, group_rows
        )
        n_gx = lax.axis_size("gx")
        joined = jnp.concatenate([projection, ray_sum], axis=1).astype(jnp.bfloat16)
        joined = vector_sum(joined.reshape(n_gx, slab_tiles // n_gx, 2 * group_rows))
        joined = joined.reshape(slab_tiles, 2 * group_rows).astype(jnp.float32)
        projection, ray_sum = joined[:, :group_rows], joined[:, group_rows:]
        residual = ((target - projection) / (ray_sum + 1.0)).astype(jnp.bfloat16)

        pixels = jnp.dot(pick_detector, residual, preferred_element_type=jnp.float32)
        product = block_apply(pixels.astype(jnp.bfloat16), blocks_column, weight_blocks, group, False)
        product = jnp.where(live, product, 0.0)
        change = lax.dot_general(
            pick_voxel.astype(jnp.float32), product, (((0,), (0,)), ((), ())),
            precision=lax.Precision.HIGHEST)
        voxel_blocks = lax.dot_general(
            pick_voxel, pick_block, (((0,), (0,)), ((), ())), preferred_element_type=jnp.float32)
        voxel_sum = jnp.dot(voxel_blocks, col_weight, precision=lax.Precision.HIGHEST)
        current = current + (change / (voxel_sum + 1.0)).reshape(current.shape)
    art_volume = jnp.maximum(current, 0.0)
    difference = art_volume - volume
    change_part = jnp.sum(difference * difference)
    stages = scalar_stages(lax.axis_size("gz"), lax.axis_size("gx"))
    padded = padded_from(art_volume, halo_exchange(art_volume))
    change_total = None
    smooth = art_volume
    for sweep_index in range(TV_STEPS):
        slope = tv_grad(pad_depth(padded))
        slope_part = jnp.sum(slope * slope)
        totals, halo = tv_exchange(
            pack_pair(slope_part, change_part if sweep_index == 0 else 0.0), slope, stages)
        if sweep_index == 0:
            change_total = totals[0, 1]
        slope_total = totals[0, 0]
        scale_now = step_gain * jnp.sqrt(change_total) / jnp.sqrt(slope_total + norm_floor)
        smooth = smooth - scale_now * slope
        if sweep_index + 1 < TV_STEPS:
            padded = padded - scale_now * padded_from(slope, halo)
    return smooth


def solution(mesh):
    return jax.shard_map(
        body,
        mesh=mesh,
        in_specs=(
            P("gz", "gx", None),
            P(None, "gz", None),
            P(),
            P(),
            P(None, "gz", "gx"),
            P(None, "gz", "gx"),
            P(None, "gz", "gx"),
            P(None, "gz", "gx"),
        ),
        out_specs=P("gz", "gx", None),
        check_vma=False,
    )
```

```python
import functools
import math

import jax
import jax.numpy as jnp
from jax import lax
from jax.experimental import pallas as pl
from jax.experimental.pallas import tpu as pltpu
from jax.sharding import PartitionSpec as P

TV_STEPS = 4


smooth_floor = 0.01
step_gain = 0.25
norm_floor = 1e-06
group_rows = 128


MESH = pl.DeviceIdType.MESH


def _peer(axis, position):
    if axis == "gz":
        return (position, lax.axis_index("gx"))
    return (lax.axis_index("gz"), position)


def vector_sum_kernel(n, x_ref, o_ref, recv, red, gath, ssem1, rsem1, ssem2, rsem2):
    me = lax.axis_index("gx")
    barrier = pltpu.get_barrier_semaphore()
    for d in range(1, n):
        pl.semaphore_signal(barrier, inc=1, device_id=_peer("gx", lax.rem(me + d, n)), device_id_type=MESH)
    pl.semaphore_wait(barrier, n - 1)

    def scatter_copy(d):
        dst = lax.rem(me + d, n)
        return pltpu.make_async_remote_copy(
            src_ref=x_ref.at[dst], dst_ref=recv.at[d], send_sem=ssem1.at[d], recv_sem=rsem1.at[d],
            device_id=_peer("gx", dst), device_id_type=MESH)

    def gather_copy(d):
        dst = lax.rem(me + d, n)
        return pltpu.make_async_remote_copy(
            src_ref=red, dst_ref=gath.at[me], send_sem=ssem2.at[d], recv_sem=rsem2.at[d],
            device_id=_peer("gx", dst), device_id_type=MESH)

    @pl.loop(1, n)
    def _(d):
        scatter_copy(d).start()

    @pl.loop(1, n)
    def _(d):
        scatter_copy(d).wait()

    total = lax.fori_loop(
        1, n, lambda d, acc: acc + recv[d].astype(jnp.float32), x_ref[me].astype(jnp.float32))
    red[...] = total.astype(red.dtype)

    @pl.loop(1, n)
    def _(d):
        gather_copy(d).start()

    @pl.loop(1, n)
    def _(d):
        gather_copy(d).wait()

    gath[me] = red[...]
    o_ref[...] = gath[...]


def vector_sum(x):
    n, rows, cols = x.shape
    return pl.pallas_call(
        functools.partial(vector_sum_kernel, n),
        out_shape=jax.ShapeDtypeStruct(x.shape, x.dtype),
        in_specs=[pl.BlockSpec(memory_space=pltpu.VMEM)],
        out_specs=pl.BlockSpec(memory_space=pltpu.VMEM),
        scratch_shapes=[
            pltpu.VMEM(x.shape, x.dtype),
            pltpu.VMEM((rows, cols), x.dtype),
            pltpu.VMEM(x.shape, x.dtype),
            pltpu.SemaphoreType.DMA((n,)),
            pltpu.SemaphoreType.DMA((n,)),
            pltpu.SemaphoreType.DMA((n,)),
            pltpu.SemaphoreType.DMA((n,)),
        ],
        compiler_params=pltpu.CompilerParams(collective_id=1, has_side_effects=True),
    )(x)


def _stage_peers(stage):
    if isinstance(stage[0], str):
        stage = [stage]
    index = {axis: lax.axis_index(axis) for axis, _, _ in stage}
    digits = [lax.rem(index[axis] // stride, size) for axis, stride, size in stage]
    total = 1
    position = 0
    for (_, _, size), digit in zip(stage, digits):
        position = position * size + digit
        total *= size
    peers = []
    for d in range(1, total):
        q = lax.rem(position + d, total)
        coords = dict(index)
        rest = total
        for (axis, stride, size), digit in zip(stage, digits):
            rest //= size
            coords[axis] = coords[axis] + (lax.rem(q // rest, size) - digit) * stride
        peers.append((coords.get("gz", lax.axis_index("gz")), coords.get("gx", lax.axis_index("gx"))))
    return position, total, peers


def fill_faces(c_ref, faces, depth, width):
    faces[pl.ds(0, depth)] = c_ref[width - 1]
    faces[pl.ds(depth, depth)] = c_ref[0]
    faces[pl.ds(2 * depth, width)] = c_ref[:, depth - 1, :]
    faces[pl.ds(2 * depth + width, width)] = c_ref[:, 0, :]
    faces[pl.ds(2 * depth + 2 * width, 1)] = c_ref[width - 1, pl.ds(0, 1), :]
    faces[pl.ds(2 * depth + 2 * width + 1, 1)] = c_ref[0, pl.ds(depth - 1, 1), :]


def write_halo(h_ref, hrecv, depth, width):
    count_z, count_x = lax.axis_size("gz"), lax.axis_size("gx")
    z, x = lax.axis_index("gz"), lax.axis_index("gx")
    corner = 2 * depth + 2 * width
    parts = [
        (0, depth, z > 0),
        (depth, depth, z < count_z - 1),
        (2 * depth, width, x > 0),
        (2 * depth + width, width, x < count_x - 1),
        (corner, 1, (z > 0) & (x < count_x - 1)),
        (corner + 1, 1, (z < count_z - 1) & (x > 0)),
    ]
    for row, rows, keep in parts:
        values = hrecv[pl.ds(row, rows)]
        h_ref[pl.ds(row, rows)] = jnp.where(keep, values, jnp.zeros_like(values))


def halo_routes(depth, width):
    count_z, count_x = lax.axis_size("gz"), lax.axis_size("gx")
    z, x = lax.axis_index("gz"), lax.axis_index("gx")
    up_z, down_z = lax.rem(z + 1, count_z), lax.rem(z + count_z - 1, count_z)
    up_x, down_x = lax.rem(x + 1, count_x), lax.rem(x + count_x - 1, count_x)
    return [
        (0, depth, (up_z, x)),
        (depth, depth, (down_z, x)),
        (2 * depth, width, (z, up_x)),
        (2 * depth + width, width, (z, down_x)),
        (2 * depth + 2 * width, 1, (up_z, down_x)),
        (2 * depth + 2 * width + 1, 1, (down_z, up_x)),
    ]


def tv_exchange_kernel(stages, shape, x_ref, c_ref, o_ref, h_ref, buf, recv, ssem, rsem, hrecv, hsend, hget, f_ref):
    routes = halo_routes(*shape)
    fill_faces(c_ref, f_ref, *shape)
    plan = [_stage_peers(stage) for stage in stages]
    barrier = pltpu.get_barrier_semaphore()
    count = 0
    for _, _, peers in plan:
        for peer in peers:
            pl.semaphore_signal(barrier, inc=1, device_id=peer, device_id_type=MESH)
            count += 1
    for _, _, target in routes:
        pl.semaphore_signal(barrier, inc=1, device_id=target, device_id_type=MESH)
        count += 1
    pl.semaphore_wait(barrier, count)
    halo = []
    for k, (row, rows, target) in enumerate(routes):
        copy = pltpu.make_async_remote_copy(
            src_ref=f_ref.at[pl.ds(row, rows)], dst_ref=hrecv.at[pl.ds(row, rows)],
            send_sem=hsend.at[k], recv_sem=hget.at[k], device_id=target, device_id_type=MESH)
        copy.start()
        halo.append(copy)
    total = x_ref[...]
    slot = 0
    for s, (position, size, peers) in enumerate(plan):
        source = x_ref if s == 0 else buf.at[s - 1]
        recv[slot] = total
        sends = []
        for d, peer in enumerate(peers, start=1):
            copy = pltpu.make_async_remote_copy(
                src_ref=source, dst_ref=recv.at[slot + d], send_sem=ssem.at[slot + d],
                recv_sem=rsem.at[slot + d], device_id=peer, device_id_type=MESH)
            copy.start()
            sends.append(copy)
        for copy in sends:
            copy.wait()
        total = recv[slot + position]
        for p in range(1, size):
            total = total + recv[slot + lax.rem(position - p + size, size)]
        slot += size
        if s + 1 < len(plan):
            buf[s] = total
    o_ref[...] = total
    for copy in halo:
        copy.wait()
    write_halo(h_ref, hrecv, *shape)


def tv_exchange(x, cells, stages):
    width, depth, lanes = cells.shape
    rows = 2 * depth + 2 * width + 2
    slots = sum(math.prod(size for _, _, size in stage) for stage in stages)
    return pl.pallas_call(
        functools.partial(tv_exchange_kernel, stages, (depth, width)),
        out_shape=(jax.ShapeDtypeStruct(x.shape, x.dtype), jax.ShapeDtypeStruct((rows, lanes), cells.dtype)),
        in_specs=[pl.BlockSpec(memory_space=pltpu.VMEM)] * 2,
        out_specs=(pl.BlockSpec(memory_space=pltpu.VMEM), pl.BlockSpec(memory_space=pltpu.VMEM)),
        scratch_shapes=[
            pltpu.VMEM((max(len(stages) - 1, 1),) + x.shape, x.dtype),
            pltpu.VMEM((slots,) + x.shape, x.dtype),
            pltpu.SemaphoreType.DMA((slots,)),
            pltpu.SemaphoreType.DMA((slots,)),
            pltpu.VMEM((rows, lanes), cells.dtype),
            pltpu.SemaphoreType.DMA((6,)),
            pltpu.SemaphoreType.DMA((6,)),
            pltpu.VMEM((rows, lanes), cells.dtype),
        ],
        compiler_params=pltpu.CompilerParams(collective_id=3, has_side_effects=True),
    )(x, cells)


def halo_exchange_kernel(shape, c_ref, h_ref, hrecv, hsend, hget, f_ref):
    routes = halo_routes(*shape)
    fill_faces(c_ref, f_ref, *shape)
    barrier = pltpu.get_barrier_semaphore()
    for _, _, target in routes:
        pl.semaphore_signal(barrier, inc=1, device_id=target, device_id_type=MESH)
    pl.semaphore_wait(barrier, len(routes))
    halo = []
    for k, (row, rows, target) in enumerate(routes):
        copy = pltpu.make_async_remote_copy(
            src_ref=f_ref.at[pl.ds(row, rows)], dst_ref=hrecv.at[pl.ds(row, rows)],
            send_sem=hsend.at[k], recv_sem=hget.at[k], device_id=target, device_id_type=MESH)
        copy.start()
        halo.append(copy)
    for copy in halo:
        copy.wait()
    write_halo(h_ref, hrecv, *shape)


def halo_exchange(cells):
    width, depth, lanes = cells.shape
    rows = 2 * depth + 2 * width + 2
    return pl.pallas_call(
        functools.partial(halo_exchange_kernel, (depth, width)),
        out_shape=jax.ShapeDtypeStruct((rows, lanes), cells.dtype),
        in_specs=[pl.BlockSpec(memory_space=pltpu.VMEM)],
        out_specs=pl.BlockSpec(memory_space=pltpu.VMEM),
        scratch_shapes=[
            pltpu.VMEM((rows, lanes), cells.dtype),
            pltpu.SemaphoreType.DMA((6,)),
            pltpu.SemaphoreType.DMA((6,)),
            pltpu.VMEM((rows, lanes), cells.dtype),
        ],
        compiler_params=pltpu.CompilerParams(collective_id=4, has_side_effects=True),
    )(cells)


def faces_of(cells):
    return jnp.concatenate(
        [cells[-1], cells[0], cells[:, -1], cells[:, 0], cells[-1, :1], cells[0, -1:]], axis=0)


def padded_from(cells, halo):
    depth, width = cells.shape[1], cells.shape[0]
    low_z = halo[:depth][None]
    high_z = halo[depth:2 * depth][None]
    low_x = halo[2 * depth:2 * depth + width][:, None]
    high_x = halo[2 * depth + width:2 * depth + 2 * width][:, None]
    corner = 2 * depth + 2 * width
    low_z_high_x = halo[corner:corner + 1][None]
    high_z_low_x = halo[corner + 1:corner + 2][None]
    zero_line = jnp.zeros_like(cells[:1, :1])
    top = jnp.concatenate([zero_line, low_z, low_z_high_x], axis=1)
    middle = jnp.concatenate([low_x, cells, high_x], axis=1)
    bottom = jnp.concatenate([high_z_low_x, high_z, zero_line], axis=1)
    return jnp.concatenate([top, middle, bottom], axis=0)


def scalar_stages(n_gz, n_gx):
    if n_gx % 4 == 0 and n_gx > 4:
        return [[("gz", 1, n_gz), ("gx", 1, 4)], [("gx", 4, n_gx // 4)]]
    return [[("gz", 1, n_gz)], [("gx", 1, n_gx)]]


def pack_pair(a, b):
    lane = lax.broadcasted_iota(jnp.int32, (8, 128), 1)
    return jnp.where(lane == 0, a, jnp.where(lane == 1, b, 0.0)).astype(jnp.float32)


def one_hot(index, size):
    return (index[:, None] == jnp.arange(size, dtype=jnp.int32)[None, :]).astype(jnp.bfloat16)


def block_apply_kernel(group, transposed, idx_ref, t_ref, blk_ref, w_ref, o_ref):
    o_ref[...] = jnp.zeros_like(o_ref)
    entries, size = idx_ref.shape[0], t_ref.shape[0]
    picks = idx_ref[...] == lax.broadcasted_iota(jnp.int32, (entries, size), 1)
    pick = jnp.where(picks, 1.0, 0.0).astype(t_ref.dtype)
    x = jnp.dot(pick, t_ref[...], preferred_element_type=jnp.float32).astype(t_ref.dtype)
    chosen = blk_ref[...]
    zero = jnp.zeros_like(x)
    dims = (((1,), (1,)), ((), ())) if transposed else (((1,), (0,)), ((), ()))

    def step(p, carry):
        parts = [jnp.where(chosen == p * group + i, x, zero) for i in range(group)]
        joined = jnp.concatenate(parts, axis=1)
        weights = jnp.concatenate(
            [w_ref[p * group + i] for i in range(group)], axis=1 if transposed else 0)
        o_ref[...] += lax.dot_general(joined, weights, dims, preferred_element_type=jnp.float32)
        return carry

    lax.fori_loop(0, w_ref.shape[0] // group, step, 0)


def block_apply(index, table, chosen, weights, group, transposed):
    entries, width = index.shape[0], table.shape[1]
    flops = 2 * entries * width * width * weights.shape[0] + 2 * entries * table.size
    return pl.pallas_call(
        functools.partial(block_apply_kernel, group, transposed),
        out_shape=jax.ShapeDtypeStruct((entries, width), jnp.float32),
        in_specs=[pl.BlockSpec(memory_space=pltpu.VMEM)] * 4,
        out_specs=pl.BlockSpec(memory_space=pltpu.VMEM),
        cost_estimate=pl.CostEstimate(
            flops=flops, transcendentals=0, bytes_accessed=weights.size * 2 + entries * width * 10),
    )(index[:, None], table, chosen, weights)


def shift_from(block, pairs_of):
    count_z, count_x = lax.axis_size("gz"), lax.axis_size("gx")
    pairs = []
    for z in range(count_z):
        for x in range(count_x):
            target = pairs_of(z, x)
            if 0 <= target[0] < count_z and 0 <= target[1] < count_x:
                pairs.append((z * count_x + x, target[0] * count_x + target[1]))
    return lax.ppermute(block, ("gz", "gx"), pairs)


def padded_2(cells):
    zero_line = jnp.zeros_like(cells[:1, :1])
    low_z = shift_from(cells[-1:], lambda z, x: (z + 1, x))
    high_z = shift_from(cells[:1], lambda z, x: (z - 1, x))
    low_x = shift_from(cells[:, -1:], lambda z, x: (z, x + 1))
    high_x = shift_from(cells[:, :1], lambda z, x: (z, x - 1))
    low_z_high_x = shift_from(cells[-1:, :1], lambda z, x: (z + 1, x - 1))
    high_z_low_x = shift_from(cells[:1, -1:], lambda z, x: (z - 1, x + 1))
    top = jnp.concatenate([zero_line, low_z, low_z_high_x], axis=1)
    middle = jnp.concatenate([low_x, cells, high_x], axis=1)
    bottom = jnp.concatenate([high_z_low_x, high_z, zero_line], axis=1)
    return jnp.concatenate([top, middle, bottom], axis=0)


def tv_grad(padded):
    base_cells = padded[:-1, :-1, :-1]
    diff_z = padded[1:, :-1, :-1] - base_cells
    diff_x = padded[:-1, 1:, :-1] - base_cells
    diff_y = padded[:-1, :-1, 1:] - base_cells
    inverse = lax.rsqrt(diff_z * diff_z + diff_x * diff_x + diff_y * diff_y + smooth_floor)
    flow_z = diff_z * inverse
    flow_x = diff_x * inverse
    flow_y = diff_y * inverse
    flow_all = flow_z + flow_x + flow_y
    return flow_z[:-1, 1:, 1:] + flow_x[1:, :-1, 1:] + flow_y[1:, 1:, :-1] - flow_all[1:, 1:, 1:]


def pad_depth(field):
    return jnp.pad(field, ((0, 0), (0, 0), (1, 1)))


def body(
    volume, measured, weight_blocks, view_order, tile_voxel, tile_column, tile_block, entry_count
):
    depth_z, depth_x, depth_y = volume.shape
    tiles_y = depth_y // group_rows
    tiles_u = measured.shape[2] // group_rows
    slab_tiles = depth_z * tiles_u
    plane_tiles = depth_x * tiles_y
    row_weight = jnp.sum(weight_blocks, axis=2, dtype=jnp.float32)
    col_weight = jnp.sum(weight_blocks, axis=1, dtype=jnp.float32)
    n_blocks = weight_blocks.shape[0]
    group = 8 if n_blocks % 8 == 0 else 1
    current = volume
    for turn_index in range(view_order.shape[0]):
        view_index = view_order[turn_index]
        voxel_list = lax.dynamic_index_in_dim(tile_voxel, view_index, 0, keepdims=False)[0]
        column_list = lax.dynamic_index_in_dim(tile_column, view_index, 0, keepdims=False)[0]
        block_list = lax.dynamic_index_in_dim(tile_block, view_index, 0, keepdims=False)[0]
        live_count = lax.dynamic_index_in_dim(entry_count, view_index, 0, keepdims=False)[0, 0]
        entries = voxel_list.shape[0]
        live = (jnp.arange(entries, dtype=jnp.int32) < live_count)[:, None]
        detector = voxel_list // plane_tiles * tiles_u + column_list
        voxel_tiles = current.astype(jnp.bfloat16).reshape(-1, group_rows)
        pick_voxel = one_hot(voxel_list, voxel_tiles.shape[0])
        pick_detector = one_hot(detector, slab_tiles)
        pick_block = jnp.where(live, one_hot(block_list, n_blocks), 0)
        blocks_column = block_list[:, None]

        product = block_apply(voxel_list, voxel_tiles, blocks_column, weight_blocks, group, True)
        product = jnp.where(live, product, 0.0)
        projection = lax.dot_general(
            pick_detector.astype(jnp.float32), product, (((0,), (0,)), ((), ())),
            precision=lax.Precision.HIGHEST)
        detector_blocks = lax.dot_general(
            pick_detector, pick_block, (((0,), (0,)), ((), ())), preferred_element_type=jnp.float32)
        ray_sum = jnp.dot(detector_blocks, row_weight, precision=lax.Precision.HIGHEST)
        target = lax.dynamic_index_in_dim(measured, view_index, 0, keepdims=False).reshape(
            slab_tiles, group_rows
        )
        n_gx = lax.axis_size("gx")
        joined = jnp.concatenate([projection, ray_sum], axis=1).astype(jnp.bfloat16)
        joined = vector_sum(joined.reshape(n_gx, slab_tiles // n_gx, 2 * group_rows))
        joined = joined.reshape(slab_tiles, 2 * group_rows).astype(jnp.float32)
        projection, ray_sum = joined[:, :group_rows], joined[:, group_rows:]
        residual = ((target - projection) / (ray_sum + 1.0)).astype(jnp.bfloat16)

        product = block_apply(detector, residual, blocks_column, weight_blocks, group, False)
        product = jnp.where(live, product, 0.0)
        change = lax.dot_general(
            pick_voxel.astype(jnp.float32), product, (((0,), (0,)), ((), ())),
            precision=lax.Precision.HIGHEST)
        voxel_blocks = lax.dot_general(
            pick_voxel, pick_block, (((0,), (0,)), ((), ())), preferred_element_type=jnp.float32)
        voxel_sum = jnp.dot(voxel_blocks, col_weight, precision=lax.Precision.HIGHEST)
        current = current + (change / (voxel_sum + 1.0)).reshape(current.shape)
    art_volume = jnp.maximum(current, 0.0)
    difference = art_volume - volume
    change_part = jnp.sum(difference * difference)
    stages = scalar_stages(lax.axis_size("gz"), lax.axis_size("gx"))
    padded = padded_from(art_volume, halo_exchange(art_volume))
    change_total = None
    smooth = art_volume
    for sweep_index in range(TV_STEPS):
        slope = tv_grad(pad_depth(padded))
        slope_part = jnp.sum(slope * slope)
        totals, halo = tv_exchange(
            pack_pair(slope_part, change_part if sweep_index == 0 else 0.0), slope, stages)
        if sweep_index == 0:
            change_total = totals[0, 1]
        slope_total = totals[0, 0]
        scale_now = step_gain * jnp.sqrt(change_total) / jnp.sqrt(slope_total + norm_floor)
        smooth = smooth - scale_now * slope
        if sweep_index + 1 < TV_STEPS:
            padded = padded - scale_now * padded_from(slope, halo)
    return smooth


def solution(mesh):
    return jax.shard_map(
        body,
        mesh=mesh,
        in_specs=(
            P("gz", "gx", None),
            P(None, "gz", None),
            P(),
            P(),
            P(None, "gz", "gx"),
            P(None, "gz", "gx"),
            P(None, "gz", "gx"),
            P(None, "gz", "gx"),
        ),
        out_specs=P("gz", "gx", None),
        check_vma=False,
    )
```

```python
import functools
import math

import jax
import jax.numpy as jnp
from jax import lax
from jax.experimental import pallas as pl
from jax.experimental.pallas import tpu as pltpu
from jax.sharding import PartitionSpec as P

TV_STEPS = 4


smooth_floor = 0.01
step_gain = 0.25
norm_floor = 1e-06
group_rows = 128


MESH = pl.DeviceIdType.MESH


def _peer(axis, position):
    if axis == "gz":
        return (position, lax.axis_index("gx"))
    return (lax.axis_index("gz"), position)


def vector_sum_kernel(n, x_ref, o_ref, recv, red, gath, ssem1, rsem1, ssem2, rsem2):
    me = lax.axis_index("gx")
    barrier = pltpu.get_barrier_semaphore()
    for d in range(1, n):
        pl.semaphore_signal(barrier, inc=1, device_id=_peer("gx", lax.rem(me + d, n)), device_id_type=MESH)
    pl.semaphore_wait(barrier, n - 1)

    def scatter_copy(d):
        dst = lax.rem(me + d, n)
        return pltpu.make_async_remote_copy(
            src_ref=x_ref.at[dst], dst_ref=recv.at[d], send_sem=ssem1.at[d], recv_sem=rsem1.at[d],
            device_id=_peer("gx", dst), device_id_type=MESH)

    def gather_copy(d):
        dst = lax.rem(me + d, n)
        return pltpu.make_async_remote_copy(
            src_ref=red, dst_ref=gath.at[me], send_sem=ssem2.at[d], recv_sem=rsem2.at[d],
            device_id=_peer("gx", dst), device_id_type=MESH)

    @pl.loop(1, n)
    def _(d):
        scatter_copy(d).start()

    @pl.loop(1, n)
    def _(d):
        scatter_copy(d).wait()

    total = lax.fori_loop(
        1, n, lambda d, acc: acc + recv[d].astype(jnp.float32), x_ref[me].astype(jnp.float32))
    red[...] = total.astype(red.dtype)

    @pl.loop(1, n)
    def _(d):
        gather_copy(d).start()

    @pl.loop(1, n)
    def _(d):
        gather_copy(d).wait()

    gath[me] = red[...]
    o_ref[...] = gath[...]


def vector_sum(x):
    n, rows, cols = x.shape
    return pl.pallas_call(
        functools.partial(vector_sum_kernel, n),
        out_shape=jax.ShapeDtypeStruct(x.shape, x.dtype),
        in_specs=[pl.BlockSpec(memory_space=pltpu.VMEM)],
        out_specs=pl.BlockSpec(memory_space=pltpu.VMEM),
        scratch_shapes=[
            pltpu.VMEM(x.shape, x.dtype),
            pltpu.VMEM((rows, cols), x.dtype),
            pltpu.VMEM(x.shape, x.dtype),
            pltpu.SemaphoreType.DMA((n,)),
            pltpu.SemaphoreType.DMA((n,)),
            pltpu.SemaphoreType.DMA((n,)),
            pltpu.SemaphoreType.DMA((n,)),
        ],
        compiler_params=pltpu.CompilerParams(collective_id=1, has_side_effects=True),
    )(x)


def _stage_peers(stage):
    if isinstance(stage[0], str):
        stage = [stage]
    index = {axis: lax.axis_index(axis) for axis, _, _ in stage}
    digits = [lax.rem(index[axis] // stride, size) for axis, stride, size in stage]
    total = 1
    position = 0
    for (_, _, size), digit in zip(stage, digits):
        position = position * size + digit
        total *= size
    peers = []
    for d in range(1, total):
        q = lax.rem(position + d, total)
        coords = dict(index)
        rest = total
        for (axis, stride, size), digit in zip(stage, digits):
            rest //= size
            coords[axis] = coords[axis] + (lax.rem(q // rest, size) - digit) * stride
        peers.append((coords.get("gz", lax.axis_index("gz")), coords.get("gx", lax.axis_index("gx"))))
    return position, total, peers


def fill_faces(c_ref, faces, depth, width):
    faces[pl.ds(0, depth)] = c_ref[width - 1]
    faces[pl.ds(depth, depth)] = c_ref[0]
    faces[pl.ds(2 * depth, width)] = c_ref[:, depth - 1, :]
    faces[pl.ds(2 * depth + width, width)] = c_ref[:, 0, :]
    faces[pl.ds(2 * depth + 2 * width, 1)] = c_ref[width - 1, pl.ds(0, 1), :]
    faces[pl.ds(2 * depth + 2 * width + 1, 1)] = c_ref[0, pl.ds(depth - 1, 1), :]


def write_halo(h_ref, hrecv, depth, width):
    count_z, count_x = lax.axis_size("gz"), lax.axis_size("gx")
    z, x = lax.axis_index("gz"), lax.axis_index("gx")
    corner = 2 * depth + 2 * width
    parts = [
        (0, depth, z > 0),
        (depth, depth, z < count_z - 1),
        (2 * depth, width, x > 0),
        (2 * depth + width, width, x < count_x - 1),
        (corner, 1, (z > 0) & (x < count_x - 1)),
        (corner + 1, 1, (z < count_z - 1) & (x > 0)),
    ]
    for row, rows, keep in parts:
        values = hrecv[pl.ds(row, rows)]
        h_ref[pl.ds(row, rows)] = jnp.where(keep, values, jnp.zeros_like(values))


def halo_routes(depth, width):
    count_z, count_x = lax.axis_size("gz"), lax.axis_size("gx")
    z, x = lax.axis_index("gz"), lax.axis_index("gx")
    up_z, down_z = lax.rem(z + 1, count_z), lax.rem(z + count_z - 1, count_z)
    up_x, down_x = lax.rem(x + 1, count_x), lax.rem(x + count_x - 1, count_x)
    return [
        (0, depth, (up_z, x)),
        (depth, depth, (down_z, x)),
        (2 * depth, width, (z, up_x)),
        (2 * depth + width, width, (z, down_x)),
        (2 * depth + 2 * width, 1, (up_z, down_x)),
        (2 * depth + 2 * width + 1, 1, (down_z, up_x)),
    ]


def tv_exchange_kernel(stages, shape, x_ref, c_ref, o_ref, h_ref, buf, recv, ssem, rsem, hrecv, hsend, hget, f_ref):
    routes = halo_routes(*shape)
    fill_faces(c_ref, f_ref, *shape)
    plan = [_stage_peers(stage) for stage in stages]
    barrier = pltpu.get_barrier_semaphore()
    count = 0
    for _, _, peers in plan:
        for peer in peers:
            pl.semaphore_signal(barrier, inc=1, device_id=peer, device_id_type=MESH)
            count += 1
    for _, _, target in routes:
        pl.semaphore_signal(barrier, inc=1, device_id=target, device_id_type=MESH)
        count += 1
    pl.semaphore_wait(barrier, count)
    halo = []
    for k, (row, rows, target) in enumerate(routes):
        copy = pltpu.make_async_remote_copy(
            src_ref=f_ref.at[pl.ds(row, rows)], dst_ref=hrecv.at[pl.ds(row, rows)],
            send_sem=hsend.at[k], recv_sem=hget.at[k], device_id=target, device_id_type=MESH)
        copy.start()
        halo.append(copy)
    cells = c_ref[...]
    square = jnp.sum(jnp.sum(cells * cells, axis=0), axis=0, keepdims=True)
    square = jnp.sum(square, axis=1, keepdims=True)
    row = lax.broadcasted_iota(jnp.int32, x_ref.shape, 0)
    lane = lax.broadcasted_iota(jnp.int32, x_ref.shape, 1)
    total = x_ref[...] + jnp.where((row == 0) & (lane == 0), square, 0.0)
    buf[0] = total
    slot = 0
    for s, (position, size, peers) in enumerate(plan):
        source = buf.at[s]
        recv[slot] = total
        sends = []
        for d, peer in enumerate(peers, start=1):
            copy = pltpu.make_async_remote_copy(
                src_ref=source, dst_ref=recv.at[slot + d], send_sem=ssem.at[slot + d],
                recv_sem=rsem.at[slot + d], device_id=peer, device_id_type=MESH)
            copy.start()
            sends.append(copy)
        for copy in sends:
            copy.wait()
        total = recv[slot + position]
        for p in range(1, size):
            total = total + recv[slot + lax.rem(position - p + size, size)]
        slot += size
        if s + 1 < len(plan):
            buf[s + 1] = total
    o_ref[...] = total
    for copy in halo:
        copy.wait()
    write_halo(h_ref, hrecv, *shape)


def tv_exchange(x, cells, stages):
    width, depth, lanes = cells.shape
    rows = 2 * depth + 2 * width + 2
    slots = sum(math.prod(size for _, _, size in stage) for stage in stages)
    return pl.pallas_call(
        functools.partial(tv_exchange_kernel, stages, (depth, width)),
        out_shape=(jax.ShapeDtypeStruct(x.shape, x.dtype), jax.ShapeDtypeStruct((rows, lanes), cells.dtype)),
        in_specs=[pl.BlockSpec(memory_space=pltpu.VMEM)] * 2,
        out_specs=(pl.BlockSpec(memory_space=pltpu.VMEM), pl.BlockSpec(memory_space=pltpu.VMEM)),
        scratch_shapes=[
            pltpu.VMEM((len(stages),) + x.shape, x.dtype),
            pltpu.VMEM((slots,) + x.shape, x.dtype),
            pltpu.SemaphoreType.DMA((slots,)),
            pltpu.SemaphoreType.DMA((slots,)),
            pltpu.VMEM((rows, lanes), cells.dtype),
            pltpu.SemaphoreType.DMA((6,)),
            pltpu.SemaphoreType.DMA((6,)),
            pltpu.VMEM((rows, lanes), cells.dtype),
        ],
        compiler_params=pltpu.CompilerParams(collective_id=3, has_side_effects=True),
    )(x, cells)


def halo_exchange_kernel(shape, c_ref, h_ref, hrecv, hsend, hget, f_ref):
    routes = halo_routes(*shape)
    fill_faces(c_ref, f_ref, *shape)
    barrier = pltpu.get_barrier_semaphore()
    for _, _, target in routes:
        pl.semaphore_signal(barrier, inc=1, device_id=target, device_id_type=MESH)
    pl.semaphore_wait(barrier, len(routes))
    halo = []
    for k, (row, rows, target) in enumerate(routes):
        copy = pltpu.make_async_remote_copy(
            src_ref=f_ref.at[pl.ds(row, rows)], dst_ref=hrecv.at[pl.ds(row, rows)],
            send_sem=hsend.at[k], recv_sem=hget.at[k], device_id=target, device_id_type=MESH)
        copy.start()
        halo.append(copy)
    for copy in halo:
        copy.wait()
    write_halo(h_ref, hrecv, *shape)


def halo_exchange(cells):
    width, depth, lanes = cells.shape
    rows = 2 * depth + 2 * width + 2
    return pl.pallas_call(
        functools.partial(halo_exchange_kernel, (depth, width)),
        out_shape=jax.ShapeDtypeStruct((rows, lanes), cells.dtype),
        in_specs=[pl.BlockSpec(memory_space=pltpu.VMEM)],
        out_specs=pl.BlockSpec(memory_space=pltpu.VMEM),
        scratch_shapes=[
            pltpu.VMEM((rows, lanes), cells.dtype),
            pltpu.SemaphoreType.DMA((6,)),
            pltpu.SemaphoreType.DMA((6,)),
            pltpu.VMEM((rows, lanes), cells.dtype),
        ],
        compiler_params=pltpu.CompilerParams(collective_id=4, has_side_effects=True),
    )(cells)


def faces_of(cells):
    return jnp.concatenate(
        [cells[-1], cells[0], cells[:, -1], cells[:, 0], cells[-1, :1], cells[0, -1:]], axis=0)


def padded_from(cells, halo):
    depth, width = cells.shape[1], cells.shape[0]
    low_z = halo[:depth][None]
    high_z = halo[depth:2 * depth][None]
    low_x = halo[2 * depth:2 * depth + width][:, None]
    high_x = halo[2 * depth + width:2 * depth + 2 * width][:, None]
    corner = 2 * depth + 2 * width
    low_z_high_x = halo[corner:corner + 1][None]
    high_z_low_x = halo[corner + 1:corner + 2][None]
    zero_line = jnp.zeros_like(cells[:1, :1])
    top = jnp.concatenate([zero_line, low_z, low_z_high_x], axis=1)
    middle = jnp.concatenate([low_x, cells, high_x], axis=1)
    bottom = jnp.concatenate([high_z_low_x, high_z, zero_line], axis=1)
    return jnp.concatenate([top, middle, bottom], axis=0)


def scalar_stages(n_gz, n_gx):
    if n_gx % 4 == 0 and n_gx > 4:
        return [[("gz", 1, n_gz), ("gx", 1, 4)], [("gx", 4, n_gx // 4)]]
    return [[("gz", 1, n_gz)], [("gx", 1, n_gx)]]


def pack_pair(a, b):
    lane = lax.broadcasted_iota(jnp.int32, (8, 128), 1)
    return jnp.where(lane == 0, a, jnp.where(lane == 1, b, 0.0)).astype(jnp.float32)


def one_hot(index, size):
    return (index[:, None] == jnp.arange(size, dtype=jnp.int32)[None, :]).astype(jnp.bfloat16)


def block_apply_kernel(group, transposed, x_ref, blk_ref, w_ref, o_ref):
    o_ref[...] = jnp.zeros_like(o_ref)
    x = x_ref[...]
    chosen = blk_ref[...]
    zero = jnp.zeros_like(x)
    dims = (((1,), (1,)), ((), ())) if transposed else (((1,), (0,)), ((), ()))

    def step(p, carry):
        parts = [jnp.where(chosen == p * group + i, x, zero) for i in range(group)]
        joined = jnp.concatenate(parts, axis=1)
        weights = jnp.concatenate(
            [w_ref[p * group + i] for i in range(group)], axis=1 if transposed else 0)
        o_ref[...] += lax.dot_general(joined, weights, dims, preferred_element_type=jnp.float32)
        return carry

    lax.fori_loop(0, w_ref.shape[0] // group, step, 0)


def block_apply(x, chosen, weights, group, transposed):
    entries, width = x.shape
    flops = 2 * entries * width * width * weights.shape[0]
    return pl.pallas_call(
        functools.partial(block_apply_kernel, group, transposed),
        out_shape=jax.ShapeDtypeStruct((entries, width), jnp.float32),
        in_specs=[pl.BlockSpec(memory_space=pltpu.VMEM)] * 3,
        out_specs=pl.BlockSpec(memory_space=pltpu.VMEM),
        cost_estimate=pl.CostEstimate(
            flops=flops, transcendentals=0, bytes_accessed=weights.size * 2 + entries * width * 10),
    )(x, chosen, weights)


def shift_from(block, pairs_of):
    count_z, count_x = lax.axis_size("gz"), lax.axis_size("gx")
    pairs = []
    for z in range(count_z):
        for x in range(count_x):
            target = pairs_of(z, x)
            if 0 <= target[0] < count_z and 0 <= target[1] < count_x:
                pairs.append((z * count_x + x, target[0] * count_x + target[1]))
    return lax.ppermute(block, ("gz", "gx"), pairs)


def padded_2(cells):
    zero_line = jnp.zeros_like(cells[:1, :1])
    low_z = shift_from(cells[-1:], lambda z, x: (z + 1, x))
    high_z = shift_from(cells[:1], lambda z, x: (z - 1, x))
    low_x = shift_from(cells[:, -1:], lambda z, x: (z, x + 1))
    high_x = shift_from(cells[:, :1], lambda z, x: (z, x - 1))
    low_z_high_x = shift_from(cells[-1:, :1], lambda z, x: (z + 1, x - 1))
    high_z_low_x = shift_from(cells[:1, -1:], lambda z, x: (z - 1, x + 1))
    top = jnp.concatenate([zero_line, low_z, low_z_high_x], axis=1)
    middle = jnp.concatenate([low_x, cells, high_x], axis=1)
    bottom = jnp.concatenate([high_z_low_x, high_z, zero_line], axis=1)
    return jnp.concatenate([top, middle, bottom], axis=0)


def tv_grad(padded):
    base_cells = padded[:-1, :-1, :-1]
    diff_z = padded[1:, :-1, :-1] - base_cells
    diff_x = padded[:-1, 1:, :-1] - base_cells
    diff_y = padded[:-1, :-1, 1:] - base_cells
    inverse = lax.rsqrt(diff_z * diff_z + diff_x * diff_x + diff_y * diff_y + smooth_floor)
    flow_z = diff_z * inverse
    flow_x = diff_x * inverse
    flow_y = diff_y * inverse
    flow_all = flow_z + flow_x + flow_y
    return flow_z[:-1, 1:, 1:] + flow_x[1:, :-1, 1:] + flow_y[1:, 1:, :-1] - flow_all[1:, 1:, 1:]


def pad_depth(field):
    return jnp.pad(field, ((0, 0), (0, 0), (1, 1)))


def body(
    volume, measured, weight_blocks, view_order, tile_voxel, tile_column, tile_block, entry_count
):
    depth_z, depth_x, depth_y = volume.shape
    tiles_y = depth_y // group_rows
    tiles_u = measured.shape[2] // group_rows
    slab_tiles = depth_z * tiles_u
    plane_tiles = depth_x * tiles_y
    row_weight = jnp.sum(weight_blocks, axis=2, dtype=jnp.float32)
    col_weight = jnp.sum(weight_blocks, axis=1, dtype=jnp.float32)
    n_blocks = weight_blocks.shape[0]
    group = 8 if n_blocks % 8 == 0 else 1
    current = volume
    for turn_index in range(view_order.shape[0]):
        view_index = view_order[turn_index]
        voxel_list = lax.dynamic_index_in_dim(tile_voxel, view_index, 0, keepdims=False)[0]
        column_list = lax.dynamic_index_in_dim(tile_column, view_index, 0, keepdims=False)[0]
        block_list = lax.dynamic_index_in_dim(tile_block, view_index, 0, keepdims=False)[0]
        live_count = lax.dynamic_index_in_dim(entry_count, view_index, 0, keepdims=False)[0, 0]
        entries = voxel_list.shape[0]
        live = (jnp.arange(entries, dtype=jnp.int32) < live_count)[:, None]
        detector = voxel_list // plane_tiles * tiles_u + column_list
        voxel_tiles = current.astype(jnp.bfloat16).reshape(-1, group_rows)
        pick_voxel = one_hot(voxel_list, voxel_tiles.shape[0])
        pick_detector = one_hot(detector, slab_tiles)
        pick_block = jnp.where(live, one_hot(block_list, n_blocks), 0)
        blocks_column = block_list[:, None]

        cells = jnp.dot(pick_voxel, voxel_tiles, preferred_element_type=jnp.float32)
        product = block_apply(cells.astype(jnp.bfloat16), blocks_column, weight_blocks, group, True)
        product = jnp.where(live, product, 0.0)
        projection = lax.dot_general(
            pick_detector.astype(jnp.float32), product, (((0,), (0,)), ((), ())),
            precision=lax.Precision.HIGHEST)
        detector_blocks = lax.dot_general(
            pick_detector, pick_block, (((0,), (0,)), ((), ())), preferred_element_type=jnp.float32)
        ray_sum = jnp.dot(detector_blocks, row_weight, precision=lax.Precision.HIGHEST)
        target = lax.dynamic_index_in_dim(measured, view_index, 0, keepdims=False).reshape(
            slab_tiles, group_rows
        )
        n_gx = lax.axis_size("gx")
        joined = jnp.concatenate([projection, ray_sum], axis=1).astype(jnp.bfloat16)
        joined = vector_sum(joined.reshape(n_gx, slab_tiles // n_gx, 2 * group_rows))
        joined = joined.reshape(slab_tiles, 2 * group_rows).astype(jnp.float32)
        projection, ray_sum = joined[:, :group_rows], joined[:, group_rows:]
        residual = ((target - projection) / (ray_sum + 1.0)).astype(jnp.bfloat16)

        pixels = jnp.dot(pick_detector, residual, preferred_element_type=jnp.float32)
        product = block_apply(pixels.astype(jnp.bfloat16), blocks_column, weight_blocks, group, False)
        product = jnp.where(live, product, 0.0)
        change = lax.dot_general(
            pick_voxel.astype(jnp.float32), product, (((0,), (0,)), ((), ())),
            precision=lax.Precision.HIGHEST)
        voxel_blocks = lax.dot_general(
            pick_voxel, pick_block, (((0,), (0,)), ((), ())), preferred_element_type=jnp.float32)
        voxel_sum = jnp.dot(voxel_blocks, col_weight, precision=lax.Precision.HIGHEST)
        current = current + (change / (voxel_sum + 1.0)).reshape(current.shape)
    art_volume = jnp.maximum(current, 0.0)
    difference = art_volume - volume
    change_part = jnp.sum(difference * difference)
    stages = scalar_stages(lax.axis_size("gz"), lax.axis_size("gx"))
    padded = padded_from(art_volume, halo_exchange(art_volume))
    change_total = None
    smooth = art_volume
    for sweep_index in range(TV_STEPS):
        slope = tv_grad(pad_depth(padded))
        extra = pack_pair(0.0, change_part) if sweep_index == 0 else jnp.zeros((8, 128), jnp.float32)
        totals, halo = tv_exchange(extra, slope, stages)
        if sweep_index == 0:
            change_total = totals[0, 1]
        slope_total = totals[0, 0]
        scale_now = step_gain * jnp.sqrt(change_total) / jnp.sqrt(slope_total + norm_floor)
        smooth = smooth - scale_now * slope
        if sweep_index + 1 < TV_STEPS:
            padded = padded - scale_now * padded_from(slope, halo)
    return smooth


def solution(mesh):
    return jax.shard_map(
        body,
        mesh=mesh,
        in_specs=(
            P("gz", "gx", None),
            P(None, "gz", None),
            P(),
            P(),
            P(None, "gz", "gx"),
            P(None, "gz", "gx"),
            P(None, "gz", "gx"),
            P(None, "gz", "gx"),
        ),
        out_specs=P("gz", "gx", None),
        check_vma=False,
    )
```

```python
import functools
import math

import jax
import jax.numpy as jnp
from jax import lax
from jax.experimental import pallas as pl
from jax.experimental.pallas import tpu as pltpu
from jax.sharding import PartitionSpec as P

TV_STEPS = 4


smooth_floor = 0.01
step_gain = 0.25
norm_floor = 1e-06
group_rows = 128


MESH = pl.DeviceIdType.MESH


def _peer(axis, position):
    if axis == "gz":
        return (position, lax.axis_index("gx"))
    return (lax.axis_index("gz"), position)


def vector_sum_kernel(n, x_ref, o_ref, recv, red, gath, ssem1, rsem1, ssem2, rsem2):
    me = lax.axis_index("gx")
    barrier = pltpu.get_barrier_semaphore()
    for d in range(1, n):
        pl.semaphore_signal(barrier, inc=1, device_id=_peer("gx", lax.rem(me + d, n)), device_id_type=MESH)
    pl.semaphore_wait(barrier, n - 1)

    def scatter_copy(d):
        dst = lax.rem(me + d, n)
        return pltpu.make_async_remote_copy(
            src_ref=x_ref.at[dst], dst_ref=recv.at[d], send_sem=ssem1.at[d], recv_sem=rsem1.at[d],
            device_id=_peer("gx", dst), device_id_type=MESH)

    def gather_copy(d):
        dst = lax.rem(me + d, n)
        return pltpu.make_async_remote_copy(
            src_ref=red, dst_ref=gath.at[me], send_sem=ssem2.at[d], recv_sem=rsem2.at[d],
            device_id=_peer("gx", dst), device_id_type=MESH)

    @pl.loop(1, n)
    def _(d):
        scatter_copy(d).start()

    @pl.loop(1, n)
    def _(d):
        scatter_copy(d).wait()

    total = lax.fori_loop(
        1, n, lambda d, acc: acc + recv[d].astype(jnp.float32), x_ref[me].astype(jnp.float32))
    red[...] = total.astype(red.dtype)

    @pl.loop(1, n)
    def _(d):
        gather_copy(d).start()

    @pl.loop(1, n)
    def _(d):
        gather_copy(d).wait()

    gath[me] = red[...]
    o_ref[...] = gath[...]


def vector_sum(x):
    n, rows, cols = x.shape
    return pl.pallas_call(
        functools.partial(vector_sum_kernel, n),
        out_shape=jax.ShapeDtypeStruct(x.shape, x.dtype),
        in_specs=[pl.BlockSpec(memory_space=pltpu.VMEM)],
        out_specs=pl.BlockSpec(memory_space=pltpu.VMEM),
        scratch_shapes=[
            pltpu.VMEM(x.shape, x.dtype),
            pltpu.VMEM((rows, cols), x.dtype),
            pltpu.VMEM(x.shape, x.dtype),
            pltpu.SemaphoreType.DMA((n,)),
            pltpu.SemaphoreType.DMA((n,)),
            pltpu.SemaphoreType.DMA((n,)),
            pltpu.SemaphoreType.DMA((n,)),
        ],
        compiler_params=pltpu.CompilerParams(collective_id=1, has_side_effects=True),
    )(x)


def _stage_peers(stage):
    if isinstance(stage[0], str):
        stage = [stage]
    index = {axis: lax.axis_index(axis) for axis, _, _ in stage}
    digits = [lax.rem(index[axis] // stride, size) for axis, stride, size in stage]
    total = 1
    position = 0
    for (_, _, size), digit in zip(stage, digits):
        position = position * size + digit
        total *= size
    peers = []
    for d in range(1, total):
        q = lax.rem(position + d, total)
        coords = dict(index)
        rest = total
        for (axis, stride, size), digit in zip(stage, digits):
            rest //= size
            coords[axis] = coords[axis] + (lax.rem(q // rest, size) - digit) * stride
        peers.append((coords.get("gz", lax.axis_index("gz")), coords.get("gx", lax.axis_index("gx"))))
    return position, total, peers


def fill_faces(c_ref, faces, depth, width):
    faces[pl.ds(0, depth)] = c_ref[width - 1]
    faces[pl.ds(depth, depth)] = c_ref[0]
    faces[pl.ds(2 * depth, width)] = c_ref[:, depth - 1, :]
    faces[pl.ds(2 * depth + width, width)] = c_ref[:, 0, :]
    faces[pl.ds(2 * depth + 2 * width, 1)] = c_ref[width - 1, pl.ds(0, 1), :]
    faces[pl.ds(2 * depth + 2 * width + 1, 1)] = c_ref[0, pl.ds(depth - 1, 1), :]


def write_halo(h_ref, hrecv, depth, width):
    count_z, count_x = lax.axis_size("gz"), lax.axis_size("gx")
    z, x = lax.axis_index("gz"), lax.axis_index("gx")
    corner = 2 * depth + 2 * width
    parts = [
        (0, depth, z > 0),
        (depth, depth, z < count_z - 1),
        (2 * depth, width, x > 0),
        (2 * depth + width, width, x < count_x - 1),
        (corner, 1, (z > 0) & (x < count_x - 1)),
        (corner + 1, 1, (z < count_z - 1) & (x > 0)),
    ]
    for row, rows, keep in parts:
        values = hrecv[pl.ds(row, rows)]
        h_ref[pl.ds(row, rows)] = jnp.where(keep, values, jnp.zeros_like(values))


def halo_routes(depth, width):
    count_z, count_x = lax.axis_size("gz"), lax.axis_size("gx")
    z, x = lax.axis_index("gz"), lax.axis_index("gx")
    up_z, down_z = lax.rem(z + 1, count_z), lax.rem(z + count_z - 1, count_z)
    up_x, down_x = lax.rem(x + 1, count_x), lax.rem(x + count_x - 1, count_x)
    return [
        (0, depth, (up_z, x)),
        (depth, depth, (down_z, x)),
        (2 * depth, width, (z, up_x)),
        (2 * depth + width, width, (z, down_x)),
        (2 * depth + 2 * width, 1, (up_z, down_x)),
        (2 * depth + 2 * width + 1, 1, (down_z, up_x)),
    ]


def tv_exchange_kernel(stages, shape, x_ref, c_ref, o_ref, h_ref, buf, recv, ssem, rsem, hrecv, hsend, hget, f_ref):
    routes = halo_routes(*shape)
    fill_faces(c_ref, f_ref, *shape)
    plan = [_stage_peers(stage) for stage in stages]
    barrier = pltpu.get_barrier_semaphore()
    count = 0
    for _, _, peers in plan:
        for peer in peers:
            pl.semaphore_signal(barrier, inc=1, device_id=peer, device_id_type=MESH)
            count += 1
    for _, _, target in routes:
        pl.semaphore_signal(barrier, inc=1, device_id=target, device_id_type=MESH)
        count += 1
    pl.semaphore_wait(barrier, count)
    halo = []
    for k, (row, rows, target) in enumerate(routes):
        copy = pltpu.make_async_remote_copy(
            src_ref=f_ref.at[pl.ds(row, rows)], dst_ref=hrecv.at[pl.ds(row, rows)],
            send_sem=hsend.at[k], recv_sem=hget.at[k], device_id=target, device_id_type=MESH)
        copy.start()
        halo.append(copy)
    cells = c_ref[...]
    square = jnp.sum(jnp.sum(cells * cells, axis=0), axis=0, keepdims=True)
    square = jnp.sum(square, axis=1, keepdims=True)
    row = lax.broadcasted_iota(jnp.int32, x_ref.shape, 0)
    lane = lax.broadcasted_iota(jnp.int32, x_ref.shape, 1)
    total = x_ref[...] + jnp.where((row == 0) & (lane == 0), square, 0.0)
    buf[0] = total
    slot = 0
    for s, (position, size, peers) in enumerate(plan):
        source = buf.at[s]
        recv[slot] = total
        sends = []
        for d, peer in enumerate(peers, start=1):
            copy = pltpu.make_async_remote_copy(
                src_ref=source, dst_ref=recv.at[slot + d], send_sem=ssem.at[slot + d],
                recv_sem=rsem.at[slot + d], device_id=peer, device_id_type=MESH)
            copy.start()
            sends.append(copy)
        for copy in sends:
            copy.wait()
        total = recv[slot + position]
        for p in range(1, size):
            total = total + recv[slot + lax.rem(position - p + size, size)]
        slot += size
        if s + 1 < len(plan):
            buf[s + 1] = total
    o_ref[...] = total
    for copy in halo:
        copy.wait()
    write_halo(h_ref, hrecv, *shape)


def tv_exchange(x, cells, stages):
    width, depth, lanes = cells.shape
    rows = 2 * depth + 2 * width + 2
    slots = sum(math.prod(size for _, _, size in stage) for stage in stages)
    return pl.pallas_call(
        functools.partial(tv_exchange_kernel, stages, (depth, width)),
        out_shape=(jax.ShapeDtypeStruct(x.shape, x.dtype), jax.ShapeDtypeStruct((rows, lanes), cells.dtype)),
        in_specs=[pl.BlockSpec(memory_space=pltpu.VMEM)] * 2,
        out_specs=(pl.BlockSpec(memory_space=pltpu.VMEM), pl.BlockSpec(memory_space=pltpu.VMEM)),
        scratch_shapes=[
            pltpu.VMEM((len(stages),) + x.shape, x.dtype),
            pltpu.VMEM((slots,) + x.shape, x.dtype),
            pltpu.SemaphoreType.DMA((slots,)),
            pltpu.SemaphoreType.DMA((slots,)),
            pltpu.VMEM((rows, lanes), cells.dtype),
            pltpu.SemaphoreType.DMA((6,)),
            pltpu.SemaphoreType.DMA((6,)),
            pltpu.VMEM((rows, lanes), cells.dtype),
        ],
        compiler_params=pltpu.CompilerParams(collective_id=3, has_side_effects=True),
    )(x, cells)


def halo_exchange_kernel(shape, c_ref, h_ref, hrecv, hsend, hget, f_ref):
    routes = halo_routes(*shape)
    fill_faces(c_ref, f_ref, *shape)
    barrier = pltpu.get_barrier_semaphore()
    for _, _, target in routes:
        pl.semaphore_signal(barrier, inc=1, device_id=target, device_id_type=MESH)
    pl.semaphore_wait(barrier, len(routes))
    halo = []
    for k, (row, rows, target) in enumerate(routes):
        copy = pltpu.make_async_remote_copy(
            src_ref=f_ref.at[pl.ds(row, rows)], dst_ref=hrecv.at[pl.ds(row, rows)],
            send_sem=hsend.at[k], recv_sem=hget.at[k], device_id=target, device_id_type=MESH)
        copy.start()
        halo.append(copy)
    for copy in halo:
        copy.wait()
    write_halo(h_ref, hrecv, *shape)


def halo_exchange(cells):
    width, depth, lanes = cells.shape
    rows = 2 * depth + 2 * width + 2
    return pl.pallas_call(
        functools.partial(halo_exchange_kernel, (depth, width)),
        out_shape=jax.ShapeDtypeStruct((rows, lanes), cells.dtype),
        in_specs=[pl.BlockSpec(memory_space=pltpu.VMEM)],
        out_specs=pl.BlockSpec(memory_space=pltpu.VMEM),
        scratch_shapes=[
            pltpu.VMEM((rows, lanes), cells.dtype),
            pltpu.SemaphoreType.DMA((6,)),
            pltpu.SemaphoreType.DMA((6,)),
            pltpu.VMEM((rows, lanes), cells.dtype),
        ],
        compiler_params=pltpu.CompilerParams(collective_id=4, has_side_effects=True),
    )(cells)


def faces_of(cells):
    return jnp.concatenate(
        [cells[-1], cells[0], cells[:, -1], cells[:, 0], cells[-1, :1], cells[0, -1:]], axis=0)


def padded_from(cells, halo):
    depth, width = cells.shape[1], cells.shape[0]
    low_z = halo[:depth][None]
    high_z = halo[depth:2 * depth][None]
    low_x = halo[2 * depth:2 * depth + width][:, None]
    high_x = halo[2 * depth + width:2 * depth + 2 * width][:, None]
    corner = 2 * depth + 2 * width
    low_z_high_x = halo[corner:corner + 1][None]
    high_z_low_x = halo[corner + 1:corner + 2][None]
    zero_line = jnp.zeros_like(cells[:1, :1])
    top = jnp.concatenate([zero_line, low_z, low_z_high_x], axis=1)
    middle = jnp.concatenate([low_x, cells, high_x], axis=1)
    bottom = jnp.concatenate([high_z_low_x, high_z, zero_line], axis=1)
    return jnp.concatenate([top, middle, bottom], axis=0)


def scalar_stages(n_gz, n_gx):
    if n_gx % 4 == 0 and n_gx > 4:
        return [[("gz", 1, n_gz), ("gx", 1, 4)], [("gx", 4, n_gx // 4)]]
    return [[("gz", 1, n_gz)], [("gx", 1, n_gx)]]


def pack_pair(a, b):
    lane = lax.broadcasted_iota(jnp.int32, (8, 128), 1)
    return jnp.where(lane == 0, a, jnp.where(lane == 1, b, 0.0)).astype(jnp.float32)


def one_hot(index, size):
    return (index[:, None] == jnp.arange(size, dtype=jnp.int32)[None, :]).astype(jnp.bfloat16)


def block_apply_kernel(group, transposed, x_ref, blk_ref, w_ref, o_ref):
    o_ref[...] = jnp.zeros_like(o_ref)
    x = x_ref[...]
    chosen = blk_ref[...]
    zero = jnp.zeros_like(x)
    dims = (((1,), (1,)), ((), ())) if transposed else (((1,), (0,)), ((), ()))

    def step(p, carry):
        parts = [jnp.where(chosen == p * group + i, x, zero) for i in range(group)]
        joined = jnp.concatenate(parts, axis=1)
        weights = jnp.concatenate(
            [w_ref[p * group + i] for i in range(group)], axis=1 if transposed else 0)
        o_ref[...] += lax.dot_general(joined, weights, dims, preferred_element_type=jnp.float32)
        return carry

    lax.fori_loop(0, w_ref.shape[0] // group, step, 0)


def block_apply(x, chosen, weights, group, transposed):
    entries, width = x.shape
    flops = 2 * entries * width * width * weights.shape[0]
    return pl.pallas_call(
        functools.partial(block_apply_kernel, group, transposed),
        out_shape=jax.ShapeDtypeStruct((entries, width), jnp.float32),
        in_specs=[pl.BlockSpec(memory_space=pltpu.VMEM)] * 3,
        out_specs=pl.BlockSpec(memory_space=pltpu.VMEM),
        cost_estimate=pl.CostEstimate(
            flops=flops, transcendentals=0, bytes_accessed=weights.size * 2 + entries * width * 10),
    )(x, chosen, weights)


def shift_from(block, pairs_of):
    count_z, count_x = lax.axis_size("gz"), lax.axis_size("gx")
    pairs = []
    for z in range(count_z):
        for x in range(count_x):
            target = pairs_of(z, x)
            if 0 <= target[0] < count_z and 0 <= target[1] < count_x:
                pairs.append((z * count_x + x, target[0] * count_x + target[1]))
    return lax.ppermute(block, ("gz", "gx"), pairs)


def padded_2(cells):
    zero_line = jnp.zeros_like(cells[:1, :1])
    low_z = shift_from(cells[-1:], lambda z, x: (z + 1, x))
    high_z = shift_from(cells[:1], lambda z, x: (z - 1, x))
    low_x = shift_from(cells[:, -1:], lambda z, x: (z, x + 1))
    high_x = shift_from(cells[:, :1], lambda z, x: (z, x - 1))
    low_z_high_x = shift_from(cells[-1:, :1], lambda z, x: (z + 1, x - 1))
    high_z_low_x = shift_from(cells[:1, -1:], lambda z, x: (z - 1, x + 1))
    top = jnp.concatenate([zero_line, low_z, low_z_high_x], axis=1)
    middle = jnp.concatenate([low_x, cells, high_x], axis=1)
    bottom = jnp.concatenate([high_z_low_x, high_z, zero_line], axis=1)
    return jnp.concatenate([top, middle, bottom], axis=0)


def tv_grad(padded):
    base_cells = padded[:-1, :-1, :-1]
    diff_z = padded[1:, :-1, :-1] - base_cells
    diff_x = padded[:-1, 1:, :-1] - base_cells
    diff_y = padded[:-1, :-1, 1:] - base_cells
    inverse = lax.rsqrt(diff_z * diff_z + diff_x * diff_x + diff_y * diff_y + smooth_floor)
    flow_z = diff_z * inverse
    flow_x = diff_x * inverse
    flow_y = diff_y * inverse
    flow_all = flow_z + flow_x + flow_y
    return flow_z[:-1, 1:, 1:] + flow_x[1:, :-1, 1:] + flow_y[1:, 1:, :-1] - flow_all[1:, 1:, 1:]


def pad_depth(field):
    return jnp.pad(field, ((0, 0), (0, 0), (1, 1)))


def body(
    volume, measured, weight_blocks, view_order, tile_voxel, tile_column, tile_block, entry_count
):
    depth_z, depth_x, depth_y = volume.shape
    tiles_y = depth_y // group_rows
    tiles_u = measured.shape[2] // group_rows
    slab_tiles = depth_z * tiles_u
    plane_tiles = depth_x * tiles_y
    row_weight = jnp.sum(weight_blocks, axis=2, dtype=jnp.float32)
    col_weight = jnp.sum(weight_blocks, axis=1, dtype=jnp.float32)
    n_blocks = weight_blocks.shape[0]
    group = 8 if n_blocks % 8 == 0 else 1
    current = volume
    for turn_index in range(view_order.shape[0]):
        view_index = view_order[turn_index]
        voxel_list = lax.dynamic_index_in_dim(tile_voxel, view_index, 0, keepdims=False)[0]
        column_list = lax.dynamic_index_in_dim(tile_column, view_index, 0, keepdims=False)[0]
        block_list = lax.dynamic_index_in_dim(tile_block, view_index, 0, keepdims=False)[0]
        live_count = lax.dynamic_index_in_dim(entry_count, view_index, 0, keepdims=False)[0, 0]
        entries = voxel_list.shape[0]
        live = (jnp.arange(entries, dtype=jnp.int32) < live_count)[:, None]
        detector = voxel_list // plane_tiles * tiles_u + column_list
        voxel_tiles = current.astype(jnp.bfloat16).reshape(-1, group_rows)
        pick_voxel = one_hot(voxel_list, voxel_tiles.shape[0])
        pick_detector = one_hot(detector, slab_tiles)
        pick_block = jnp.where(live, one_hot(block_list, n_blocks), 0)
        blocks_column = block_list[:, None]

        cells = jnp.dot(pick_voxel, voxel_tiles, preferred_element_type=jnp.float32)
        product = block_apply(cells.astype(jnp.bfloat16), blocks_column, weight_blocks, group, True)
        product = jnp.where(live, product, 0.0)
        projection = lax.dot_general(
            pick_detector.astype(jnp.float32), product, (((0,), (0,)), ((), ())),
            precision=lax.Precision.HIGHEST)
        detector_blocks = lax.dot_general(
            pick_detector, pick_block, (((0,), (0,)), ((), ())), preferred_element_type=jnp.float32)
        ray_sum = jnp.dot(detector_blocks, row_weight, precision=lax.Precision.HIGHEST)
        target = lax.dynamic_index_in_dim(measured, view_index, 0, keepdims=False).reshape(
            slab_tiles, group_rows
        )
        n_gx = lax.axis_size("gx")
        joined = jnp.concatenate([projection, ray_sum], axis=1).astype(jnp.bfloat16)
        joined = vector_sum(joined.reshape(n_gx, slab_tiles // n_gx, 2 * group_rows))
        joined = joined.reshape(slab_tiles, 2 * group_rows).astype(jnp.float32)
        projection, ray_sum = joined[:, :group_rows], joined[:, group_rows:]
        residual = ((target - projection) / (ray_sum + 1.0)).astype(jnp.bfloat16)

        pixels = jnp.dot(pick_detector, residual, preferred_element_type=jnp.float32)
        product = block_apply(pixels.astype(jnp.bfloat16), blocks_column, weight_blocks, group, False)
        product = jnp.where(live, product, 0.0)
        change = lax.dot_general(
            pick_voxel.astype(jnp.float32), product, (((0,), (0,)), ((), ())),
            precision=lax.Precision.HIGHEST)
        voxel_blocks = lax.dot_general(
            pick_voxel, pick_block, (((0,), (0,)), ((), ())), preferred_element_type=jnp.float32)
        voxel_sum = jnp.dot(voxel_blocks, col_weight, precision=lax.Precision.HIGHEST)
        current = current + (change / (voxel_sum + 1.0)).reshape(current.shape)
    art_volume = jnp.maximum(current, 0.0)
    difference = art_volume - volume
    change_part = jnp.sum(difference * difference)
    stages = scalar_stages(lax.axis_size("gz"), lax.axis_size("gx"))
    padded = padded_from(art_volume, halo_exchange(art_volume))
    change_total = None
    smooth = art_volume
    for sweep_index in range(TV_STEPS):
        slope = tv_grad(pad_depth(padded))
        extra = pack_pair(0.0, change_part) if sweep_index == 0 else jnp.zeros((8, 128), jnp.float32)
        totals, halo = tv_exchange(extra, slope, stages)
        if sweep_index == 0:
            change_total = totals[0, 1]
        slope_total = totals[0, 0]
        scale_now = step_gain * jnp.sqrt(change_total) / jnp.sqrt(slope_total + norm_floor)
        if sweep_index + 1 < TV_STEPS:
            padded = padded - scale_now * padded_from(slope, halo)
        else:
            smooth = padded[1:-1, 1:-1] - scale_now * slope
    return smooth


def solution(mesh):
    return jax.shard_map(
        body,
        mesh=mesh,
        in_specs=(
            P("gz", "gx", None),
            P(None, "gz", None),
            P(),
            P(),
            P(None, "gz", "gx"),
            P(None, "gz", "gx"),
            P(None, "gz", "gx"),
            P(None, "gz", "gx"),
        ),
        out_specs=P("gz", "gx", None),
        check_vma=False,
    )
```

```python
import functools
import math

import jax
import jax.numpy as jnp
from jax import lax
from jax.experimental import pallas as pl
from jax.experimental.pallas import tpu as pltpu
from jax.sharding import PartitionSpec as P

TV_STEPS = 4


smooth_floor = 0.01
step_gain = 0.25
norm_floor = 1e-06
group_rows = 128


MESH = pl.DeviceIdType.MESH


def _peer(axis, position):
    if axis == "gz":
        return (position, lax.axis_index("gx"))
    return (lax.axis_index("gz"), position)


def vector_sum_kernel(n, x_ref, o_ref, recv, red, gath, ssem1, rsem1, ssem2, rsem2):
    me = lax.axis_index("gx")
    barrier = pltpu.get_barrier_semaphore()
    for d in range(1, n):
        pl.semaphore_signal(barrier, inc=1, device_id=_peer("gx", lax.rem(me + d, n)), device_id_type=MESH)
    pl.semaphore_wait(barrier, n - 1)

    def scatter_copy(d):
        dst = lax.rem(me + d, n)
        return pltpu.make_async_remote_copy(
            src_ref=x_ref.at[dst], dst_ref=recv.at[d], send_sem=ssem1.at[d], recv_sem=rsem1.at[d],
            device_id=_peer("gx", dst), device_id_type=MESH)

    def gather_copy(d):
        dst = lax.rem(me + d, n)
        return pltpu.make_async_remote_copy(
            src_ref=red, dst_ref=gath.at[me], send_sem=ssem2.at[d], recv_sem=rsem2.at[d],
            device_id=_peer("gx", dst), device_id_type=MESH)

    @pl.loop(1, n)
    def _(d):
        scatter_copy(d).start()

    @pl.loop(1, n)
    def _(d):
        scatter_copy(d).wait()

    total = lax.fori_loop(
        1, n, lambda d, acc: acc + recv[d].astype(jnp.float32), x_ref[me].astype(jnp.float32))
    red[...] = total.astype(red.dtype)

    @pl.loop(1, n)
    def _(d):
        gather_copy(d).start()

    @pl.loop(1, n)
    def _(d):
        gather_copy(d).wait()

    gath[me] = red[...]
    o_ref[...] = gath[...]


def vector_sum(x):
    n, rows, cols = x.shape
    return pl.pallas_call(
        functools.partial(vector_sum_kernel, n),
        out_shape=jax.ShapeDtypeStruct(x.shape, x.dtype),
        in_specs=[pl.BlockSpec(memory_space=pltpu.VMEM)],
        out_specs=pl.BlockSpec(memory_space=pltpu.VMEM),
        scratch_shapes=[
            pltpu.VMEM(x.shape, x.dtype),
            pltpu.VMEM((rows, cols), x.dtype),
            pltpu.VMEM(x.shape, x.dtype),
            pltpu.SemaphoreType.DMA((n,)),
            pltpu.SemaphoreType.DMA((n,)),
            pltpu.SemaphoreType.DMA((n,)),
            pltpu.SemaphoreType.DMA((n,)),
        ],
        compiler_params=pltpu.CompilerParams(collective_id=1, has_side_effects=True),
    )(x)


def _stage_peers(stage):
    if isinstance(stage[0], str):
        stage = [stage]
    index = {axis: lax.axis_index(axis) for axis, _, _ in stage}
    digits = [lax.rem(index[axis] // stride, size) for axis, stride, size in stage]
    total = 1
    position = 0
    for (_, _, size), digit in zip(stage, digits):
        position = position * size + digit
        total *= size
    peers = []
    for d in range(1, total):
        q = lax.rem(position + d, total)
        coords = dict(index)
        rest = total
        for (axis, stride, size), digit in zip(stage, digits):
            rest //= size
            coords[axis] = coords[axis] + (lax.rem(q // rest, size) - digit) * stride
        peers.append((coords.get("gz", lax.axis_index("gz")), coords.get("gx", lax.axis_index("gx"))))
    return position, total, peers


def fill_faces(c_ref, faces, depth, width):
    faces[pl.ds(0, depth)] = c_ref[width - 1]
    faces[pl.ds(depth, depth)] = c_ref[0]
    faces[pl.ds(2 * depth, width)] = c_ref[:, depth - 1, :]
    faces[pl.ds(2 * depth + width, width)] = c_ref[:, 0, :]
    faces[pl.ds(2 * depth + 2 * width, 1)] = c_ref[width - 1, pl.ds(0, 1), :]
    faces[pl.ds(2 * depth + 2 * width + 1, 1)] = c_ref[0, pl.ds(depth - 1, 1), :]


def write_halo(h_ref, hrecv, depth, width):
    count_z, count_x = lax.axis_size("gz"), lax.axis_size("gx")
    z, x = lax.axis_index("gz"), lax.axis_index("gx")
    corner = 2 * depth + 2 * width
    parts = [
        (0, depth, z > 0),
        (depth, depth, z < count_z - 1),
        (2 * depth, width, x > 0),
        (2 * depth + width, width, x < count_x - 1),
        (corner, 1, (z > 0) & (x < count_x - 1)),
        (corner + 1, 1, (z < count_z - 1) & (x > 0)),
    ]
    for row, rows, keep in parts:
        values = hrecv[pl.ds(row, rows)]
        h_ref[pl.ds(row, rows)] = jnp.where(keep, values, jnp.zeros_like(values))


def halo_routes(depth, width):
    count_z, count_x = lax.axis_size("gz"), lax.axis_size("gx")
    z, x = lax.axis_index("gz"), lax.axis_index("gx")
    up_z, down_z = lax.rem(z + 1, count_z), lax.rem(z + count_z - 1, count_z)
    up_x, down_x = lax.rem(x + 1, count_x), lax.rem(x + count_x - 1, count_x)
    return [
        (0, depth, (up_z, x)),
        (depth, depth, (down_z, x)),
        (2 * depth, width, (z, up_x)),
        (2 * depth + width, width, (z, down_x)),
        (2 * depth + 2 * width, 1, (up_z, down_x)),
        (2 * depth + 2 * width + 1, 1, (down_z, up_x)),
    ]


def tv_exchange_kernel(stages, shape, x_ref, c_ref, o_ref, h_ref, buf, recv, ssem, rsem, hrecv, hsend, hget, f_ref):
    routes = halo_routes(*shape)
    fill_faces(c_ref, f_ref, *shape)
    plan = [_stage_peers(stage) for stage in stages]
    barrier = pltpu.get_barrier_semaphore()
    count = 0
    for _, _, peers in plan:
        for peer in peers:
            pl.semaphore_signal(barrier, inc=1, device_id=peer, device_id_type=MESH)
            count += 1
    for _, _, target in routes:
        pl.semaphore_signal(barrier, inc=1, device_id=target, device_id_type=MESH)
        count += 1
    pl.semaphore_wait(barrier, count)
    halo = []
    for k, (row, rows, target) in enumerate(routes):
        copy = pltpu.make_async_remote_copy(
            src_ref=f_ref.at[pl.ds(row, rows)], dst_ref=hrecv.at[pl.ds(row, rows)],
            send_sem=hsend.at[k], recv_sem=hget.at[k], device_id=target, device_id_type=MESH)
        copy.start()
        halo.append(copy)
    cells = c_ref[...]
    square = jnp.sum(jnp.sum(cells * cells, axis=0), axis=0, keepdims=True)
    square = jnp.sum(square, axis=1, keepdims=True)
    row = lax.broadcasted_iota(jnp.int32, x_ref.shape, 0)
    lane = lax.broadcasted_iota(jnp.int32, x_ref.shape, 1)
    total = x_ref[...] + jnp.where((row == 0) & (lane == 0), square, 0.0)
    buf[0] = total
    slot = 0
    for s, (position, size, peers) in enumerate(plan):
        source = buf.at[s]
        recv[slot] = total
        sends = []
        for d, peer in enumerate(peers, start=1):
            copy = pltpu.make_async_remote_copy(
                src_ref=source, dst_ref=recv.at[slot + d], send_sem=ssem.at[slot + d],
                recv_sem=rsem.at[slot + d], device_id=peer, device_id_type=MESH)
            copy.start()
            sends.append(copy)
        for copy in sends:
            copy.wait()
        total = recv[slot + position]
        for p in range(1, size):
            total = total + recv[slot + lax.rem(position - p + size, size)]
        slot += size
        if s + 1 < len(plan):
            buf[s + 1] = total
    o_ref[...] = total
    for copy in halo:
        copy.wait()
    write_halo(h_ref, hrecv, *shape)


def tv_exchange(x, cells, stages):
    width, depth, lanes = cells.shape
    rows = 2 * depth + 2 * width + 2
    slots = sum(math.prod(size for _, _, size in stage) for stage in stages)
    return pl.pallas_call(
        functools.partial(tv_exchange_kernel, stages, (depth, width)),
        out_shape=(jax.ShapeDtypeStruct(x.shape, x.dtype), jax.ShapeDtypeStruct((rows, lanes), cells.dtype)),
        in_specs=[pl.BlockSpec(memory_space=pltpu.VMEM)] * 2,
        out_specs=(pl.BlockSpec(memory_space=pltpu.VMEM), pl.BlockSpec(memory_space=pltpu.VMEM)),
        scratch_shapes=[
            pltpu.VMEM((len(stages),) + x.shape, x.dtype),
            pltpu.VMEM((slots,) + x.shape, x.dtype),
            pltpu.SemaphoreType.DMA((slots,)),
            pltpu.SemaphoreType.DMA((slots,)),
            pltpu.VMEM((rows, lanes), cells.dtype),
            pltpu.SemaphoreType.DMA((6,)),
            pltpu.SemaphoreType.DMA((6,)),
            pltpu.VMEM((rows, lanes), cells.dtype),
        ],
        compiler_params=pltpu.CompilerParams(collective_id=3, has_side_effects=True),
    )(x, cells)


def halo_exchange_kernel(shape, c_ref, h_ref, hrecv, hsend, hget, f_ref):
    routes = halo_routes(*shape)
    fill_faces(c_ref, f_ref, *shape)
    barrier = pltpu.get_barrier_semaphore()
    for _, _, target in routes:
        pl.semaphore_signal(barrier, inc=1, device_id=target, device_id_type=MESH)
    pl.semaphore_wait(barrier, len(routes))
    halo = []
    for k, (row, rows, target) in enumerate(routes):
        copy = pltpu.make_async_remote_copy(
            src_ref=f_ref.at[pl.ds(row, rows)], dst_ref=hrecv.at[pl.ds(row, rows)],
            send_sem=hsend.at[k], recv_sem=hget.at[k], device_id=target, device_id_type=MESH)
        copy.start()
        halo.append(copy)
    for copy in halo:
        copy.wait()
    write_halo(h_ref, hrecv, *shape)


def halo_exchange(cells):
    width, depth, lanes = cells.shape
    rows = 2 * depth + 2 * width + 2
    return pl.pallas_call(
        functools.partial(halo_exchange_kernel, (depth, width)),
        out_shape=jax.ShapeDtypeStruct((rows, lanes), cells.dtype),
        in_specs=[pl.BlockSpec(memory_space=pltpu.VMEM)],
        out_specs=pl.BlockSpec(memory_space=pltpu.VMEM),
        scratch_shapes=[
            pltpu.VMEM((rows, lanes), cells.dtype),
            pltpu.SemaphoreType.DMA((6,)),
            pltpu.SemaphoreType.DMA((6,)),
            pltpu.VMEM((rows, lanes), cells.dtype),
        ],
        compiler_params=pltpu.CompilerParams(collective_id=4, has_side_effects=True),
    )(cells)


def faces_of(cells):
    return jnp.concatenate(
        [cells[-1], cells[0], cells[:, -1], cells[:, 0], cells[-1, :1], cells[0, -1:]], axis=0)


def padded_from(cells, halo):
    depth, width = cells.shape[1], cells.shape[0]
    low_z = halo[:depth][None]
    high_z = halo[depth:2 * depth][None]
    low_x = halo[2 * depth:2 * depth + width][:, None]
    high_x = halo[2 * depth + width:2 * depth + 2 * width][:, None]
    corner = 2 * depth + 2 * width
    low_z_high_x = halo[corner:corner + 1][None]
    high_z_low_x = halo[corner + 1:corner + 2][None]
    zero_line = jnp.zeros_like(cells[:1, :1])
    top = jnp.concatenate([zero_line, low_z, low_z_high_x], axis=1)
    middle = jnp.concatenate([low_x, cells, high_x], axis=1)
    bottom = jnp.concatenate([high_z_low_x, high_z, zero_line], axis=1)
    return jnp.concatenate([top, middle, bottom], axis=0)


def scalar_stages(n_gz, n_gx):
    if n_gx % 4 == 0 and n_gx > 4:
        return [[("gz", 1, n_gz), ("gx", 1, 4)], [("gx", 4, n_gx // 4)]]
    return [[("gz", 1, n_gz)], [("gx", 1, n_gx)]]


def pack_pair(a, b):
    lane = lax.broadcasted_iota(jnp.int32, (8, 128), 1)
    return jnp.where(lane == 0, a, jnp.where(lane == 1, b, 0.0)).astype(jnp.float32)


def one_hot(index, size):
    return (index[:, None] == jnp.arange(size, dtype=jnp.int32)[None, :]).astype(jnp.bfloat16)


def block_apply_kernel(group, transposed, x_ref, blk_ref, w_ref, o_ref):
    o_ref[...] = jnp.zeros_like(o_ref)
    x = x_ref[...]
    chosen = blk_ref[...]
    zero = jnp.zeros_like(x)
    dims = (((1,), (1,)), ((), ())) if transposed else (((1,), (0,)), ((), ()))

    def step(p, carry):
        parts = [jnp.where(chosen == p * group + i, x, zero) for i in range(group)]
        joined = jnp.concatenate(parts, axis=1)
        weights = jnp.concatenate(
            [w_ref[p * group + i] for i in range(group)], axis=1 if transposed else 0)
        o_ref[...] += lax.dot_general(joined, weights, dims, preferred_element_type=jnp.float32)
        return carry

    lax.fori_loop(0, w_ref.shape[0] // group, step, 0, unroll=2)


def block_apply(x, chosen, weights, group, transposed):
    entries, width = x.shape
    flops = 2 * entries * width * width * weights.shape[0]
    return pl.pallas_call(
        functools.partial(block_apply_kernel, group, transposed),
        out_shape=jax.ShapeDtypeStruct((entries, width), jnp.float32),
        in_specs=[pl.BlockSpec(memory_space=pltpu.VMEM)] * 3,
        out_specs=pl.BlockSpec(memory_space=pltpu.VMEM),
        cost_estimate=pl.CostEstimate(
            flops=flops, transcendentals=0, bytes_accessed=weights.size * 2 + entries * width * 10),
    )(x, chosen, weights)


def shift_from(block, pairs_of):
    count_z, count_x = lax.axis_size("gz"), lax.axis_size("gx")
    pairs = []
    for z in range(count_z):
        for x in range(count_x):
            target = pairs_of(z, x)
            if 0 <= target[0] < count_z and 0 <= target[1] < count_x:
                pairs.append((z * count_x + x, target[0] * count_x + target[1]))
    return lax.ppermute(block, ("gz", "gx"), pairs)


def padded_2(cells):
    zero_line = jnp.zeros_like(cells[:1, :1])
    low_z = shift_from(cells[-1:], lambda z, x: (z + 1, x))
    high_z = shift_from(cells[:1], lambda z, x: (z - 1, x))
    low_x = shift_from(cells[:, -1:], lambda z, x: (z, x + 1))
    high_x = shift_from(cells[:, :1], lambda z, x: (z, x - 1))
    low_z_high_x = shift_from(cells[-1:, :1], lambda z, x: (z + 1, x - 1))
    high_z_low_x = shift_from(cells[:1, -1:], lambda z, x: (z - 1, x + 1))
    top = jnp.concatenate([zero_line, low_z, low_z_high_x], axis=1)
    middle = jnp.concatenate([low_x, cells, high_x], axis=1)
    bottom = jnp.concatenate([high_z_low_x, high_z, zero_line], axis=1)
    return jnp.concatenate([top, middle, bottom], axis=0)


def tv_grad(padded):
    base_cells = padded[:-1, :-1, :-1]
    diff_z = padded[1:, :-1, :-1] - base_cells
    diff_x = padded[:-1, 1:, :-1] - base_cells
    diff_y = padded[:-1, :-1, 1:] - base_cells
    inverse = lax.rsqrt(diff_z * diff_z + diff_x * diff_x + diff_y * diff_y + smooth_floor)
    flow_z = diff_z * inverse
    flow_x = diff_x * inverse
    flow_y = diff_y * inverse
    flow_all = flow_z + flow_x + flow_y
    return flow_z[:-1, 1:, 1:] + flow_x[1:, :-1, 1:] + flow_y[1:, 1:, :-1] - flow_all[1:, 1:, 1:]


def pad_depth(field):
    return jnp.pad(field, ((0, 0), (0, 0), (1, 1)))


def body(
    volume, measured, weight_blocks, view_order, tile_voxel, tile_column, tile_block, entry_count
):
    depth_z, depth_x, depth_y = volume.shape
    tiles_y = depth_y // group_rows
    tiles_u = measured.shape[2] // group_rows
    slab_tiles = depth_z * tiles_u
    plane_tiles = depth_x * tiles_y
    row_weight = jnp.sum(weight_blocks, axis=2, dtype=jnp.float32)
    col_weight = jnp.sum(weight_blocks, axis=1, dtype=jnp.float32)
    n_blocks = weight_blocks.shape[0]
    group = 8 if n_blocks % 8 == 0 else 1
    current = volume
    for turn_index in range(view_order.shape[0]):
        view_index = view_order[turn_index]
        voxel_list = lax.dynamic_index_in_dim(tile_voxel, view_index, 0, keepdims=False)[0]
        column_list = lax.dynamic_index_in_dim(tile_column, view_index, 0, keepdims=False)[0]
        block_list = lax.dynamic_index_in_dim(tile_block, view_index, 0, keepdims=False)[0]
        live_count = lax.dynamic_index_in_dim(entry_count, view_index, 0, keepdims=False)[0, 0]
        entries = voxel_list.shape[0]
        live = (jnp.arange(entries, dtype=jnp.int32) < live_count)[:, None]
        detector = voxel_list // plane_tiles * tiles_u + column_list
        voxel_tiles = current.astype(jnp.bfloat16).reshape(-1, group_rows)
        pick_voxel = one_hot(voxel_list, voxel_tiles.shape[0])
        pick_detector = one_hot(detector, slab_tiles)
        pick_block = jnp.where(live, one_hot(block_list, n_blocks), 0)
        blocks_column = block_list[:, None]

        cells = jnp.dot(pick_voxel, voxel_tiles, preferred_element_type=jnp.float32)
        product = block_apply(cells.astype(jnp.bfloat16), blocks_column, weight_blocks, group, True)
        product = jnp.where(live, product, 0.0)
        projection = lax.dot_general(
            pick_detector.astype(jnp.float32), product, (((0,), (0,)), ((), ())),
            precision=lax.Precision.HIGHEST)
        detector_blocks = lax.dot_general(
            pick_detector, pick_block, (((0,), (0,)), ((), ())), preferred_element_type=jnp.float32)
        ray_sum = jnp.dot(detector_blocks, row_weight, precision=lax.Precision.HIGHEST)
        target = lax.dynamic_index_in_dim(measured, view_index, 0, keepdims=False).reshape(
            slab_tiles, group_rows
        )
        n_gx = lax.axis_size("gx")
        joined = jnp.concatenate([projection, ray_sum], axis=1).astype(jnp.bfloat16)
        joined = vector_sum(joined.reshape(n_gx, slab_tiles // n_gx, 2 * group_rows))
        joined = joined.reshape(slab_tiles, 2 * group_rows).astype(jnp.float32)
        projection, ray_sum = joined[:, :group_rows], joined[:, group_rows:]
        residual = ((target - projection) / (ray_sum + 1.0)).astype(jnp.bfloat16)

        pixels = jnp.dot(pick_detector, residual, preferred_element_type=jnp.float32)
        product = block_apply(pixels.astype(jnp.bfloat16), blocks_column, weight_blocks, group, False)
        product = jnp.where(live, product, 0.0)
        change = lax.dot_general(
            pick_voxel.astype(jnp.float32), product, (((0,), (0,)), ((), ())),
            precision=lax.Precision.HIGHEST)
        voxel_blocks = lax.dot_general(
            pick_voxel, pick_block, (((0,), (0,)), ((), ())), preferred_element_type=jnp.float32)
        voxel_sum = jnp.dot(voxel_blocks, col_weight, precision=lax.Precision.HIGHEST)
        current = current + (change / (voxel_sum + 1.0)).reshape(current.shape)
    art_volume = jnp.maximum(current, 0.0)
    difference = art_volume - volume
    change_part = jnp.sum(difference * difference)
    stages = scalar_stages(lax.axis_size("gz"), lax.axis_size("gx"))
    padded = padded_from(art_volume, halo_exchange(art_volume))
    change_total = None
    smooth = art_volume
    for sweep_index in range(TV_STEPS):
        slope = tv_grad(pad_depth(padded))
        extra = pack_pair(0.0, change_part) if sweep_index == 0 else jnp.zeros((8, 128), jnp.float32)
        totals, halo = tv_exchange(extra, slope, stages)
        if sweep_index == 0:
            change_total = totals[0, 1]
        slope_total = totals[0, 0]
        scale_now = step_gain * jnp.sqrt(change_total) / jnp.sqrt(slope_total + norm_floor)
        smooth = smooth - scale_now * slope
        if sweep_index + 1 < TV_STEPS:
            padded = padded - scale_now * padded_from(slope, halo)
    return smooth


def solution(mesh):
    return jax.shard_map(
        body,
        mesh=mesh,
        in_specs=(
            P("gz", "gx", None),
            P(None, "gz", None),
            P(),
            P(),
            P(None, "gz", "gx"),
            P(None, "gz", "gx"),
            P(None, "gz", "gx"),
            P(None, "gz", "gx"),
        ),
        out_specs=P("gz", "gx", None),
        check_vma=False,
    )
```
